32 devices in a mesh: dp: 8 (over y, x, core), tensor: 4 (over z).
Axes of the slice: x: 2, y: 2, z: 4, core: 2. Of those that a mesh axis runs over, the one named last changes fastest.
Arguments:
- tokens: bfloat16 [6144, 2048], P(('dp', 'tensor')), may hold values from -6 to 6
- cotangent: bfloat16 [6144, 2048], P(('dp', 'tensor')), may hold values from -6 to 6
- deal: int32 [6144], P(('dp', 'tensor')), may hold values from 0 to 6143, as said below
- segment: int32 [6144], P('dp'), may hold values from 0 to 3, as said below
- norm1_gain: float32 [2, 2048], replicated, may hold values from 0.5 to 1.5
- norm1_shift: float32 [2, 2048], replicated, may hold values from -1.25 to 1.25
- query_weight: bfloat16 [2, 2048, 2048], P(None, 'dp', 'tensor'), may hold values from -0.125 to 0.125
- query_bias: float32 [2, 2048], P(None, 'tensor'), may hold values from -3 to 3
- kv_weight: bfloat16 [2, 2048, 256], P(None, 'dp', 'tensor'), may hold values from -0.125 to 0.125
- value_bias: float32 [2, 128], replicated, may hold values from -0.3125 to 0.3125
- out_weight: bfloat16 [2, 2048, 2048], P(None, 'tensor', 'dp'), may hold values from -1.5 to 1.5
- out_bias: float32 [2, 2048], replicated, may hold values from -1.75 to 1.75
- norm2_gain: float32 [2, 2048], replicated, may hold values from 0.5 to 1.5
- norm2_shift: float32 [2, 2048], replicated, may hold values from -1.25 to 1.25
- up_weight: bfloat16 [2, 2048, 8192], P(None, 'dp', 'tensor'), may hold values from -0.125 to 0.125
- up_bias: float32 [2, 8192], P(None, 'tensor'), may hold values from -3 to 3
- down_weight: bfloat16 [2, 8192, 2048], P(None, 'tensor', 'dp'), may hold values from -0.0625 to 0.0625
- down_bias: float32 [2, 2048], replicated, may hold values from -1.75 to 1.75
Outputs:
- layer_out: bfloat16 [6144, 2048], P(('dp', 'tensor'))
- tokens_grad: bfloat16 [6144, 2048], P(('dp', 'tensor'))
- norm1_gain_grad: float32 [2, 2048], replicated
- norm1_shift_grad: float32 [2, 2048], replicated
- query_weight_grad: float32 [2, 2048, 2048], P(None, 'dp', 'tensor')
- query_bias_grad: float32 [2, 2048], P(None, 'tensor')
- kv_weight_grad: float32 [2, 2048, 256], P(None, 'dp', 'tensor')
- value_bias_grad: float32 [2, 128], replicated
- out_weight_grad: float32 [2, 2048, 2048], P(None, 'tensor', 'dp')
- out_bias_grad: float32 [2, 2048], replicated
- norm2_gain_grad: float32 [2, 2048], replicated
- norm2_shift_grad: float32 [2, 2048], replicated
- up_weight_grad: float32 [2, 2048, 8192], P(None, 'dp', 'tensor')
- up_bias_grad: float32 [2, 8192], P(None, 'tensor')
- down_weight_grad: float32 [2, 8192, 2048], P(None, 'tensor', 'dp')
- down_bias_grad: float32 [2, 2048], replicated
The draws below stay inside these ranges and needn't reach their ends.
Inputs may be any that keep to these rules, and one draw needn't show every extreme that they name: deal is a permutation: input row i becomes working row deal[i]; rows of both orders are laid out over the devices in order, 192 a device; a row stays on a device of the same tensor index, and every device deals exactly 24 rows to each dp index. `segment`: within each group of 768 working rows the labels never fall; each run of equal labels is one sequence of 96 to 768 rows; the first group is one sequence of all its rows.
All inputs are finite; a program needn't handle non-finite values.
Results may differ from the reference program's by a relative error of at most 0.025.
Values may be sent and summed in bfloat16 or wider, within the bound.
No kernel may reach another device: no remote copies, remote signals or barrier semaphores. Data moves between devices by JAX's collectives and lax.ppermute only.
A program may use at most 256 MiB of HBM per device.

```python
import jax
import jax.numpy as jnp
from jax import lax

D = 2048
HEADS = 16
HEAD = 128
FF = 8192
LAYERS = 2
TOK_DEV = 192
KV = 256
GROUP = 768
TOKENS = 6144
N_DP = 8
N_TENSOR = 4


def draw_deal(key, part):
    first_key, second_key = jax.random.split(key)
    device_count = N_DP * N_TENSOR
    slot_rows = TOK_DEV // N_DP
    first_keys = jax.random.split(first_key, device_count)
    orders = jax.vmap(lambda single: jax.random.permutation(single, TOK_DEV))(first_keys)
    inverse = jnp.argsort(orders, axis=1).astype(jnp.int32)
    inverse = inverse.reshape(N_DP, N_TENSOR, N_DP, slot_rows)
    dest_ids = jnp.arange(N_DP, dtype=jnp.int32)[:, None, None, None]
    tensor_ids = jnp.arange(N_TENSOR, dtype=jnp.int32)[None, :, None, None]
    work_rows = (dest_ids * N_TENSOR + tensor_ids) * TOK_DEV + inverse
    work_rows = jnp.transpose(work_rows, (2, 1, 0, 3)).reshape(device_count, TOK_DEV)
    second_keys = jax.random.split(second_key, device_count)
    shuffles = jax.vmap(lambda single: jax.random.permutation(single, TOK_DEV))(second_keys)
    dealt = jnp.take_along_axis(work_rows, shuffles.astype(jnp.int32), axis=1)
    return dealt.reshape(TOKENS).astype(jnp.int32)


def draw_segment(key, part):
    quarter = GROUP // 4
    jitter = GROUP // 16
    cut_key, move_key = jax.random.split(jax.random.fold_in(key, 7))
    chosen = jax.random.randint(cut_key, (N_DP, 3), 0, 2)
    chosen = chosen.at[0].set(0).at[1].set(1)
    moves = jax.random.randint(move_key, (N_DP, 3), -jitter, jitter + 1)
    cuts = (jnp.arange(1, 4, dtype=jnp.int32) * quarter)[None, :] + moves
    places = jnp.arange(GROUP, dtype=jnp.int32)
    passed = (places[None, :, None] >= cuts[:, None, :]) & (chosen[:, None, :] == 1)
    labels = jnp.sum(passed.astype(jnp.int32), axis=2)
    return labels.reshape(TOKENS).astype(jnp.int32)


def steps_of(stream_key, shape, shards, least, largest):
    level, own = 1.0, jax.random.fold_in(stream_key, 6)
    for axis_at, blocks in shards:
        steps = jnp.exp(jax.random.uniform(jax.random.fold_in(own, axis_at), (blocks,), jnp.float32, least / len(shards), largest / len(shards)))
        level = level * jnp.repeat(steps, shape[axis_at] // blocks).reshape([-1 if axis == axis_at else 1 for axis in range(len(shape))])
    return level


def bell_draw(stream_key, dims, scale, limit, cuts=(), held_as=jnp.bfloat16):
    level = steps_of(stream_key, dims, cuts, -0.22, 0.18) if cuts else 1.0
    drawn = jax.random.normal(stream_key, dims, jnp.float32) * scale * level
    return jnp.minimum(jnp.maximum(drawn, -limit), limit).astype(held_as)


def setup_inputs(seed: int = 0) -> dict:
    key_of = jax.random.split(jax.random.key(seed), 19)
    tokens = bell_draw(key_of[0], (TOKENS, D), 1.0, 6.0, ((0, 32),))
    cotangent = bell_draw(key_of[1], (TOKENS, D), 1.0, 6.0, ((0, 32),))
    deal = draw_deal(jax.random.fold_in(key_of[18], 71), 0)
    segment = draw_segment(jax.random.fold_in(key_of[18], 71), 0)
    norm1_gain = jnp.clip(1.0 + 0.1 * jax.random.normal(key_of[4], (LAYERS, D), jnp.float32), 0.5, 1.5)
    norm1_shift = bell_draw(key_of[5], (LAYERS, D), 0.2, 1.25, (), jnp.float32)
    query_weight = bell_draw(key_of[6], (LAYERS, D, D), D ** -0.5, 0.125, ((1, 8), (2, 4)))
    query_bias = bell_draw(key_of[7], (LAYERS, D), 0.5, 3.0, ((1, 4),), jnp.float32)
    kv_weight = bell_draw(key_of[8], (LAYERS, D, KV), D ** -0.5, 0.125, ((1, 8), (2, 4)))
    value_bias = bell_draw(key_of[9], (LAYERS, HEAD), 0.05, 0.3125, (), jnp.float32)
    out_weight = bell_draw(key_of[10], (LAYERS, D, D), (max(D // 128, 1)) ** -0.5, 1.5, ((1, 4), (2, 8)))
    out_bias = bell_draw(key_of[11], (LAYERS, D), 0.3, 1.75, (), jnp.float32)
    norm2_gain = jnp.clip(1.0 + 0.1 * jax.random.normal(key_of[12], (LAYERS, D), jnp.float32), 0.5, 1.5)
    norm2_shift = bell_draw(key_of[13], (LAYERS, D), 0.2, 1.25, (), jnp.float32)
    up_weight = bell_draw(key_of[14], (LAYERS, D, FF), D ** -0.5, 0.125, ((1, 8), (2, 4)))
    up_bias = bell_draw(key_of[15], (LAYERS, FF), 0.5, 3.0, ((1, 4),), jnp.float32)
    down_weight = bell_draw(key_of[16], (LAYERS, FF, D), FF ** -0.5, 0.0625, ((1, 4), (2, 8)))
    down_bias = bell_draw(key_of[17], (LAYERS, D), 0.3, 1.75, (), jnp.float32)
    return dict(tokens=tokens, cotangent=cotangent, deal=deal, segment=segment, norm1_gain=norm1_gain, norm1_shift=norm1_shift, query_weight=query_weight, query_bias=query_bias, kv_weight=kv_weight, value_bias=value_bias, out_weight=out_weight, out_bias=out_bias, norm2_gain=norm2_gain, norm2_shift=norm2_shift, up_weight=up_weight, up_bias=up_bias, down_weight=down_weight, down_bias=down_bias)


EPSILON = 1e-05
HIGH = lax.Precision.HIGHEST

@jax.custom_vjp
def low(v):
    return lax.optimization_barrier(v.astype(jnp.bfloat16)).astype(jnp.float32)

@jax.custom_vjp
def low_back(v):
    return v

def low_keep(v):
    return (low(v), None)

def low_pass(kept, grad):
    return (grad,)

def back_keep(v):
    return (v, None)

def back_low(kept, grad):
    return (low(grad),)
low.defvjp(low_keep, low_pass)
low_back.defvjp(back_keep, back_low)

def product(left, right):
    return jnp.dot(left, right, precision=HIGH, preferred_element_type=jnp.float32)

def layer_norm(values, scales, offsets):
    row_mean = lax.optimization_barrier(jnp.mean(values, axis=-1, keepdims=True))
    centred = values - row_mean
    row_var = lax.optimization_barrier(jnp.mean(centred * centred, axis=-1, keepdims=True))
    return centred * lax.rsqrt(row_var + EPSILON) * scales + offsets

def block(stream, params, labels):
    gain_one, shift_one, w_query, b_query, w_pair, b_value, w_out, b_out, gain_two, shift_two, w_up, b_up, w_down, b_down = params
    row_count = stream.shape[0]
    score_scale = HEAD ** (-0.5)
    normed = low(layer_norm(stream, gain_one, shift_one))
    queries = low(low_back(product(normed, w_query) + b_query))
    pair_bias = jnp.concatenate([jnp.zeros((HEAD,), jnp.float32), b_value])
    pairs = low(low_back(product(normed, w_pair) + pair_bias))
    key_rows = pairs[:, :HEAD]
    value_rows = pairs[:, HEAD:]
    places = jnp.arange(row_count, dtype=jnp.int32)
    allowed = (places[None, :] <= places[:, None]) & (labels[:, None] == labels[None, :])

    def one_head(query_one):
        raw_score = low_back(product(query_one, key_rows.T))
        masked = jnp.where(allowed, raw_score * score_scale, -1e+30)
        row_top = lax.optimization_barrier(jnp.max(masked, axis=-1, keepdims=True))
        exp_score = jnp.exp(masked - row_top)
        weights = exp_score / lax.optimization_barrier(jnp.sum(exp_score, axis=-1, keepdims=True))
        return product(low(weights), value_rows)
    per_head = lax.map(jax.checkpoint(one_head), jnp.transpose(queries.reshape(row_count, HEADS, HEAD), (1, 0, 2)))
    head_mix = low(low_back(jnp.transpose(per_head, (1, 0, 2)).reshape(row_count, HEADS * HEAD)))
    hidden_state = stream + low_back(product(head_mix, w_out) + b_out)
    normed_two = low(layer_norm(hidden_state, gain_two, shift_two))
    pre_gelu = low_back(product(normed_two, w_up) + b_up)
    activation = low(jax.nn.gelu(pre_gelu, approximate=True))
    return hidden_state + low_back(product(activation, w_down) + b_down)

def forward(stream, params, labels):
    for layer_index in range(LAYERS):
        layer_params = tuple((member[layer_index] for member in params))
        stream = block(stream, layer_params, labels)
    return stream

def reference(tokens, cotangent, deal, segment, norm1_gain, norm1_shift, query_weight, query_bias, kv_weight, value_bias, out_weight, out_bias, norm2_gain, norm2_shift, up_weight, up_bias, down_weight, down_bias):
    params = (norm1_gain, norm1_shift, query_weight, query_bias, kv_weight, value_bias, out_weight, out_bias, norm2_gain, norm2_shift, up_weight, up_bias, down_weight, down_bias)
    params = tuple((member.astype(jnp.float32) for member in params))
    work_in = jnp.zeros((TOKENS, D), jnp.float32).at[deal].set(tokens.astype(jnp.float32))
    work_tangent = jnp.zeros((TOKENS, D), jnp.float32).at[deal].set(cotangent.astype(jnp.float32))
    stacked_in = work_in.reshape(N_DP, GROUP, D)
    stacked_tangent = work_tangent.reshape(N_DP, GROUP, D)
    stacked_labels = segment.reshape(N_DP, GROUP)

    def one_group(carried, inputs):
        stream, tangent, labels = inputs
        result, pullback = jax.vjp(lambda values, weights: forward(values, weights, labels), stream, params)
        stream_grad, param_grads = pullback(tangent)
        carried = jax.tree.map(lambda total, extra: total + extra, carried, param_grads)
        return (carried, (result, stream_grad))
    starting = jax.tree.map(jnp.zeros_like, params)
    totals, (outputs, input_grads) = lax.scan(one_group, starting, (stacked_in, stacked_tangent, stacked_labels))
    layer_out = outputs.reshape(TOKENS, D)[deal].astype(jnp.bfloat16)
    tokens_grad = input_grads.reshape(TOKENS, D)[deal].astype(jnp.bfloat16)
    return (layer_out, tokens_grad, totals[0], totals[1], totals[2], totals[3], totals[4], totals[5], totals[6], totals[7], totals[8], totals[9], totals[10], totals[11], totals[12], totals[13])
```

```python
import jax
import jax.numpy as jnp
from jax import lax
from jax.experimental import pallas as pl
from jax.experimental.pallas import tpu as pltpu
from jax.sharding import PartitionSpec as P

HEAD = 128
EPSILON = 1e-05
BF16 = jnp.bfloat16
F32 = jnp.float32


def layer_norm(values, scales, offsets):
    row_mean = jnp.mean(values, axis=-1, keepdims=True)
    centred = values - row_mean
    row_var = jnp.mean(centred * centred, axis=-1, keepdims=True)
    return centred * lax.rsqrt(row_var + EPSILON) * scales + offsets


def gelu_tanh(values):
    return jax.nn.gelu(values, approximate=True)


def matmul(left, right):
    return jnp.dot(left, right, preferred_element_type=F32)


def contract_rows(left, right):
    return lax.dot_general(left, right, (((0,), (0,)), ((), ())), preferred_element_type=F32)


def contract_cols(left, right):
    return lax.dot_general(left, right, (((1,), (1,)), ((), ())), preferred_element_type=F32)


def after(values, *others):
    return lax.optimization_barrier((values, others))[0]


def flip(values, bit):
    count = lax.axis_size("dp")
    return lax.ppermute(values, "dp", [(i, i ^ bit) for i in range(count)])


def turn(values, step):
    count = lax.axis_size("tensor")
    return lax.ppermute(values, "tensor", [((i + step) % count, i) for i in range(count)])


def plane_bits():
    count = lax.axis_size("dp")
    return [1 << k for k in range(1, count.bit_length() - 1)]


def slot_order():
    count = lax.axis_size("dp")
    evens = list(range(0, count, 2))
    return evens + [r ^ 1 for r in evens]


def join_rows(arrays):
    return arrays[0] if len(arrays) == 1 else jnp.concatenate(arrays, axis=0)


def blocks_of(parts, wanted):
    runs = []
    where = {}
    for array, blocks in parts:
        rows = array.shape[0] // len(blocks)
        for i, block in enumerate(blocks):
            where[block] = (array, i * rows, rows)
    for block in wanted:
        array, start, rows = where[block]
        if runs and runs[-1][0] is array and runs[-1][2] == start:
            runs[-1][2] += rows
        else:
            runs.append([array, start, start + rows])
    return join_rows([lax.slice_in_dim(array, low, high) for array, low, high in runs])


class Gather:
    def __init__(self, first, second):
        bits = plane_bits()
        self.members = [
            [order, [(array, [0])]]
            for group, order in ((first, bits), (second, bits[::-1]))
            for array in group
        ]
        self.taken = 0

    def send(self, *gate):
        for member in self.members:
            order, parts = member
            bit = order[self.taken]
            blocks = [block for _, part in parts for block in part]
            whole = join_rows([array for array, _ in parts])
            come = flip(after(whole, *gate) if gate else whole, bit)
            member[1] = [(whole, blocks), (come, [block | bit for block in blocks])]
        self.taken += 1
        return self

    def settle(self, *late):
        for member in self.members:
            own, (come, blocks) = member[1]
            member[1] = [own, (after(come, *late), blocks)]
        return self

    def finish(self, *gate):
        while self.taken < len(plane_bits()):
            self.send(*gate)
        return [
            parts + [(flip(array, 1), [block | 1 for block in blocks]) for array, blocks in parts]
            for _, parts in self.members
        ]


class Scatter:
    def __init__(self, first, second):
        bits = plane_bits()
        evens = list(range(0, lax.axis_size("dp"), 2))
        self.members = [
            [order, half, evens]
            for group, order in ((first, bits), (second, bits[::-1]))
            for half in group
        ]
        self.taken = 0
        self.come = None

    def send(self, *gate):
        self.come = []
        for order, half, blocks in self.members:
            sent = [block for block in blocks if block & order[self.taken]]
            piece = blocks_of([(half, blocks)], sent)
            piece = after(piece, *gate) if gate else piece
            self.come.append(flip(piece, order[self.taken]))
        self.taken += 1
        return self

    def settle(self, *late):
        last = self.taken == len(plane_bits())
        for member, come in zip(self.members, self.come):
            order, half, blocks = member
            keep = [block for block in blocks if not block & order[self.taken - 1]]
            if late:
                come = after(come, *late)
            total = blocks_of([(half, blocks)], keep).astype(F32) + come.astype(F32)
            member[1:] = [total if last else total.astype(BF16), keep]
        self.come = None
        return self

    def now(self):
        return [half for _, half, _ in self.members]

    def finish(self, *late):
        if self.come:
            self.settle(*late)
        while self.taken < len(plane_bits()):
            self.send()
            self.settle(*late)
        return [half.astype(F32) for _, half, _ in self.members]


def gradient_half(features, values):
    half = features.shape[1] // 2
    far = contract_rows(features[:, half:], values).astype(BF16)
    near = contract_rows(features[:, :half], values) + flip(far, 1).astype(F32)
    return near.astype(BF16)


def plain_product(total):
    return (total,)


def round_product(total):
    return (total.astype(BF16),)


def gelu_both(total, bias):
    value = total + bias
    return value, gelu_tanh(value).astype(BF16)


def gelu_slope(values):
    factor = 0.7978845608028654
    square = values * values
    wave = jnp.tanh(factor * (values + 0.044715 * (square * values)))
    return 0.5 * (1.0 + wave) + (0.5 * factor) * values * (1.0 - wave * wave) * (
        1.0 + (3.0 * 0.044715) * square
    )


def gelu_and_back(total, bias, act_grad):
    value = total + bias
    return gelu_tanh(value).astype(BF16), (act_grad * gelu_slope(value)).astype(BF16)


def gelu_back(total, value):
    return ((total * gelu_slope(value)).astype(BF16),)


def times(left, parts, finish, extras, types):
    rows, depth = left.shape
    columns = parts[0][0].shape[1]
    height = depth // lax.axis_size("dp")
    place = {block: i for i, block in enumerate(slot_order())}
    if height % 128:
        return finish(matmul(left, blocks_of(parts, slot_order())), *extras)
    tile = next(size for size in (768, 640, 512, 384, 256, 128, columns) if columns % size == 0)
    spots = [[place[block] * height for block in blocks] for _, blocks in parts]

    def kernel(left_ref, *refs):
        part_refs = refs[: len(parts)]
        extra_refs = refs[len(parts) : len(parts) + len(extras)]
        total = None
        for ref, starts in zip(part_refs, spots):
            for i, start in enumerate(starts):
                piece = matmul(
                    left_ref[:, start : start + height], ref[i * height : (i + 1) * height, :]
                )
                total = piece if total is None else total + piece
        values = finish(total, *[ref[...] for ref in extra_refs])
        for ref, value in zip(refs[len(parts) + len(extras) :], values):
            ref[...] = value

    return pl.pallas_call(
        kernel,
        grid=(columns // tile,),
        in_specs=[pl.BlockSpec((rows, depth), lambda j: (0, 0))]
        + [pl.BlockSpec((array.shape[0], tile), lambda j: (0, j)) for array, _ in parts]
        + [pl.BlockSpec((extra.shape[0], tile), lambda j: (0, j)) for extra in extras],
        out_specs=[pl.BlockSpec((rows, tile), lambda j: (0, j)) for _ in types],
        out_shape=[jax.ShapeDtypeStruct((rows, columns), kind) for kind in types],
        cost_estimate=pl.CostEstimate(
            flops=2 * rows * depth * columns,
            transcendentals=rows * columns if extras else 0,
            bytes_accessed=2 * depth * (rows + columns) + 6 * rows * columns,
        ),
        name="times",
    )(left, *[array for array, _ in parts], *extras)


def times_turned(left, parts, kind):
    rows, depth = left.shape
    count = lax.axis_size("dp")
    height = sum(array.shape[0] for array, _ in parts) // count
    place = {block: i for i, block in enumerate(slot_order())}
    if height % 128:
        return contract_cols(left, blocks_of(parts, slot_order())).astype(kind)
    tile = 256 if rows % 256 == 0 else rows
    spots = [[place[block] * height for block in blocks] for _, blocks in parts]

    def kernel(left_ref, *refs):
        for ref, starts in zip(refs, spots):
            for i, start in enumerate(starts):
                piece = contract_cols(left_ref[...], ref[i * height : (i + 1) * height, :])
                refs[-1][:, start : start + height] = piece.astype(kind)

    whole = [
        pl.BlockSpec(array.shape, lambda i: (0, 0), pipeline_mode=pl.Buffered(1))
        for array, _ in parts
    ]
    return pl.pallas_call(
        kernel,
        grid=(rows // tile,),
        in_specs=[pl.BlockSpec((tile, depth), lambda i: (i, 0))] + whole,
        out_specs=pl.BlockSpec((tile, count * height), lambda i: (i, 0)),
        out_shape=jax.ShapeDtypeStruct((rows, count * height), kind),
        cost_estimate=pl.CostEstimate(
            flops=2 * rows * depth * count * height,
            transcendentals=0,
            bytes_accessed=2 * depth * (rows + count * height) + 4 * rows * count * height,
        ),
        name="times_turned",
    )(left, *[array for array, _ in parts])


def arrays_of(*weights):
    return [array for parts in weights for array, _ in parts]


def tensor_slots(values):
    return [values] + [turn(values, k) for k in range(1, lax.axis_size("tensor"))]


def tensor_rows(values):
    return lax.all_gather(values, "tensor", axis=0, tiled=True)


def tensor_sum(values):
    return lax.psum_scatter(values, "tensor", scatter_dimension=0, tiled=True)


def sum_columns(whole, count):
    width = whole.shape[1] // count
    whole = whole.astype(BF16)
    pieces = [whole[:, k * width : (k + 1) * width] for k in range(count)]
    return tensor_sum(jnp.concatenate(pieces, axis=0)).astype(F32)


def sum_query(whole, width, query_cols, pair_cols):
    count = lax.axis_size("tensor")
    rows = whole.shape[0]
    whole = whole.astype(BF16)
    pieces = []
    for k in range(count):
        pieces.append(whole[:, k * query_cols : (k + 1) * query_cols])
        pair = whole[:, width + k * pair_cols : width + (k + 1) * pair_cols]
        pieces.append(pair.reshape(rows * pair_cols // query_cols, query_cols))
    total = tensor_sum(jnp.concatenate(pieces, axis=0)).astype(F32)
    return total[:rows], total[rows:].reshape(rows, pair_cols)


def copy_block(table, source, target):
    target[...] = source[...]


def reorder(values, table):
    rows, columns = values.shape
    count = table.shape[0]
    width = columns // count
    if width % 128:
        return jnp.take(values.reshape(rows, count, width), table, axis=1).reshape(rows, columns)
    return pl.pallas_call(
        copy_block,
        grid_spec=pltpu.PrefetchScalarGridSpec(
            num_scalar_prefetch=1,
            grid=(count,),
            in_specs=[pl.BlockSpec((rows, width), lambda j, table: (0, table[j]))],
            out_specs=pl.BlockSpec((rows, width), lambda j, table: (0, j)),
        ),
        out_shape=jax.ShapeDtypeStruct(values.shape, values.dtype),
        name="reorder",
    )(table, values)


def stack_heads(block):
    return jnp.concatenate([block[:, :HEAD], block[:, HEAD:]], axis=0)


def attend_kernel(scale, query_ref, key_ref, value_t_ref, bias_ref, out_ref, log_ref):
    rows = query_ref.shape[0]
    queries = stack_heads(query_ref[...])
    scores = contract_cols(key_ref[...], queries) * scale + bias_ref[...]
    top = jnp.max(scores, axis=0, keepdims=True)
    exps = jnp.exp(scores - top)
    total = jnp.sum(exps, axis=0, keepdims=True)
    probs = (exps * (1.0 / total)).astype(BF16)
    mixed = matmul(value_t_ref[...], probs).T.astype(BF16)
    out_ref[:, :HEAD] = mixed[:rows]
    out_ref[:, HEAD:] = mixed[rows:]
    log_ref[0] = top + jnp.log(total)


def attend(queries, key_rows, value_t, bias, scale):
    rows, columns = queries.shape
    pairs = columns // (2 * HEAD)
    keys = key_rows.shape[0]

    def kernel(*refs):
        attend_kernel(scale, *refs)

    return pl.pallas_call(
        kernel,
        grid=(pairs,),
        in_specs=[
            pl.BlockSpec((rows, 2 * HEAD), lambda i: (0, i)),
            pl.BlockSpec((keys, HEAD), lambda i: (0, 0)),
            pl.BlockSpec((HEAD, keys), lambda i: (0, 0)),
            pl.BlockSpec((keys, 2 * rows), lambda i: (0, 0)),
        ],
        out_specs=[
            pl.BlockSpec((rows, 2 * HEAD), lambda i: (0, i)),
            pl.BlockSpec((1, 1, 2 * rows), lambda i: (i, 0, 0)),
        ],
        out_shape=[
            jax.ShapeDtypeStruct((rows, columns), BF16),
            jax.ShapeDtypeStruct((pairs, 1, 2 * rows), F32),
        ],
        cost_estimate=pl.CostEstimate(
            flops=4 * rows * keys * columns,
            transcendentals=rows * keys * columns // HEAD,
            bytes_accessed=4 * rows * columns + 8 * keys * rows,
        ),
        name="attend",
    )(queries, key_rows, value_t, bias)


def attend_back_kernel(
    scale, query_ref, dout_ref, key_ref, value_ref, key_t_ref, bias_ref, log_ref, grad_ref, pair_ref
):
    rows = query_ref.shape[0]

    @pl.when(pl.program_id(0) == 0)
    def _():
        pair_ref[...] = jnp.zeros_like(pair_ref)

    queries = stack_heads(query_ref[...])
    douts = stack_heads(dout_ref[...])
    scores = contract_cols(key_ref[...], queries) * scale + bias_ref[...]
    probs = jnp.exp(scores - log_ref[0])
    prob_grad = contract_cols(value_ref[...], douts)
    inner = jnp.sum(probs * prob_grad, axis=0, keepdims=True)
    score_grad = (probs * (prob_grad - inner) * scale).astype(BF16)
    pair_ref[:, :HEAD] += matmul(score_grad, queries)
    pair_ref[:, HEAD:] += matmul(probs.astype(BF16), douts)
    query_grad = matmul(key_t_ref[...], score_grad).T.astype(BF16)
    grad_ref[:, :HEAD] = query_grad[:rows]
    grad_ref[:, HEAD:] = query_grad[rows:]


def attend_back(queries, douts, key_rows, value_rows, key_t, bias, log_totals, scale):
    rows, columns = queries.shape
    pairs = columns // (2 * HEAD)
    keys = key_rows.shape[0]

    def kernel(*refs):
        attend_back_kernel(scale, *refs)

    return pl.pallas_call(
        kernel,
        grid=(pairs,),
        in_specs=[
            pl.BlockSpec((rows, 2 * HEAD), lambda i: (0, i)),
            pl.BlockSpec((rows, 2 * HEAD), lambda i: (0, i)),
            pl.BlockSpec((keys, HEAD), lambda i: (0, 0)),
            pl.BlockSpec((keys, HEAD), lambda i: (0, 0)),
            pl.BlockSpec((HEAD, keys), lambda i: (0, 0)),
            pl.BlockSpec((keys, 2 * rows), lambda i: (0, 0)),
            pl.BlockSpec((1, 1, 2 * rows), lambda i: (i, 0, 0)),
        ],
        out_specs=[
            pl.BlockSpec((rows, 2 * HEAD), lambda i: (0, i)),
            pl.BlockSpec((keys, 2 * HEAD), lambda i: (0, 0)),
        ],
        out_shape=[
            jax.ShapeDtypeStruct((rows, columns), BF16),
            jax.ShapeDtypeStruct((keys, 2 * HEAD), F32),
        ],
        cost_estimate=pl.CostEstimate(
            flops=10 * rows * keys * columns,
            transcendentals=rows * keys * columns // HEAD,
            bytes_accessed=6 * rows * columns + 12 * keys * rows,
        ),
        name="attend_back",
    )(queries, douts, key_rows, value_rows, key_t, bias, log_totals)


def local(
    tokens,
    cotangent,
    deal,
    segment,
    norm1_gain,
    norm1_shift,
    query_weight,
    query_bias,
    kv_weight,
    value_bias,
    out_weight,
    out_bias,
    norm2_gain,
    norm2_shift,
    up_weight,
    up_bias,
    down_weight,
    down_bias,
):
    local_rows, width = tokens.shape
    dp_count = lax.axis_size("dp")
    tensor_count = lax.axis_size("tensor")
    dp_rank = lax.axis_index("dp")
    tensor_rank = lax.axis_index("tensor")
    slot_rows = local_rows // dp_count
    layer_total = query_weight.shape[0]
    group_rows = local_rows * tensor_count
    query_cols = query_weight.shape[2]
    pair_cols = kv_weight.shape[2]
    score_scale = HEAD ** (-0.5)
    order = slot_order()
    to_slots = jnp.asarray(order, jnp.int32) ^ dp_rank
    place_of = [order.index(r) for r in range(dp_count)]
    from_slots = jnp.take(
        jnp.asarray(place_of, jnp.int32), jnp.arange(dp_count, dtype=jnp.int32) ^ dp_rank
    )

    last = layer_total - 1
    split = width // 2
    cut = tensor_count // 2
    bias_slots = jnp.roll(
        jnp.concatenate(tensor_slots(query_bias), axis=1), tensor_rank * query_cols, axis=1
    )
    kv_full = jnp.roll(
        jnp.concatenate(tensor_slots(kv_weight), axis=2), tensor_rank * pair_cols, axis=2
    )
    depth = query_weight.shape[1]

    def columns(rows, *more):
        count = rows.shape[0] // depth
        pieces = [rows[k * depth : (k + 1) * depth] for k in range(count)]
        return jnp.concatenate(pieces + list(more), axis=1)

    out_turned = [out_weight[l].T for l in range(layer_total)]
    down_turned = [down_weight[l].T for l in range(layer_total)]
    query_rows = tensor_rows(query_weight[0])
    out_rows = tensor_rows(after(out_turned[0], query_rows))
    cut_rows = cut * depth
    ff_gather = Gather([up_weight[0]], [down_turned[0]]).send()
    query_gather = Gather(
        [columns(query_rows[:cut_rows])], [columns(query_rows[cut_rows:], kv_full[0])]
    )
    w_query = query_gather.finish()
    out_gather = Gather([columns(out_rows[:cut_rows])], [columns(out_rows[cut_rows:])])
    w_out = out_gather.finish()
    ff_gather.settle()

    target_dev = deal // local_rows // tensor_count
    target_row = deal % local_rows
    dev_ids = jnp.arange(dp_count, dtype=jnp.int32)
    dev_match = (target_dev[:, None] == dev_ids[None, :]).astype(jnp.int32)
    earlier = jnp.cumsum(dev_match, axis=0) - dev_match
    slot_of = target_dev * slot_rows + jnp.sum(earlier * dev_match, axis=1)
    row_ids = jnp.arange(local_rows, dtype=jnp.int32)
    send_table = (row_ids[:, None] == slot_of[None, :]).astype(BF16)
    place_cols = jnp.broadcast_to(target_row.astype(BF16)[:, None], (local_rows, HEAD))
    tokens_sent = matmul(send_table, jnp.concatenate([tokens, place_cols], axis=1)).astype(BF16)
    tokens_come = lax.all_to_all(tokens_sent, "dp", split_axis=0, concat_axis=0, tiled=True)
    tangent_sent = matmul(send_table, cotangent).astype(BF16)
    tangent_come = lax.all_to_all(tangent_sent, "dp", split_axis=0, concat_axis=0, tiled=True)
    arrived_place = tokens_come[:, width].astype(jnp.int32)
    place_table = (row_ids[:, None] == arrived_place[None, :]).astype(BF16)
    stream = reorder(matmul(place_table, tokens_come[:, :width]).astype(BF16), to_slots).astype(F32)
    last_branch = reorder(matmul(place_table, tangent_come).astype(BF16), to_slots)
    tangent = last_branch.astype(F32)
    stream = after(stream, last_branch)

    vectors = jnp.concatenate(
        [norm1_gain, norm1_shift, out_bias, norm2_gain, norm2_shift, down_bias], axis=0
    )
    vectors = reorder(vectors, to_slots)
    gain_one, shift_one, bias_out, gain_two, shift_two, bias_down = [
        vectors[i * layer_total : (i + 1) * layer_total] for i in range(6)
    ]

    places = jnp.arange(group_rows, dtype=jnp.int32)
    key_places = (places + tensor_rank * local_rows) % group_rows
    key_labels = jnp.roll(segment, -tensor_rank * local_rows)
    allowed = (key_places[:, None] <= key_places[None, :local_rows]) & (
        key_labels[:, None] == key_labels[None, :local_rows]
    )
    score_bias = jnp.where(allowed, 0.0, -1e30).astype(F32)
    score_bias = jnp.concatenate([score_bias, score_bias], axis=1)

    def product(left, weights):
        pieces = [times(left, parts, plain_product, (), (F32,))[0] for parts in weights]
        return pieces[0] if len(pieces) == 1 else jnp.concatenate(pieces, axis=1)

    def product_turned(left, weights):
        total, start = None, 0
        for parts in weights:
            size = parts[0][0].shape[1]
            piece = times_turned(left[:, start : start + size], parts, F32)
            total = piece if total is None else total + piece
            start += size
        return total

    saved = []
    for l in range(layer_total):
        if l < last:
            query_rows = tensor_rows(after(query_weight[l + 1], out_rows))
            out_rows = tensor_rows(after(out_turned[l + 1], query_rows))
        normed = layer_norm(stream, gain_one[l], shift_one[l]).astype(BF16)
        projected = product(normed, w_query)
        pair_bias = jnp.concatenate([jnp.zeros((HEAD,), F32), value_bias[l]])
        pair_own = (projected[:, width:] + pair_bias).astype(BF16)
        queries = (projected[:, :width] + bias_slots[l]).astype(BF16)
        pair_all = jnp.concatenate(tensor_slots(pair_own))
        pair_t = pair_all.T
        mixed, log_totals = attend(
            queries, pair_all[:, :HEAD], pair_t[HEAD:], score_bias, score_scale
        )
        w_up, w_down = ff_gather.settle(mixed).finish(mixed)
        hidden_state = stream + product_turned(mixed, w_out) + bias_out[l]
        normed_two = layer_norm(hidden_state, gain_two[l], shift_two[l]).astype(BF16)
        normed_two_all = tensor_rows(normed_two)
        normed_two_all = after(normed_two_all, *arrays_of(w_up, w_down))
        if l == last:
            if last == 0:
                branch_all = tensor_rows(last_branch)
            act_grad = times(branch_all, w_down, plain_product, (), (F32,))[0]
            normed_two_all = after(normed_two_all, act_grad)
            activation, pre_grad = times(
                normed_two_all, w_up, gelu_and_back, (up_bias[l][None], act_grad), (BF16, BF16)
            )
            pre_gelu = None
        else:
            pre_gelu, activation = times(
                normed_two_all, w_up, gelu_both, (up_bias[l][None],), (F32, BF16)
            )
        saved.append(
            (
                stream,
                normed,
                queries,
                pair_all,
                pair_t,
                log_totals,
                mixed,
                hidden_state,
                normed_two_all,
                pre_gelu,
                activation,
                w_query,
                w_out,
                w_up,
                w_down,
            )
        )
        if l < last:
            attn_gather = Gather([columns(query_rows, kv_full[l + 1])], [columns(out_rows)])
            attn_gather.send(normed_two_all)
            down_part = times_turned(activation, w_down, BF16)
            down_sum = tensor_sum(down_part)
            w_query, w_out = [[parts] for parts in attn_gather.settle(down_part).finish(down_part)]
            down_sum = after(down_sum, *arrays_of(*w_query, *w_out))
            if l == last - 1:
                branch_all = tensor_rows(after(last_branch, down_sum))
            stream = hidden_state + down_sum.astype(F32) + bias_down[l]
            ff_gather = Gather([up_weight[l + 1]], [down_turned[l + 1]]).send(down_sum)

    reduced = [None] * layer_total
    vector_grads = [None] * layer_total
    query_bias_grads = [None] * layer_total
    value_bias_grads = [None] * layer_total
    up_bias_grads = [None] * layer_total
    later = None
    for l in reversed(range(layer_total)):
        (
            stream_in,
            normed,
            queries,
            pair_all,
            pair_t,
            log_totals,
            mixed,
            hidden_state,
            normed_two_all,
            pre_gelu,
            activation,
            w_query,
            w_out,
            w_up,
            w_down,
        ) = saved[l]
        branch_grad = tangent.astype(BF16)
        if l < last:
            branch_all = tensor_rows(branch_grad)
            above, both_above, normed_above, attn_above, mixed_above, ff_scatter = later
            ff_scatter.settle(branch_grad).send()
            both_late, attn_late = after((both_above, attn_above), branch_grad)
            attn_scatter = Scatter(
                [gradient_half(normed_above, both_late)], [gradient_half(attn_late, mixed_above)]
            )
            attn_scatter.send()
            branch_all = after(branch_all, *ff_scatter.now(), *attn_scatter.now())
            pre_grad = times(branch_all, w_down, gelu_back, (pre_gelu,), (BF16,))[0]
        normed_part = times_turned(pre_grad, w_up, BF16)
        normed_two_grad = tensor_sum(normed_part)
        if l < last:
            up_grad, down_grad = ff_scatter.finish(normed_part)
            reduced[above] = (up_grad, down_grad.T)
            attn_scatter.settle(normed_part).send()
        pre_late, branch_late = after((pre_grad, branch_all), normed_part)
        down_bias_part = jnp.sum(after(branch_grad, normed_part).astype(F32), axis=0)
        up_bias_grads[l] = jnp.sum(pre_late.astype(F32), axis=0)
        ff_scatter = Scatter(
            [gradient_half(normed_two_all, pre_late)], [gradient_half(branch_late, activation)]
        )
        ff_scatter.send()
        beside = ff_scatter.now()
        if l == last:
            final_part = times_turned(after(activation, *beside), w_down, BF16)
            beside = beside + [final_part]
        else:
            beside = beside + attn_scatter.now()
        normed_two_grad = after(normed_two_grad, *beside)
        if l == last:
            final_sum = tensor_sum(after(final_part, normed_two_grad))
        hidden_part, gain_two_part, shift_two_part = jax.vjp(
            layer_norm, hidden_state, gain_two[l], shift_two[l]
        )[1](normed_two_grad.astype(F32))
        hidden_grad = tangent + hidden_part
        attn_grad = hidden_grad.astype(BF16)
        out_bias_part = jnp.sum(attn_grad.astype(F32), axis=0)
        mixed_grad = product(attn_grad, w_out).astype(BF16)
        if l == 0:
            ff_scatter.settle(attn_grad).send()
            attn_late = after(attn_grad, mixed_grad)
            out_scatter = Scatter(
                [gradient_half(attn_late, mixed[:, :split])],
                [gradient_half(attn_late, mixed[:, split:])],
            ).send()
            mixed_grad = after(mixed_grad, *ff_scatter.now(), *out_scatter.now())
        query_grad, pair_part = attend_back(
            queries,
            mixed_grad,
            pair_all[:, :HEAD],
            pair_all[:, HEAD:],
            pair_t[:HEAD],
            score_bias,
            log_totals,
            score_scale,
        )
        pair_grad = pair_part[:local_rows]
        for k in range(1, tensor_count):
            piece = pair_part[k * local_rows : (k + 1) * local_rows].astype(BF16)
            pair_grad = pair_grad + turn(piece, tensor_count - k).astype(F32)
        pair_grad = pair_grad.astype(BF16)
        query_bias_grads[l] = jnp.sum(query_grad.astype(F32), axis=0)
        value_bias_grads[l] = jnp.sum(pair_grad[:, HEAD:].astype(F32), axis=0)
        both_grad = jnp.concatenate([query_grad, pair_grad], axis=1)
        if l == 0 and last > 0:
            both_whole, out_whole = attn_scatter.finish(query_grad)
            out_grad = sum_columns(out_whole, tensor_count).T
            query_w_grad, kv_grad = sum_query(both_whole, width, query_cols, pair_cols)
            reduced[above] = (query_w_grad, kv_grad, out_grad) + reduced[above]
        normed_grad = product_turned(both_grad, w_query)
        stream_part, gain_one_part, shift_one_part = jax.vjp(
            layer_norm, stream_in, gain_one[l], shift_one[l]
        )[1](normed_grad)
        tangent = hidden_grad + stream_part
        later = (l, both_grad, normed, attn_grad, mixed, ff_scatter)
        vector_grads[l] = [
            gain_one_part,
            shift_one_part,
            out_bias_part,
            gain_two_part,
            shift_two_part,
            down_bias_part,
        ]
    out_scatter.settle(both_grad).send()
    both_scatter = Scatter(
        [gradient_half(normed, both_grad[:, :split])], [gradient_half(normed, both_grad[:, split:])]
    ).send()
    up_grad, down_grad = ff_scatter.finish(both_grad)
    out_grad = sum_columns(jnp.concatenate(out_scatter.finish(), axis=1), tensor_count).T
    both_whole = jnp.concatenate(both_scatter.finish(), axis=1)
    query_w_grad, kv_grad = sum_query(both_whole, width, query_cols, pair_cols)
    reduced[0] = (query_w_grad, kv_grad, out_grad, up_grad, down_grad.T)
    final_sum = after(final_sum, normed_two_grad)
    layer_out = (saved[last][7] + final_sum.astype(F32) + bias_down[last]).astype(BF16)

    stacked = jnp.stack([vector_grads[l][m] for m in range(6) for l in range(layer_total)])
    stacked = reorder(stacked, from_slots)
    query_rows = jnp.stack(query_bias_grads)
    value_rows = jnp.pad(jnp.stack(value_bias_grads), ((0, 0), (0, width - HEAD)))
    smalls = jnp.concatenate([stacked, query_rows, value_rows], axis=0)
    small_count = smalls.shape[0]
    smalls = jnp.concatenate([smalls, jnp.stack(up_bias_grads)], axis=0)
    for k in range(dp_count.bit_length() - 1):
        smalls = smalls + flip(smalls, 1 << k)
    up_bias_grad = smalls[small_count:]
    smalls = smalls[:small_count]
    total = smalls
    if tensor_count & (tensor_count - 1) == 0:
        for k in range(tensor_count.bit_length() - 1):
            total = total + lax.ppermute(
                total, "tensor", [(i, i ^ (1 << k)) for i in range(tensor_count)]
            )
    else:
        total = lax.psum(total, "tensor")
    vector_sums = [total[m * layer_total : (m + 1) * layer_total] for m in range(8)]
    query_bias_grad = lax.dynamic_slice_in_dim(
        vector_sums[6], tensor_rank * query_cols, query_cols, 1
    )
    value_bias_grad = vector_sums[7][:, :HEAD]

    out_slots = contract_rows(place_table, reorder(layer_out, from_slots)).astype(BF16)
    grad_slots = contract_rows(place_table, reorder(tangent.astype(BF16), from_slots)).astype(BF16)
    out_back = lax.all_to_all(out_slots, "dp", split_axis=0, concat_axis=0, tiled=True)
    grad_back = lax.all_to_all(grad_slots, "dp", split_axis=0, concat_axis=0, tiled=True)
    layer_rows = contract_rows(send_table, out_back).astype(BF16)
    token_rows = contract_rows(send_table, grad_back).astype(BF16)
    summed = [jnp.stack([reduced[l][m] for l in range(layer_total)]) for m in range(5)]
    return (
        layer_rows,
        token_rows,
        vector_sums[0],
        vector_sums[1],
        summed[0],
        query_bias_grad,
        summed[1],
        value_bias_grad,
        summed[2],
        vector_sums[2],
        vector_sums[3],
        vector_sums[4],
        summed[3],
        up_bias_grad,
        summed[4],
        vector_sums[5],
    )


def solution(mesh):
    rows = P(("dp", "tensor"), None)
    in_specs = (
        rows,
        rows,
        P(("dp", "tensor")),
        P("dp"),
        P(),
        P(),
        P(None, "dp", "tensor"),
        P(None, "tensor"),
        P(None, "dp", "tensor"),
        P(),
        P(None, "tensor", "dp"),
        P(),
        P(),
        P(),
        P(None, "dp", "tensor"),
        P(None, "tensor"),
        P(None, "tensor", "dp"),
        P(),
    )
    out_specs = (
        rows,
        rows,
        P(),
        P(),
        P(None, "dp", "tensor"),
        P(None, "tensor"),
        P(None, "dp", "tensor"),
        P(),
        P(None, "tensor", "dp"),
        P(),
        P(),
        P(),
        P(None, "dp", "tensor"),
        P(None, "tensor"),
        P(None, "tensor", "dp"),
        P(),
    )
    return jax.shard_map(local, mesh=mesh, in_specs=in_specs, out_specs=out_specs, check_vma=False)
```

```python
import jax
import jax.numpy as jnp
from jax import lax
from jax.experimental import pallas as pl
from jax.experimental.pallas import tpu as pltpu
from jax.sharding import PartitionSpec as P

HEAD = 128
EPSILON = 1e-05
BF16 = jnp.bfloat16
F32 = jnp.float32
LIGHT = pl.CostEstimate(flops=1, transcendentals=0, bytes_accessed=1)


def layer_norm(values, scales, offsets):
    row_mean = jnp.mean(values, axis=-1, keepdims=True)
    centred = values - row_mean
    row_var = jnp.mean(centred * centred, axis=-1, keepdims=True)
    return centred * lax.rsqrt(row_var + EPSILON) * scales + offsets


def gelu_tanh(values):
    return jax.nn.gelu(values, approximate=True)


def matmul(left, right):
    return jnp.dot(left, right, preferred_element_type=F32)


def contract_rows(left, right):
    return lax.dot_general(left, right, (((0,), (0,)), ((), ())), preferred_element_type=F32)


def contract_cols(left, right):
    return lax.dot_general(left, right, (((1,), (1,)), ((), ())), preferred_element_type=F32)


def after(values, *others):
    return lax.optimization_barrier((values, others))[0]


def flip(values, bit):
    count = lax.axis_size("dp")
    return lax.ppermute(values, "dp", [(i, i ^ bit) for i in range(count)])


def turn(values, step):
    count = lax.axis_size("tensor")
    return lax.ppermute(values, "tensor", [((i + step) % count, i) for i in range(count)])


def plane_bits():
    count = lax.axis_size("dp")
    return [1 << k for k in range(1, count.bit_length() - 1)]


def slot_order():
    count = lax.axis_size("dp")
    evens = list(range(0, count, 2))
    return evens + [r ^ 1 for r in evens]


def join_rows(arrays):
    return arrays[0] if len(arrays) == 1 else jnp.concatenate(arrays, axis=0)


def blocks_of(parts, wanted):
    runs = []
    where = {}
    for array, blocks in parts:
        rows = array.shape[0] // len(blocks)
        for i, block in enumerate(blocks):
            where[block] = (array, i * rows, rows)
    for block in wanted:
        array, start, rows = where[block]
        if runs and runs[-1][0] is array and runs[-1][2] == start:
            runs[-1][2] += rows
        else:
            runs.append([array, start, start + rows])
    return join_rows([lax.slice_in_dim(array, low, high) for array, low, high in runs])


class Gather:
    def __init__(self, first, second):
        bits = plane_bits()
        self.members = [
            [order, [(array, [0])]]
            for group, order in ((first, bits), (second, bits[::-1]))
            for array in group
        ]
        self.taken = 0
        self.come = []

    def send(self, *gate):
        gate = gate + tuple(self.come)
        self.come = []
        for member in self.members:
            order, parts = member
            bit = order[self.taken]
            blocks = [block for _, part in parts for block in part]
            whole = join_rows([array for array, _ in parts])
            come = flip(after(whole, *gate) if gate else whole, bit)
            self.come.append(come)
            member[1] = [(whole, blocks), (come, [block | bit for block in blocks])]
        self.taken += 1
        return self

    def settle(self, *late):
        for member in self.members:
            own, (come, blocks) = member[1]
            member[1] = [own, (after(come, *late), blocks)]
        return self

    def finish(self, *gate):
        while self.taken < len(plane_bits()):
            self.send(*gate)
        come = tuple(self.come)
        return [
            parts
            + [
                (flip(after(array, *come), 1), [block | 1 for block in blocks])
                for array, blocks in parts
            ]
            for _, parts in self.members
        ]


def add_blocks(half, count, keep, come, kind):
    rows, columns = half.shape[0] // count, half.shape[1]
    stride = keep[1] - keep[0] if len(keep) > 1 else 1

    def kernel(half_ref, come_ref, out_ref):
        out_ref[...] = (half_ref[...].astype(F32) + come_ref[...].astype(F32)).astype(kind)

    block = (rows, columns)
    return pl.pallas_call(
        kernel,
        grid=(len(keep),),
        in_specs=[
            pl.BlockSpec(block, lambda i: (keep[0] + i * stride, 0)),
            pl.BlockSpec(block, lambda i: (i, 0)),
        ],
        out_specs=pl.BlockSpec(block, lambda i: (i, 0)),
        out_shape=jax.ShapeDtypeStruct(come.shape, kind),
        cost_estimate=LIGHT,
        name="add_blocks",
    )(half, come)


class Scatter:
    def __init__(self, first, second):
        bits = plane_bits()
        evens = list(range(0, lax.axis_size("dp"), 2))
        self.members = [
            [order, half, evens]
            for group, order in ((first, bits), (second, bits[::-1]))
            for half in group
        ]
        self.taken = 0
        self.come = None

    def send(self, *gate):
        self.come = []
        self.sent = []
        for order, half, blocks in self.members:
            sent = [block for block in blocks if block & order[self.taken]]
            piece = blocks_of([(half, blocks)], sent)
            piece = after(piece, *gate) if gate else piece
            self.sent.append(piece)
            self.come.append(flip(piece, order[self.taken]))
        self.taken += 1
        return self

    def settle(self, *late):
        last = self.taken == len(plane_bits())
        late = late + tuple(self.come)
        for member, come in zip(self.members, self.come):
            order, half, blocks = member
            keep = [block for block in blocks if not block & order[self.taken - 1]]
            if late:
                come = after(come, *late)
            spots = [blocks.index(block) for block in keep]
            member[1:] = [
                add_blocks(half, len(blocks), spots, come, F32 if last else BF16),
                keep,
            ]
        self.come = None
        return self

    def now(self):
        return [half for _, half, _ in self.members]

    def finish(self, *late):
        if self.come:
            self.settle(*late)
        while self.taken < len(plane_bits()):
            self.send()
            self.settle(*late)
        return [half.astype(F32) for _, half, _ in self.members]


def turned_product(features, values, side, extra=None):
    rows, depth = features.shape
    columns = values.shape[1]
    tile = 256
    steps = depth // 2 // tile

    def kernel(left_ref, right_ref, *refs):
        total = matmul(left_ref[...].T, right_ref[...])
        if extra is not None:
            total = total + refs[0][...].astype(F32)
        refs[-1][...] = total.astype(BF16)

    tiles = pl.BlockSpec((tile, columns), lambda i: (i, 0))
    return pl.pallas_call(
        kernel,
        grid=(steps,),
        in_specs=[
            pl.BlockSpec((rows, tile), lambda i: (0, i + side * steps)),
            pl.BlockSpec((rows, columns), lambda i: (0, 0)),
        ]
        + ([tiles] if extra is not None else []),
        out_specs=tiles,
        out_shape=jax.ShapeDtypeStruct((depth // 2, columns), BF16),
        cost_estimate=LIGHT,
        name="turned_product",
    )(features, values, *([extra] if extra is not None else []))


def gradient_half(features, values, kernel=False):
    if kernel:
        return turned_product(features, values, 0, flip(turned_product(features, values, 1), 1))
    half = features.shape[1] // 2
    far = contract_rows(features[:, half:], values).astype(BF16)
    near = contract_rows(features[:, :half], values) + flip(far, 1).astype(F32)
    return near.astype(BF16)


def plain_product(total):
    return (total,)


def round_product(total):
    return (total.astype(BF16),)


def gelu_both(total, bias):
    value = total + bias
    return value, gelu_tanh(value).astype(BF16)


def gelu_slope(values):
    factor = 0.7978845608028654
    square = values * values
    wave = jnp.tanh(factor * (values + 0.044715 * (square * values)))
    return 0.5 * (1.0 + wave) + (0.5 * factor) * values * (1.0 - wave * wave) * (
        1.0 + (3.0 * 0.044715) * square
    )


def gelu_and_back(total, bias, act_grad):
    value = total + bias
    return gelu_tanh(value).astype(BF16), (act_grad * gelu_slope(value)).astype(BF16)


def gelu_back(total, value):
    return ((total * gelu_slope(value)).astype(BF16),)


def times(left, parts, finish, extras, types):
    rows, depth = left.shape
    columns = parts[0][0].shape[1]
    height = depth // lax.axis_size("dp")
    place = {block: i for i, block in enumerate(slot_order())}
    if height % 128:
        return finish(matmul(left, blocks_of(parts, slot_order())), *extras)
    tile = next(size for size in (768, 640, 512, 384, 256, 128, columns) if columns % size == 0)
    spots = [[place[block] * height for block in blocks] for _, blocks in parts]

    def kernel(left_ref, *refs):
        part_refs = refs[: len(parts)]
        extra_refs = refs[len(parts) : len(parts) + len(extras)]
        total = None
        for ref, starts in zip(part_refs, spots):
            for i, start in enumerate(starts):
                piece = matmul(
                    left_ref[:, start : start + height], ref[i * height : (i + 1) * height, :]
                )
                total = piece if total is None else total + piece
        values = finish(total, *[ref[...] for ref in extra_refs])
        for ref, value in zip(refs[len(parts) + len(extras) :], values):
            ref[...] = value

    return pl.pallas_call(
        kernel,
        grid=(columns // tile,),
        in_specs=[pl.BlockSpec((rows, depth), lambda j: (0, 0))]
        + [pl.BlockSpec((array.shape[0], tile), lambda j: (0, j)) for array, _ in parts]
        + [pl.BlockSpec((extra.shape[0], tile), lambda j: (0, j)) for extra in extras],
        out_specs=[pl.BlockSpec((rows, tile), lambda j: (0, j)) for _ in types],
        out_shape=[jax.ShapeDtypeStruct((rows, columns), kind) for kind in types],
        cost_estimate=LIGHT,
        name="times",
    )(left, *[array for array, _ in parts], *extras)


def times_turned(left, parts, kind):
    rows, depth = left.shape
    count = lax.axis_size("dp")
    height = sum(array.shape[0] for array, _ in parts) // count
    place = {block: i for i, block in enumerate(slot_order())}
    if height % 128:
        return contract_cols(left, blocks_of(parts, slot_order())).astype(kind)
    tile = 256 if rows % 256 == 0 else rows
    spots = [[place[block] * height for block in blocks] for _, blocks in parts]

    def kernel(left_ref, *refs):
        for ref, starts in zip(refs, spots):
            for i, start in enumerate(starts):
                piece = contract_cols(left_ref[...], ref[i * height : (i + 1) * height, :])
                refs[-1][:, start : start + height] = piece.astype(kind)

    whole = [
        pl.BlockSpec(array.shape, lambda i: (0, 0), pipeline_mode=pl.Buffered(1))
        for array, _ in parts
    ]
    return pl.pallas_call(
        kernel,
        grid=(rows // tile,),
        in_specs=[pl.BlockSpec((tile, depth), lambda i: (i, 0))] + whole,
        out_specs=pl.BlockSpec((tile, count * height), lambda i: (i, 0)),
        out_shape=jax.ShapeDtypeStruct((rows, count * height), kind),
        cost_estimate=LIGHT,
        name="times_turned",
    )(left, *[array for array, _ in parts])


def arrays_of(*weights):
    return [array for parts in weights for array, _ in parts]


def tensor_swap(values):
    return lax.all_to_all(values, "tensor", split_axis=0, concat_axis=0, tiled=True)


def tensor_rows(values):
    return lax.all_gather(values, "tensor", axis=0, tiled=True)


def tensor_sum(values):
    return lax.psum_scatter(values, "tensor", scatter_dimension=0, tiled=True)


def stack_columns(whole, count):
    width = whole.shape[1] // count
    whole = whole.astype(BF16)
    return jnp.concatenate([whole[:, k * width : (k + 1) * width] for k in range(count)], axis=0)


def stack_query(whole, width, query_cols, pair_cols):
    rows = whole.shape[0]
    whole = whole.astype(BF16)
    pieces = []
    for k in range(width // query_cols):
        pieces.append(whole[:, k * query_cols : (k + 1) * query_cols])
        pair = whole[:, width + k * pair_cols : width + (k + 1) * pair_cols]
        pieces.append(pair.reshape(rows * pair_cols // query_cols, query_cols))
    return jnp.concatenate(pieces, axis=0)


def split_query(total, rows, pair_cols):
    total = total.astype(F32)
    return total[:rows], total[rows:].reshape(rows, pair_cols)


def copy_block(table, source, target):
    target[...] = source[...]


def reorder(values, table):
    rows, columns = values.shape
    count = table.shape[0]
    width = columns // count
    if width % 128:
        return jnp.take(values.reshape(rows, count, width), table, axis=1).reshape(rows, columns)
    return pl.pallas_call(
        copy_block,
        grid_spec=pltpu.PrefetchScalarGridSpec(
            num_scalar_prefetch=1,
            grid=(count,),
            in_specs=[pl.BlockSpec((rows, width), lambda j, table: (0, table[j]))],
            out_specs=pl.BlockSpec((rows, width), lambda j, table: (0, j)),
        ),
        out_shape=jax.ShapeDtypeStruct(values.shape, values.dtype),
        cost_estimate=LIGHT,
        name="reorder",
    )(table, values)


def stack_heads(block):
    return jnp.concatenate([block[:, :HEAD], block[:, HEAD:]], axis=0)


def attend_kernel(scale, query_ref, key_ref, value_t_ref, bias_ref, out_ref, log_ref):
    rows = query_ref.shape[0]
    queries = stack_heads(query_ref[...])
    scores = contract_cols(key_ref[...], queries) * scale + bias_ref[...]
    top = jnp.max(scores, axis=0, keepdims=True)
    exps = jnp.exp(scores - top)
    total = jnp.sum(exps, axis=0, keepdims=True)
    probs = (exps * (1.0 / total)).astype(BF16)
    mixed = matmul(value_t_ref[...], probs).T.astype(BF16)
    out_ref[:, :HEAD] = mixed[:rows]
    out_ref[:, HEAD:] = mixed[rows:]
    log_ref[0] = top + jnp.log(total)


def attend(queries, key_rows, value_t, bias, scale):
    rows, columns = queries.shape
    pairs = columns // (2 * HEAD)
    keys = key_rows.shape[0]

    def kernel(*refs):
        attend_kernel(scale, *refs)

    return pl.pallas_call(
        kernel,
        grid=(pairs,),
        in_specs=[
            pl.BlockSpec((rows, 2 * HEAD), lambda i: (0, i)),
            pl.BlockSpec((keys, HEAD), lambda i: (0, 0)),
            pl.BlockSpec((HEAD, keys), lambda i: (0, 0)),
            pl.BlockSpec((keys, 2 * rows), lambda i: (0, 0)),
        ],
        out_specs=[
            pl.BlockSpec((rows, 2 * HEAD), lambda i: (0, i)),
            pl.BlockSpec((1, 1, 2 * rows), lambda i: (i, 0, 0)),
        ],
        out_shape=[
            jax.ShapeDtypeStruct((rows, columns), BF16),
            jax.ShapeDtypeStruct((pairs, 1, 2 * rows), F32),
        ],
        cost_estimate=LIGHT,
        name="attend",
    )(queries, key_rows, value_t, bias)


def attend_back_kernel(
    scale, query_ref, dout_ref, key_ref, value_ref, key_t_ref, bias_ref, log_ref, grad_ref, pair_ref
):
    rows = query_ref.shape[0]

    @pl.when(pl.program_id(0) == 0)
    def _():
        pair_ref[...] = jnp.zeros_like(pair_ref)

    queries = stack_heads(query_ref[...])
    douts = stack_heads(dout_ref[...])
    scores = contract_cols(key_ref[...], queries) * scale + bias_ref[...]
    probs = jnp.exp(scores - log_ref[0])
    prob_grad = contract_cols(value_ref[...], douts)
    inner = jnp.sum(probs * prob_grad, axis=0, keepdims=True)
    score_grad = (probs * (prob_grad - inner) * scale).astype(BF16)
    pair_ref[:, :HEAD] += matmul(score_grad, queries)
    pair_ref[:, HEAD:] += matmul(probs.astype(BF16), douts)
    query_grad = matmul(key_t_ref[...], score_grad).T.astype(BF16)
    grad_ref[:, :HEAD] = query_grad[:rows]
    grad_ref[:, HEAD:] = query_grad[rows:]


def attend_back(queries, douts, key_rows, value_rows, key_t, bias, log_totals, scale):
    rows, columns = queries.shape
    pairs = columns // (2 * HEAD)
    keys = key_rows.shape[0]

    def kernel(*refs):
        attend_back_kernel(scale, *refs)

    return pl.pallas_call(
        kernel,
        grid=(pairs,),
        in_specs=[
            pl.BlockSpec((rows, 2 * HEAD), lambda i: (0, i)),
            pl.BlockSpec((rows, 2 * HEAD), lambda i: (0, i)),
            pl.BlockSpec((keys, HEAD), lambda i: (0, 0)),
            pl.BlockSpec((keys, HEAD), lambda i: (0, 0)),
            pl.BlockSpec((HEAD, keys), lambda i: (0, 0)),
            pl.BlockSpec((keys, 2 * rows), lambda i: (0, 0)),
            pl.BlockSpec((1, 1, 2 * rows), lambda i: (i, 0, 0)),
        ],
        out_specs=[
            pl.BlockSpec((rows, 2 * HEAD), lambda i: (0, i)),
            pl.BlockSpec((keys, 2 * HEAD), lambda i: (0, 0)),
        ],
        out_shape=[
            jax.ShapeDtypeStruct((rows, columns), BF16),
            jax.ShapeDtypeStruct((keys, 2 * HEAD), F32),
        ],
        cost_estimate=LIGHT,
        name="attend_back",
    )(queries, douts, key_rows, value_rows, key_t, bias, log_totals)


def local(
    tokens,
    cotangent,
    deal,
    segment,
    norm1_gain,
    norm1_shift,
    query_weight,
    query_bias,
    kv_weight,
    value_bias,
    out_weight,
    out_bias,
    norm2_gain,
    norm2_shift,
    up_weight,
    up_bias,
    down_weight,
    down_bias,
):
    local_rows, width = tokens.shape
    dp_count = lax.axis_size("dp")
    tensor_count = lax.axis_size("tensor")
    dp_rank = lax.axis_index("dp")
    tensor_rank = lax.axis_index("tensor")
    slot_rows = local_rows // dp_count
    layer_total = query_weight.shape[0]
    group_rows = local_rows * tensor_count
    query_cols = query_weight.shape[2]
    pair_cols = kv_weight.shape[2]
    score_scale = HEAD ** (-0.5)
    order = slot_order()
    to_slots = jnp.asarray(order, jnp.int32) ^ dp_rank
    place_of = [order.index(r) for r in range(dp_count)]
    from_slots = jnp.take(
        jnp.asarray(place_of, jnp.int32), jnp.arange(dp_count, dtype=jnp.int32) ^ dp_rank
    )

    target_dev = deal // local_rows // tensor_count
    target_row = deal % local_rows
    dev_ids = jnp.arange(dp_count, dtype=jnp.int32)
    dev_match = (target_dev[:, None] == dev_ids[None, :]).astype(jnp.int32)
    earlier = jnp.cumsum(dev_match, axis=0) - dev_match
    slot_of = target_dev * slot_rows + jnp.sum(earlier * dev_match, axis=1)
    row_ids = jnp.arange(local_rows, dtype=jnp.int32)
    send_table = (row_ids[:, None] == slot_of[None, :]).astype(BF16)
    place_cols = jnp.broadcast_to(target_row.astype(BF16)[:, None], (local_rows, HEAD))
    tokens_sent = matmul(send_table, jnp.concatenate([tokens, place_cols], axis=1)).astype(BF16)
    tokens_come = lax.all_to_all(tokens_sent, "dp", split_axis=0, concat_axis=0, tiled=True)
    tangent_sent = matmul(send_table, cotangent).astype(BF16)
    tangent_come = lax.all_to_all(tangent_sent, "dp", split_axis=0, concat_axis=0, tiled=True)
    arrived_place = tokens_come[:, width].astype(jnp.int32)
    place_table = (row_ids[:, None] == arrived_place[None, :]).astype(BF16)
    stream = reorder(matmul(place_table, tokens_come[:, :width]).astype(BF16), to_slots).astype(F32)
    last_branch = reorder(matmul(place_table, tangent_come).astype(BF16), to_slots)
    tangent = last_branch.astype(F32)
    stream = after(stream, last_branch)

    places = jnp.arange(group_rows, dtype=jnp.int32)
    own_places = tensor_rank * local_rows + row_ids
    own_labels = lax.dynamic_slice_in_dim(segment, tensor_rank * local_rows, local_rows)
    allowed = (places[:, None] <= own_places[None, :]) & (
        segment[:, None] == own_labels[None, :]
    )
    score_bias = jnp.where(allowed, 0.0, -1e30).astype(F32)
    score_bias = jnp.concatenate([score_bias, score_bias], axis=1)

    def product(left, weights):
        pieces = [times(left, parts, plain_product, (), (F32,))[0] for parts in weights]
        return pieces[0] if len(pieces) == 1 else jnp.concatenate(pieces, axis=1)

    def product_turned(left, weights):
        total, start = None, 0
        for parts in weights:
            size = parts[0][0].shape[1]
            piece = times_turned(left[:, start : start + size], parts, F32)
            total = piece if total is None else total + piece
            start += size
        return total

    last = layer_total - 1
    split = width // 2
    cut = tensor_count // 2
    depth = query_weight.shape[1]
    pair_rows = depth * pair_cols // query_cols
    bias_rows = 16

    def query_payload(l):
        rest, terms = query_bias[l], []
        for _ in range(3):
            terms.append(rest.astype(BF16))
            rest = rest - terms[-1].astype(F32)
        terms = jnp.pad(jnp.stack(terms), ((0, bias_rows - 3), (0, 0)))
        return jnp.concatenate(
            [query_weight[l], kv_weight[l].reshape(pair_rows, query_cols), terms], axis=0
        )

    def query_parts(rows):
        size = rows.shape[0] // tensor_count
        each = [rows[k * size : (k + 1) * size] for k in range(tensor_count)]
        pair = [part[depth : depth + pair_rows].reshape(depth, pair_cols) for part in each]
        bias = [
            sum(part[depth + pair_rows + i].astype(F32) for i in range(3)) for part in each
        ]
        return (
            [part[:depth] for part in each],
            jnp.concatenate(pair, axis=1),
            jnp.concatenate(bias),
        )

    def columns(rows):
        count = rows.shape[0] // depth
        return jnp.concatenate([rows[k * depth : (k + 1) * depth] for k in range(count)], axis=1)

    out_turned = [out_weight[l].T for l in range(layer_total)]
    down_turned = [down_weight[l].T for l in range(layer_total)]
    query_rows = tensor_rows(query_payload(0))
    out_rows = tensor_rows(after(out_turned[0], tangent_come))
    if last > 0:
        rest = jnp.concatenate([query_payload(1), out_turned[1]], axis=0)
        rest = tensor_rows(after(rest, tokens_come))
        size = rest.shape[0] // tensor_count
        rest = [rest[k * size : (k + 1) * size] for k in range(tensor_count)]
    query_rows = after(query_rows, tokens_come, tangent_come, score_bias)
    cut_rows = cut * depth
    query_each, kv_full, bias_full = query_parts(query_rows)
    query_gather = Gather(
        [jnp.concatenate(query_each[:cut], axis=1)],
        [jnp.concatenate(query_each[cut:] + [kv_full], axis=1)],
    ).send()
    out_gather = Gather([columns(out_rows[:cut_rows])], [columns(out_rows[cut_rows:])]).send(
        *query_gather.come
    )
    w_query = query_gather.finish()
    early_rows = local_rows // 2
    if last > 0:
        query_rows = jnp.concatenate([part[: size - depth] for part in rest], axis=0)
        out_rows = jnp.concatenate([part[size - depth :] for part in rest], axis=0)
        branch_early = tensor_rows(last_branch[:early_rows])

    def branch_whole(early, late):
        parts = []
        for k in range(tensor_count):
            parts.append(early[k * early_rows : (k + 1) * early_rows])
            size = local_rows - early_rows
            parts.append(late[k * size : (k + 1) * size])
        return jnp.concatenate(parts, axis=0)

    vectors = jnp.concatenate(
        [norm1_gain, norm1_shift, out_bias, norm2_gain, norm2_shift, down_bias], axis=0
    )
    vectors = reorder(vectors, to_slots)
    gain_one, shift_one, bias_out, gain_two, shift_two, bias_down = [
        vectors[i * layer_total : (i + 1) * layer_total] for i in range(6)
    ]

    def rows_back(values):
        slots_out = contract_rows(place_table, reorder(values, from_slots)).astype(BF16)
        come = lax.all_to_all(slots_out, "dp", split_axis=0, concat_axis=0, tiled=True)
        return slots_out, come

    saved = []
    for l in range(layer_total):
        if 0 < l < last:
            query_rows = tensor_rows(after(query_payload(l + 1), out_rows))
            out_rows = tensor_rows(after(out_turned[l + 1], query_rows))
        normed = layer_norm(stream, gain_one[l], shift_one[l]).astype(BF16)
        projected = product(normed, w_query)
        pair_bias = jnp.concatenate([jnp.zeros((HEAD,), F32), value_bias[l]])
        pair_own = (projected[:, width:] + pair_bias).astype(BF16)
        queries = (projected[:, :width] + bias_full).astype(BF16)
        pair_all = tensor_swap(jnp.concatenate([pair_own] * tensor_count))
        pair_t = pair_all.T
        if l == 0:
            w_out = out_gather.settle(projected).finish(projected)
            queries = after(queries, *arrays_of(*w_out)[:2])
            ff_gather = Gather([up_weight[0]], [down_turned[0]]).send(pair_all)
        mixed, log_totals = attend(
            queries, pair_all[:, :HEAD], pair_t[HEAD:], score_bias, score_scale
        )
        if l > 0:
            mixed = after(mixed, *ff_gather.come)
            w_up, w_down = ff_gather.settle(mixed).finish(mixed)
        hidden_state = stream + product_turned(mixed, w_out) + bias_out[l]
        normed_two = layer_norm(hidden_state, gain_two[l], shift_two[l]).astype(BF16)
        if l == 0:
            normed_two = after(normed_two, *ff_gather.come)
            w_up, w_down = ff_gather.settle(normed_two).finish(normed_two)
        if l == 0 and last > 0:
            normed_two = after(normed_two, branch_early)
        normed_two_all = tensor_rows(normed_two)
        normed_two_all = after(normed_two_all, *arrays_of(w_up, w_down))
        if l == last:
            if last == 0:
                branch_all = tensor_rows(last_branch)
            act_grad = times(branch_all, w_down, plain_product, (), (F32,))[0]
            normed_two_all = after(normed_two_all, act_grad)
            activation, pre_grad = times(
                normed_two_all, w_up, gelu_and_back, (up_bias[l][None], act_grad), (BF16, BF16)
            )
            pre_gelu = None
        else:
            pre_gelu, activation = times(
                normed_two_all, w_up, gelu_both, (up_bias[l][None],), (F32, BF16)
            )
        saved.append(
            (
                stream,
                normed,
                queries,
                pair_all,
                pair_t,
                log_totals,
                mixed,
                hidden_state,
                normed_two_all,
                pre_gelu,
                activation,
                w_query,
                w_out,
                w_up,
                w_down,
            )
        )
        if l < last:
            query_each, kv_full, bias_full = query_parts(query_rows)
            attn_gather = Gather(
                [jnp.concatenate(query_each + [kv_full], axis=1)], [columns(out_rows)]
            )
            attn_gather.send(normed_two_all)
            down_part = times_turned(activation, w_down, BF16)
            down_part = after(down_part, *attn_gather.come)
            down_sum = tensor_sum(down_part)
            ff_gather = Gather([up_weight[l + 1]], [down_turned[l + 1]]).send(down_sum)
            w_query, w_out = [[parts] for parts in attn_gather.settle(down_part).finish(down_part)]
            if l == last - 1:
                sent = after(last_branch[early_rows:], w_query[0][0][0], w_out[0][0][0])
                branch_all = branch_whole(branch_early, tensor_rows(sent))
            down_sum = after(down_sum, *arrays_of(*w_query, *w_out))
            stream = hidden_state + down_sum.astype(F32) + bias_down[l]

    reduced = [None] * layer_total
    vector_grads = [None] * layer_total
    query_bias_grads = [None] * layer_total
    value_bias_grads = [None] * layer_total
    up_bias_grads = [None] * layer_total
    later = None
    for l in reversed(range(layer_total)):
        (
            stream_in,
            normed,
            queries,
            pair_all,
            pair_t,
            log_totals,
            mixed,
            hidden_state,
            normed_two_all,
            pre_gelu,
            activation,
            w_query,
            w_out,
            w_up,
            w_down,
        ) = saved[l]
        branch_grad = tangent.astype(BF16)
        if l == last - 1:
            branch_grad, final_sum = lax.optimization_barrier((branch_grad, final_sum))
        if l < last:
            branch_all = tensor_rows(branch_grad)
            above, both_above, normed_above, attn_above, mixed_above, ff_scatter = later
            ff_scatter.settle(branch_grad).send()
            both_late, attn_late = after((both_above, attn_above), branch_grad, *ff_scatter.now())
            attn_scatter = Scatter(
                [gradient_half(normed_above, both_late, True)],
                [gradient_half(attn_late, mixed_above, True)],
            )
            attn_scatter.send()
            beside = ff_scatter.sent + attn_scatter.sent
            if above == last:
                final_sum = after(final_sum, *beside)
                layer_out = (saved[last][7] + final_sum.astype(F32) + bias_down[last]).astype(BF16)
                out_slots, out_back = rows_back(layer_out)
                beside.append(out_slots)
            branch_all = after(branch_all, *beside)
            pre_grad = times(branch_all, w_down, gelu_back, (pre_gelu,), (BF16,))[0]
        normed_part = times_turned(pre_grad, w_up, BF16)
        if l < last:
            normed_part = after(normed_part, *ff_scatter.come, *attn_scatter.come)
        normed_two_grad = tensor_sum(normed_part)
        beside = []
        if l < last:
            attn_scatter.settle(normed_part).send()
            up_grad, down_grad = ff_scatter.finish(normed_part)
            reduced[above] = (up_grad, down_grad.T)
            beside += [up_grad, down_grad] + attn_scatter.sent
        pre_late, branch_late = after((pre_grad, branch_all), normed_part)
        ff_scatter = Scatter(
            [gradient_half(normed_two_all, pre_late, True)],
            [gradient_half(branch_late, activation, True)],
        )
        ff_scatter.send()
        beside += ff_scatter.now() + ff_scatter.sent
        down_bias_part = jnp.sum(after(branch_grad, normed_part).astype(F32), axis=0)
        up_bias_grads[l] = jnp.sum(pre_late.astype(F32), axis=0)
        beside += [down_bias_part, up_bias_grads[l]]
        if l == last:
            final_part = times_turned(after(activation, *ff_scatter.sent), w_down, BF16)
            beside.append(final_part)
        else:
            both_whole, out_whole = attn_scatter.finish(*ff_scatter.now())
            out_stack = stack_columns(out_whole, tensor_count)
            query_stack = stack_query(both_whole, width, query_cols, pair_cols)
            beside += [out_stack, query_stack]
        normed_two_grad = after(normed_two_grad, *beside)
        if l == last:
            final_sum = tensor_sum(after(final_part, normed_two_grad))
        else:
            out_grad = tensor_sum(after(out_stack, normed_two_grad)).astype(F32).T
            query_sum = tensor_sum(after(query_stack, normed_two_grad))
            query_w_grad, kv_grad = split_query(query_sum, depth, pair_cols)
            reduced[above] = (query_w_grad, kv_grad, out_grad) + reduced[above]
        hidden_part, gain_two_part, shift_two_part = jax.vjp(
            layer_norm, hidden_state, gain_two[l], shift_two[l]
        )[1](normed_two_grad.astype(F32))
        hidden_grad = tangent + hidden_part
        attn_grad = hidden_grad.astype(BF16)
        out_bias_part = jnp.sum(attn_grad.astype(F32), axis=0)
        mixed_grad = product(attn_grad, w_out).astype(BF16)
        if l == 0:
            attn_late = after(attn_grad, mixed_grad)
            out_scatter = Scatter(
                [gradient_half(attn_late, mixed[:, :split])],
                [gradient_half(attn_late, mixed[:, split:])],
            ).send()
            mixed_grad = after(mixed_grad, *out_scatter.sent)
        elif l == last:
            mixed_grad = after(mixed_grad, *ff_scatter.come)
        query_grad, pair_part = attend_back(
            queries,
            mixed_grad,
            pair_all[:, :HEAD],
            pair_all[:, HEAD:],
            pair_t[:HEAD],
            score_bias,
            log_totals,
            score_scale,
        )
        pair_come = tensor_swap(pair_part.astype(BF16))
        pair_grad = sum(
            pair_come[k * local_rows : (k + 1) * local_rows].astype(F32)
            for k in range(tensor_count)
        ).astype(BF16)
        query_bias_grads[l] = jnp.sum(query_grad.astype(F32), axis=0)
        value_bias_grads[l] = jnp.sum(pair_grad[:, HEAD:].astype(F32), axis=0)
        both_grad = jnp.concatenate([query_grad, pair_grad], axis=1)
        if l == 0:
            both_grad = after(both_grad, *ff_scatter.come)
            both_scatter = Scatter(
                [gradient_half(normed, both_grad[:, :split])],
                [gradient_half(normed, both_grad[:, split:])],
            ).send()
            out_scatter.settle(*both_scatter.sent).send()
            ff_scatter.settle(*out_scatter.sent).send()
            both_grad = after(both_grad, *both_scatter.sent, *out_scatter.sent, *ff_scatter.sent)
        normed_grad = product_turned(both_grad, w_query)
        stream_part, gain_one_part, shift_one_part = jax.vjp(
            layer_norm, stream_in, gain_one[l], shift_one[l]
        )[1](normed_grad)
        tangent = hidden_grad + stream_part
        later = (l, both_grad, normed, attn_grad, mixed, ff_scatter)
        vector_grads[l] = [
            gain_one_part,
            shift_one_part,
            out_bias_part,
            gain_two_part,
            shift_two_part,
            down_bias_part,
        ]
    stacked = jnp.stack([vector_grads[l][m] for m in range(6) for l in range(layer_total)])
    stacked = reorder(stacked, from_slots)
    query_rows = jnp.stack(query_bias_grads)
    value_rows = jnp.pad(jnp.stack(value_bias_grads), ((0, 0), (0, width - HEAD)))
    smalls = jnp.concatenate([stacked, query_rows, value_rows], axis=0)
    small_count = smalls.shape[0]
    smalls = jnp.concatenate([smalls, jnp.stack(up_bias_grads)], axis=0)
    smalls = smalls + flip(smalls, 1)
    total = smalls[:small_count]
    if tensor_count & (tensor_count - 1) == 0:
        for k in range(tensor_count.bit_length() - 1):
            total = total + lax.ppermute(
                total, "tensor", [(i, i ^ (1 << k)) for i in range(tensor_count)]
            )
    else:
        total = lax.psum(total, "tensor")
    total = jnp.concatenate([total, smalls[small_count:]], axis=0)
    for bit in plane_bits():
        total = total + flip(total, bit)
    up_bias_grad = total[small_count:]
    vector_sums = [total[m * layer_total : (m + 1) * layer_total] for m in range(8)]
    query_bias_grad = lax.dynamic_slice_in_dim(
        vector_sums[6], tensor_rank * query_cols, query_cols, 1
    )
    value_bias_grad = vector_sums[7][:, :HEAD]

    grad_back = rows_back(tangent.astype(BF16))[1]
    out_back = after(out_back, tangent)
    both_scatter.settle(normed_grad).send()
    out_whole = jnp.concatenate(out_scatter.finish(), axis=1)
    out_grad = tensor_sum(stack_columns(out_whole, tensor_count)).astype(F32).T
    both_whole = jnp.concatenate(both_scatter.finish(), axis=1)
    query_stack = stack_query(both_whole, width, query_cols, pair_cols)
    query_w_grad, kv_grad = split_query(tensor_sum(query_stack), depth, pair_cols)
    up_grad, down_grad = ff_scatter.finish()
    reduced[0] = (query_w_grad, kv_grad, out_grad, up_grad, down_grad.T)
    if last == 0:
        layer_out = (saved[last][7] + final_sum.astype(F32) + bias_down[last]).astype(BF16)
        out_back = rows_back(layer_out)[1]
    layer_rows = contract_rows(send_table, out_back).astype(BF16)
    token_rows = contract_rows(send_table, grad_back).astype(BF16)
    summed = [jnp.stack([reduced[l][m] for l in range(layer_total)]) for m in range(5)]
    return (
        layer_rows,
        token_rows,
        vector_sums[0],
        vector_sums[1],
        summed[0],
        query_bias_grad,
        summed[1],
        value_bias_grad,
        summed[2],
        vector_sums[2],
        vector_sums[3],
        vector_sums[4],
        summed[3],
        up_bias_grad,
        summed[4],
        vector_sums[5],
    )


def solution(mesh):
    rows = P(("dp", "tensor"), None)
    in_specs = (
        rows,
        rows,
        P(("dp", "tensor")),
        P("dp"),
        P(),
        P(),
        P(None, "dp", "tensor"),
        P(None, "tensor"),
        P(None, "dp", "tensor"),
        P(),
        P(None, "tensor", "dp"),
        P(),
        P(),
        P(),
        P(None, "dp", "tensor"),
        P(None, "tensor"),
        P(None, "tensor", "dp"),
        P(),
    )
    out_specs = (
        rows,
        rows,
        P(),
        P(),
        P(None, "dp", "tensor"),
        P(None, "tensor"),
        P(None, "dp", "tensor"),
        P(),
        P(None, "tensor", "dp"),
        P(),
        P(),
        P(),
        P(None, "dp", "tensor"),
        P(None, "tensor"),
        P(None, "tensor", "dp"),
        P(),
    )
    return jax.shard_map(local, mesh=mesh, in_specs=in_specs, out_specs=out_specs, check_vma=False)
```

```python
import jax
import jax.numpy as jnp
from jax import lax
from jax.experimental import pallas as pl
from jax.experimental.pallas import tpu as pltpu
from jax.sharding import PartitionSpec as P

HEAD = 128
EPSILON = 1e-05
BF16 = jnp.bfloat16
F32 = jnp.float32
LIGHT = pl.CostEstimate(flops=1, transcendentals=0, bytes_accessed=1)


def gelu_tanh(values):
    return jax.nn.gelu(values, approximate=True)


def matmul(left, right):
    return jnp.dot(left, right, preferred_element_type=F32)


def contract_rows(left, right):
    return lax.dot_general(left, right, (((0,), (0,)), ((), ())), preferred_element_type=F32)


def contract_cols(left, right):
    return lax.dot_general(left, right, (((1,), (1,)), ((), ())), preferred_element_type=F32)


def after(values, *others):
    return lax.optimization_barrier((values, others))[0]


def flip(values, bit):
    count = lax.axis_size("dp")
    return lax.ppermute(values, "dp", [(i, i ^ bit) for i in range(count)])


def turn(values, step):
    count = lax.axis_size("tensor")
    return lax.ppermute(values, "tensor", [((i + step) % count, i) for i in range(count)])


def plane_bits():
    count = lax.axis_size("dp")
    return [1 << k for k in range(1, count.bit_length() - 1)]


def slot_order():
    count = lax.axis_size("dp")
    evens = list(range(0, count, 2))
    return evens + [r ^ 1 for r in evens]


def join_rows(arrays):
    return arrays[0] if len(arrays) == 1 else jnp.concatenate(arrays, axis=0)


def blocks_of(parts, wanted):
    runs = []
    where = {}
    for array, blocks in parts:
        rows = array.shape[0] // len(blocks)
        for i, block in enumerate(blocks):
            where[block] = (array, i * rows, rows)
    for block in wanted:
        array, start, rows = where[block]
        if runs and runs[-1][0] is array and runs[-1][2] == start:
            runs[-1][2] += rows
        else:
            runs.append([array, start, start + rows])
    return join_rows([lax.slice_in_dim(array, low, high) for array, low, high in runs])


class Gather:
    def __init__(self, first, second):
        bits = plane_bits()
        self.members = [
            [order, [(array, [0])]]
            for group, order in ((first, bits), (second, bits[::-1]))
            for array in group
        ]
        self.taken = 0
        self.come = []

    def send(self, *gate):
        gate = gate + tuple(self.come)
        self.come = []
        for member in self.members:
            order, parts = member
            bit = order[self.taken]
            blocks = [block for _, part in parts for block in part]
            whole = join_rows([array for array, _ in parts])
            come = flip(after(whole, *gate) if gate else whole, bit)
            self.come.append(come)
            member[1] = [(whole, blocks), (come, [block | bit for block in blocks])]
        self.taken += 1
        return self

    def settle(self, *late):
        for member in self.members:
            own, (come, blocks) = member[1]
            member[1] = [own, (after(come, *late), blocks)]
        return self

    def finish(self, *gate):
        while self.taken < len(plane_bits()):
            self.send(*gate)
        return [
            parts + [(flip(array, 1), [block | 1 for block in blocks]) for array, blocks in parts]
            for _, parts in self.members
        ]


def add_blocks(half, count, keep, come, kind):
    rows, columns = half.shape[0] // count, half.shape[1]
    stride = keep[1] - keep[0] if len(keep) > 1 else 1

    def kernel(half_ref, come_ref, out_ref):
        out_ref[...] = (half_ref[...].astype(F32) + come_ref[...].astype(F32)).astype(kind)

    block = (rows, columns)
    return pl.pallas_call(
        kernel,
        grid=(len(keep),),
        in_specs=[
            pl.BlockSpec(block, lambda i: (keep[0] + i * stride, 0)),
            pl.BlockSpec(block, lambda i: (i, 0)),
        ],
        out_specs=pl.BlockSpec(block, lambda i: (i, 0)),
        out_shape=jax.ShapeDtypeStruct(come.shape, kind),
        cost_estimate=LIGHT,
        name="add_blocks",
    )(half, come)


def take_blocks(half, count, keep):
    rows, columns = half.shape[0] // count, half.shape[1]
    stride = keep[1] - keep[0] if len(keep) > 1 else 1
    block = (rows, columns)
    return pl.pallas_call(
        lambda half_ref, out_ref: out_ref.__setitem__(..., half_ref[...]),
        grid=(len(keep),),
        in_specs=[pl.BlockSpec(block, lambda i: (keep[0] + i * stride, 0))],
        out_specs=pl.BlockSpec(block, lambda i: (i, 0)),
        out_shape=jax.ShapeDtypeStruct((len(keep) * rows, columns), half.dtype),
        cost_estimate=LIGHT,
        name="take_blocks",
    )(half)


def column_sum(values):
    rows, columns = values.shape
    tile = 256 if rows % 256 == 0 else rows

    def kernel(values_ref, out_ref):
        @pl.when(pl.program_id(0) == 0)
        def _():
            out_ref[...] = jnp.zeros_like(out_ref)

        out_ref[...] += jnp.sum(values_ref[...].astype(F32), axis=0, keepdims=True)

    return pl.pallas_call(
        kernel,
        grid=(rows // tile,),
        in_specs=[pl.BlockSpec((tile, columns), lambda i: (i, 0))],
        out_specs=pl.BlockSpec((1, columns), lambda i: (0, 0)),
        out_shape=jax.ShapeDtypeStruct((1, columns), F32),
        cost_estimate=LIGHT,
        name="column_sum",
    )(values)[0]


class Scatter:
    def __init__(self, first, second):
        bits = plane_bits()
        evens = list(range(0, lax.axis_size("dp"), 2))
        self.members = [
            [order, half, evens]
            for group, order in ((first, bits), (second, bits[::-1]))
            for half in group
        ]
        self.taken = 0
        self.come = None

    def send(self, *gate):
        self.come = []
        self.sent = []
        for order, half, blocks in self.members:
            spots = [i for i, block in enumerate(blocks) if block & order[self.taken]]
            piece = take_blocks(half, len(blocks), spots)
            piece = after(piece, *gate) if gate else piece
            self.sent.append(piece)
            self.come.append(flip(piece, order[self.taken]))
        self.taken += 1
        return self

    def settle(self, *late):
        last = self.taken == len(plane_bits())
        late = late + tuple(self.come)
        for member, come in zip(self.members, self.come):
            order, half, blocks = member
            keep = [block for block in blocks if not block & order[self.taken - 1]]
            if late:
                come = after(come, *late)
            spots = [blocks.index(block) for block in keep]
            member[1:] = [
                add_blocks(half, len(blocks), spots, come, F32 if last else BF16),
                keep,
            ]
        self.come = None
        return self

    def now(self):
        return [half for _, half, _ in self.members]

    def open_sum(self, member):
        while self.taken < len(plane_bits()):
            self.settle()
            self.send()
        order, half, blocks = self.members[member]
        spot = next(i for i, block in enumerate(blocks) if not block & order[-1])
        return half, len(blocks), spot, self.come[member]

    def finish(self, *late):
        if self.come:
            self.settle(*late)
        while self.taken < len(plane_bits()):
            self.send()
            self.settle(*late)
        return [half.astype(F32) for _, half, _ in self.members]


def stack_sums(items, turned):
    rows, columns = items[0][3].shape
    shape = (1, columns, rows) if turned else (1, rows, columns)

    def kernel(*refs):
        for l in range(len(items)):

            @pl.when(pl.program_id(0) == l)
            def _():
                total = refs[2 * l][...].astype(F32) + refs[2 * l + 1][...].astype(F32)
                refs[-1][0] = total.T if turned else total

    specs, arrays = [], []
    for half, _, spot, come in items:
        specs.append(pl.BlockSpec((rows, columns), lambda l, spot=spot: (spot, 0)))
        specs.append(pl.BlockSpec((rows, columns), lambda l: (0, 0)))
        arrays += [half, come]
    return pl.pallas_call(
        kernel,
        grid=(len(items),),
        in_specs=specs,
        out_specs=pl.BlockSpec(shape, lambda l: (l, 0, 0)),
        out_shape=jax.ShapeDtypeStruct((len(items),) + shape[1:], F32),
        cost_estimate=LIGHT,
        name="stack_sums",
    )(*arrays)


def turned_product(features, values, side, extra=None):
    rows, depth = features.shape
    columns = values.shape[1]
    tile = 256
    steps = depth // 2 // tile

    def kernel(left_ref, right_ref, *refs):
        total = matmul(left_ref[...].T, right_ref[...])
        if extra is not None:
            total = total + refs[0][...].astype(F32)
        refs[-1][...] = total.astype(BF16)

    tiles = pl.BlockSpec((tile, columns), lambda i: (i, 0))
    return pl.pallas_call(
        kernel,
        grid=(steps,),
        in_specs=[
            pl.BlockSpec((rows, tile), lambda i: (0, i + side * steps)),
            pl.BlockSpec((rows, columns), lambda i: (0, 0)),
        ]
        + ([tiles] if extra is not None else []),
        out_specs=tiles,
        out_shape=jax.ShapeDtypeStruct((depth // 2, columns), BF16),
        cost_estimate=LIGHT,
        name="turned_product",
    )(features, values, *([extra] if extra is not None else []))


def gradient_half(features, values, kernel=False):
    if kernel:
        return turned_product(features, values, 0, flip(turned_product(features, values, 1), 1))
    half = features.shape[1] // 2
    far = contract_rows(features[:, half:], values).astype(BF16)
    near = contract_rows(features[:, :half], values) + flip(far, 1).astype(F32)
    return near.astype(BF16)


def norm_parts(values):
    centred = values - jnp.mean(values, axis=-1, keepdims=True)
    return centred, lax.rsqrt(jnp.mean(centred * centred, axis=-1, keepdims=True) + EPSILON)


def row_tile(rows):
    return 64 if rows % 64 == 0 else rows


def add_and_norm(base, part, bias, gain, shift):
    rows, width = base.shape
    tile = row_tile(rows)
    wide = pl.BlockSpec((tile, width), lambda i: (i, 0))
    line = pl.BlockSpec((1, width), lambda i: (0, 0))
    added = [] if part is None else [part, bias]

    def kernel(gain_ref, shift_ref, base_ref, *refs):
        total = base_ref[...].astype(F32)
        if part is not None:
            total = total + refs[0][...].astype(F32) + refs[1][...]
        centred, slope = norm_parts(total)
        refs[-2][...] = total
        refs[-1][...] = (centred * slope * gain_ref[...] + shift_ref[...]).astype(BF16)

    return pl.pallas_call(
        kernel,
        grid=(rows // tile,),
        in_specs=[line, line, wide] + [wide, line][: len(added)],
        out_specs=[wide, wide],
        out_shape=[
            jax.ShapeDtypeStruct((rows, width), F32),
            jax.ShapeDtypeStruct((rows, width), BF16),
        ],
        cost_estimate=LIGHT,
        name="add_and_norm",
    )(gain, shift, base, *added)


def norm_back(values, grad, gain, tangent):
    rows, width = values.shape
    tile = row_tile(rows)
    wide = pl.BlockSpec((tile, width), lambda i: (i, 0))

    def kernel(gain_ref, values_ref, grad_ref, tangent_ref, out_ref, low_ref, sums_ref):
        centred, slope = norm_parts(values_ref[...])
        scaled = centred * slope
        grads = grad_ref[...].astype(F32)
        inner = grads * gain_ref[...]
        mean_inner = jnp.mean(inner, axis=-1, keepdims=True)
        mean_scaled = jnp.mean(inner * scaled, axis=-1, keepdims=True)
        total = tangent_ref[...] + slope * (inner - mean_inner - scaled * mean_scaled)
        low = total.astype(BF16)
        out_ref[...] = total
        low_ref[...] = low

        @pl.when(pl.program_id(0) == 0)
        def _():
            sums_ref[...] = jnp.zeros_like(sums_ref)

        for i, term in enumerate((grads * scaled, grads, low.astype(F32))):
            sums_ref[i : i + 1, :] += jnp.sum(term, axis=0, keepdims=True)

    return pl.pallas_call(
        kernel,
        grid=(rows // tile,),
        in_specs=[pl.BlockSpec((1, width), lambda i: (0, 0)), wide, wide, wide],
        out_specs=[wide, wide, pl.BlockSpec((8, width), lambda i: (0, 0))],
        out_shape=[
            jax.ShapeDtypeStruct((rows, width), F32),
            jax.ShapeDtypeStruct((rows, width), BF16),
            jax.ShapeDtypeStruct((8, width), F32),
        ],
        cost_estimate=LIGHT,
        name="norm_back",
    )(gain, values, grad, tangent)


def plain_product(total):
    return (total,)


def round_product(total):
    return (total.astype(BF16),)


def bias_round(total, bias):
    return ((total + bias).astype(BF16),)


def gelu_both(total, bias):
    value = total + bias
    return value, gelu_tanh(value).astype(BF16)


def gelu_slope(values):
    factor = 0.7978845608028654
    square = values * values
    wave = jnp.tanh(factor * (values + 0.044715 * (square * values)))
    return 0.5 * (1.0 + wave) + (0.5 * factor) * values * (1.0 - wave * wave) * (
        1.0 + (3.0 * 0.044715) * square
    )


def gelu_and_back(total, bias, act_grad):
    value = total + bias
    return gelu_tanh(value).astype(BF16), (act_grad * gelu_slope(value)).astype(BF16)


def gelu_back(total, value):
    return ((total * gelu_slope(value)).astype(BF16),)


def times(left, parts, finish, extras, types):
    rows, depth = left.shape
    columns = parts[0][0].shape[1]
    height = depth // lax.axis_size("dp")
    place = {block: i for i, block in enumerate(slot_order())}
    if height % 128:
        return finish(matmul(left, blocks_of(parts, slot_order())), *extras)
    tile = next(size for size in (768, 640, 512, 384, 256, 128, columns) if columns % size == 0)
    spots = [[place[block] * height for block in blocks] for _, blocks in parts]

    def kernel(left_ref, *refs):
        part_refs = refs[: len(parts)]
        extra_refs = refs[len(parts) : len(parts) + len(extras)]
        total = None
        for ref, starts in zip(part_refs, spots):
            for i, start in enumerate(starts):
                piece = matmul(
                    left_ref[:, start : start + height], ref[i * height : (i + 1) * height, :]
                )
                total = piece if total is None else total + piece
        values = finish(total, *[ref[...] for ref in extra_refs])
        for ref, value in zip(refs[len(parts) + len(extras) :], values):
            ref[...] = value

    return pl.pallas_call(
        kernel,
        grid=(columns // tile,),
        in_specs=[pl.BlockSpec((rows, depth), lambda j: (0, 0))]
        + [pl.BlockSpec((array.shape[0], tile), lambda j: (0, j)) for array, _ in parts]
        + [pl.BlockSpec((extra.shape[0], tile), lambda j: (0, j)) for extra in extras],
        out_specs=[pl.BlockSpec((rows, tile), lambda j: (0, j)) for _ in types],
        out_shape=[jax.ShapeDtypeStruct((rows, columns), kind) for kind in types],
        cost_estimate=LIGHT,
        name="times",
    )(left, *[array for array, _ in parts], *extras)


def times_turned(left, parts, kind):
    rows, depth = left.shape
    count = lax.axis_size("dp")
    height = sum(array.shape[0] for array, _ in parts) // count
    place = {block: i for i, block in enumerate(slot_order())}
    if height % 128:
        return contract_cols(left, blocks_of(parts, slot_order())).astype(kind)
    tile = 256 if rows % 256 == 0 else rows
    spots = [[place[block] * height for block in blocks] for _, blocks in parts]

    def kernel(left_ref, *refs):
        for ref, starts in zip(refs, spots):
            for i, start in enumerate(starts):
                piece = contract_cols(left_ref[...], ref[i * height : (i + 1) * height, :])
                refs[-1][:, start : start + height] = piece.astype(kind)

    whole = [
        pl.BlockSpec(array.shape, lambda i: (0, 0), pipeline_mode=pl.Buffered(1))
        for array, _ in parts
    ]
    return pl.pallas_call(
        kernel,
        grid=(rows // tile,),
        in_specs=[pl.BlockSpec((tile, depth), lambda i: (i, 0))] + whole,
        out_specs=pl.BlockSpec((tile, count * height), lambda i: (i, 0)),
        out_shape=jax.ShapeDtypeStruct((rows, count * height), kind),
        cost_estimate=LIGHT,
        name="times_turned",
    )(left, *[array for array, _ in parts])


def arrays_of(*weights):
    return [array for parts in weights for array, _ in parts]


def tensor_swap(values):
    return lax.all_to_all(values, "tensor", split_axis=0, concat_axis=0, tiled=True)


def tensor_rows(values):
    return lax.all_gather(values, "tensor", axis=0, tiled=True)


def tensor_sum(values):
    return lax.psum_scatter(values, "tensor", scatter_dimension=0, tiled=True)


def stack_columns(whole, count):
    width = whole.shape[1] // count
    whole = whole.astype(BF16)
    return jnp.concatenate([whole[:, k * width : (k + 1) * width] for k in range(count)], axis=0)


def stack_query(whole, width, query_cols, pair_cols):
    rows = whole.shape[0]
    whole = whole.astype(BF16)
    pieces = []
    for k in range(width // query_cols):
        pieces.append(whole[:, k * query_cols : (k + 1) * query_cols])
        pair = whole[:, width + k * pair_cols : width + (k + 1) * pair_cols]
        pieces.append(pair.reshape(rows * pair_cols // query_cols, query_cols))
    return jnp.concatenate(pieces, axis=0)


def split_query(total, rows, pair_cols):
    total = total.astype(F32)
    return total[:rows], total[rows:].reshape(rows, pair_cols)


def copy_block(table, source, target):
    target[...] = source[...]


def reorder(values, table):
    rows, columns = values.shape
    count = table.shape[0]
    width = columns // count
    if width % 128:
        return jnp.take(values.reshape(rows, count, width), table, axis=1).reshape(rows, columns)
    return pl.pallas_call(
        copy_block,
        grid_spec=pltpu.PrefetchScalarGridSpec(
            num_scalar_prefetch=1,
            grid=(count,),
            in_specs=[pl.BlockSpec((rows, width), lambda j, table: (0, table[j]))],
            out_specs=pl.BlockSpec((rows, width), lambda j, table: (0, j)),
        ),
        out_shape=jax.ShapeDtypeStruct(values.shape, values.dtype),
        cost_estimate=LIGHT,
        name="reorder",
    )(table, values)


def place_rows(left, values, table):
    rows, count = values.shape[0], table.shape[0]
    width = values.shape[1] // (128 * count) * 128
    if width * count != values.shape[1] // 256 * 256:
        columns = values.shape[1] // (count * 64) * (count * 64)
        return matmul(left, reorder(values[:, :columns], table)).astype(BF16)

    def kernel(table_ref, left_ref, source, target):
        target[...] = matmul(left_ref[...], source[...]).astype(BF16)

    return pl.pallas_call(
        kernel,
        grid_spec=pltpu.PrefetchScalarGridSpec(
            num_scalar_prefetch=1,
            grid=(count,),
            in_specs=[
                pl.BlockSpec((rows, rows), lambda j, table: (0, 0)),
                pl.BlockSpec((rows, width), lambda j, table: (0, table[j])),
            ],
            out_specs=pl.BlockSpec((rows, width), lambda j, table: (0, j)),
        ),
        out_shape=jax.ShapeDtypeStruct((rows, width * count), BF16),
        cost_estimate=LIGHT,
        name="place_rows",
    )(table, left, values)


def add_rounded(base, part, bias):
    rows, width = base.shape
    tile = 64 if rows % 64 == 0 else rows
    wide = pl.BlockSpec((tile, width), lambda i: (i, 0))

    def kernel(base_ref, part_ref, bias_ref, out_ref):
        total = base_ref[...] + part_ref[...].astype(F32) + bias_ref[...]
        out_ref[...] = total.astype(BF16)

    return pl.pallas_call(
        kernel,
        grid=(rows // tile,),
        in_specs=[wide, wide, pl.BlockSpec((1, width), lambda i: (0, 0))],
        out_specs=wide,
        out_shape=jax.ShapeDtypeStruct((rows, width), BF16),
        cost_estimate=LIGHT,
        name="add_rounded",
    )(base, part, bias)


def stack_heads(block):
    return jnp.concatenate([block[:, :HEAD], block[:, HEAD:]], axis=0)


def attend_kernel(scale, query_ref, key_ref, value_t_ref, bias_ref, out_ref, log_ref):
    rows = query_ref.shape[0]
    queries = stack_heads(query_ref[...])
    scores = contract_cols(key_ref[...], queries) * scale + bias_ref[...]
    top = jnp.max(scores, axis=0, keepdims=True)
    exps = jnp.exp(scores - top)
    total = jnp.sum(exps, axis=0, keepdims=True)
    probs = (exps * (1.0 / total)).astype(BF16)
    mixed = matmul(value_t_ref[...], probs).T.astype(BF16)
    out_ref[:, :HEAD] = mixed[:rows]
    out_ref[:, HEAD:] = mixed[rows:]
    log_ref[0] = top + jnp.log(total)


def attend(queries, columns, key_rows, value_t, bias, scale):
    rows, keys = queries.shape[0], key_rows.shape[0]
    pairs = columns // (2 * HEAD)

    def kernel(*refs):
        attend_kernel(scale, *refs)

    return pl.pallas_call(
        kernel,
        grid=(pairs,),
        in_specs=[
            pl.BlockSpec((rows, 2 * HEAD), lambda i: (0, i)),
            pl.BlockSpec((keys, HEAD), lambda i: (0, 0)),
            pl.BlockSpec((HEAD, keys), lambda i: (0, 0)),
            pl.BlockSpec((keys, 2 * rows), lambda i: (0, 0)),
        ],
        out_specs=[
            pl.BlockSpec((rows, 2 * HEAD), lambda i: (0, i)),
            pl.BlockSpec((1, 1, 2 * rows), lambda i: (i, 0, 0)),
        ],
        out_shape=[
            jax.ShapeDtypeStruct((rows, columns), BF16),
            jax.ShapeDtypeStruct((pairs, 1, 2 * rows), F32),
        ],
        cost_estimate=LIGHT,
        name="attend",
    )(queries, key_rows, value_t, bias)


def attend_back_kernel(
    scale, query_ref, dout_ref, key_ref, value_ref, key_t_ref, bias_ref, log_ref, grad_ref, pair_ref
):
    rows = query_ref.shape[0]

    @pl.when(pl.program_id(0) == 0)
    def _():
        pair_ref[...] = jnp.zeros_like(pair_ref)

    queries = stack_heads(query_ref[...])
    douts = stack_heads(dout_ref[...])
    scores = contract_cols(key_ref[...], queries) * scale + bias_ref[...]
    probs = jnp.exp(scores - log_ref[0])
    prob_grad = contract_cols(value_ref[...], douts)
    inner = jnp.sum(probs * prob_grad, axis=0, keepdims=True)
    score_grad = (probs * (prob_grad - inner) * scale).astype(BF16)
    pair_ref[:, :HEAD] += matmul(score_grad, queries)
    pair_ref[:, HEAD:] += matmul(probs.astype(BF16), douts)
    query_grad = matmul(key_t_ref[...], score_grad).T.astype(BF16)
    grad_ref[:, :HEAD] = query_grad[:rows]
    grad_ref[:, HEAD:] = query_grad[rows:]


def attend_back(queries, columns, douts, key_rows, value_rows, key_t, bias, log_totals, scale):
    rows, keys = queries.shape[0], key_rows.shape[0]
    pairs = columns // (2 * HEAD)

    def kernel(*refs):
        attend_back_kernel(scale, *refs)

    return pl.pallas_call(
        kernel,
        grid=(pairs,),
        in_specs=[
            pl.BlockSpec((rows, 2 * HEAD), lambda i: (0, i)),
            pl.BlockSpec((rows, 2 * HEAD), lambda i: (0, i)),
            pl.BlockSpec((keys, HEAD), lambda i: (0, 0)),
            pl.BlockSpec((keys, HEAD), lambda i: (0, 0)),
            pl.BlockSpec((HEAD, keys), lambda i: (0, 0)),
            pl.BlockSpec((keys, 2 * rows), lambda i: (0, 0)),
            pl.BlockSpec((1, 1, 2 * rows), lambda i: (i, 0, 0)),
        ],
        out_specs=[
            pl.BlockSpec((rows, 2 * HEAD), lambda i: (0, i)),
            pl.BlockSpec((keys, 2 * HEAD), lambda i: (0, 0)),
        ],
        out_shape=[
            jax.ShapeDtypeStruct((rows, columns), BF16),
            jax.ShapeDtypeStruct((keys, 2 * HEAD), F32),
        ],
        cost_estimate=LIGHT,
        name="attend_back",
    )(queries, douts, key_rows, value_rows, key_t, bias, log_totals)


def local(
    tokens,
    cotangent,
    deal,
    segment,
    norm1_gain,
    norm1_shift,
    query_weight,
    query_bias,
    kv_weight,
    value_bias,
    out_weight,
    out_bias,
    norm2_gain,
    norm2_shift,
    up_weight,
    up_bias,
    down_weight,
    down_bias,
):
    local_rows, width = tokens.shape
    dp_count = lax.axis_size("dp")
    tensor_count = lax.axis_size("tensor")
    dp_rank = lax.axis_index("dp")
    tensor_rank = lax.axis_index("tensor")
    slot_rows = local_rows // dp_count
    layer_total = query_weight.shape[0]
    group_rows = local_rows * tensor_count
    query_cols = query_weight.shape[2]
    pair_cols = kv_weight.shape[2]
    score_scale = HEAD ** (-0.5)
    order = slot_order()
    to_slots = jnp.asarray(order, jnp.int32) ^ dp_rank
    place_of = [order.index(r) for r in range(dp_count)]
    from_slots = jnp.take(
        jnp.asarray(place_of, jnp.int32), jnp.arange(dp_count, dtype=jnp.int32) ^ dp_rank
    )

    target_dev = deal // local_rows // tensor_count
    target_row = deal % local_rows
    dev_ids = jnp.arange(dp_count, dtype=jnp.int32)
    dev_match = (target_dev[:, None] == dev_ids[None, :]).astype(jnp.int32)
    earlier = jnp.cumsum(dev_match, axis=0) - dev_match
    slot_of = target_dev * slot_rows + jnp.sum(earlier * dev_match, axis=1)
    row_ids = jnp.arange(local_rows, dtype=jnp.int32)
    send_table = (row_ids[:, None] == slot_of[None, :]).astype(BF16)
    place_cols = jnp.broadcast_to(target_row.astype(BF16)[:, None], (local_rows, HEAD))
    tokens_sent = matmul(send_table, jnp.concatenate([tokens, place_cols], axis=1)).astype(BF16)
    tokens_come = lax.all_to_all(tokens_sent, "dp", split_axis=0, concat_axis=0, tiled=True)
    tangent_sent = matmul(send_table, cotangent).astype(BF16)
    tangent_come = lax.all_to_all(tangent_sent, "dp", split_axis=0, concat_axis=0, tiled=True)
    arrived_place = tokens_come[:, width].astype(jnp.int32)
    place_table = (row_ids[:, None] == arrived_place[None, :]).astype(BF16)
    stream = place_rows(place_table, tokens_come, to_slots)
    last_branch = place_rows(place_table, tangent_come, to_slots)
    tangent = last_branch.astype(F32)
    stream = after(stream, last_branch)

    places = jnp.arange(group_rows, dtype=jnp.int32)
    own_places = tensor_rank * local_rows + row_ids
    own_labels = lax.dynamic_slice_in_dim(segment, tensor_rank * local_rows, local_rows)
    allowed = (places[:, None] <= own_places[None, :]) & (
        segment[:, None] == own_labels[None, :]
    )
    score_bias = jnp.where(allowed, 0.0, -1e30).astype(F32)
    score_bias = jnp.concatenate([score_bias, score_bias], axis=1)

    def product(left, weights, bias=None):
        pieces, start = [], 0
        for parts in weights:
            size = parts[0][0].shape[1]
            if bias is None:
                pieces.append(times(left, parts, round_product, (), (BF16,))[0])
            else:
                extra = (bias[:, start : start + size],)
                pieces.append(times(left, parts, bias_round, extra, (BF16,))[0])
            start += size
        return pieces[0] if len(pieces) == 1 else jnp.concatenate(pieces, axis=1)

    def product_turned(left, weights):
        total, start = None, 0
        for parts in weights:
            size = parts[0][0].shape[1]
            piece = times_turned(left[:, start : start + size], parts, F32)
            total = piece if total is None else total + piece
            start += size
        return total

    last = layer_total - 1
    split = width // 2
    cut = tensor_count // 2
    depth = query_weight.shape[1]
    pair_rows = depth * pair_cols // query_cols
    bias_rows = 16

    def query_payload(l):
        rest, terms = query_bias[l], []
        for _ in range(3):
            terms.append(rest.astype(BF16))
            rest = rest - terms[-1].astype(F32)
        terms = jnp.pad(jnp.stack(terms), ((0, bias_rows - 3), (0, 0)))
        return jnp.concatenate(
            [query_weight[l], kv_weight[l].reshape(pair_rows, query_cols), terms], axis=0
        )

    def query_parts(rows):
        size = rows.shape[0] // tensor_count
        each = [rows[k * size : (k + 1) * size] for k in range(tensor_count)]
        pair = [part[depth : depth + pair_rows].reshape(depth, pair_cols) for part in each]
        bias = [
            sum(part[depth + pair_rows + i].astype(F32) for i in range(3)) for part in each
        ]
        return (
            [part[:depth] for part in each],
            jnp.concatenate(pair, axis=1),
            jnp.concatenate(bias),
        )

    def columns(rows):
        count = rows.shape[0] // depth
        return jnp.concatenate([rows[k * depth : (k + 1) * depth] for k in range(count)], axis=1)

    out_turned = [out_weight[l].T for l in range(layer_total)]
    down_turned = [down_weight[l].T for l in range(layer_total)]
    query_rows = tensor_rows(query_payload(0))
    out_rows = tensor_rows(after(out_turned[0], tangent_come))
    if last > 0:
        rest = jnp.concatenate([query_payload(1), out_turned[1]], axis=0)
        rest = tensor_rows(after(rest, tokens_come))
        size = rest.shape[0] // tensor_count
        rest = [rest[k * size : (k + 1) * size] for k in range(tensor_count)]
    query_rows = after(query_rows, tokens_come, tangent_come, score_bias)
    cut_rows = cut * depth
    query_each, kv_full, bias_full = query_parts(query_rows)
    query_gather = Gather(
        [jnp.concatenate(query_each[:cut], axis=1)],
        [jnp.concatenate(query_each[cut:] + [kv_full], axis=1)],
    ).send()
    out_gather = Gather([columns(out_rows[:cut_rows])], [columns(out_rows[cut_rows:])]).send(
        *query_gather.come
    )
    w_query = query_gather.finish()
    early_rows = local_rows // 2
    if last > 0:
        query_rows = jnp.concatenate([part[: size - depth] for part in rest], axis=0)
        out_rows = jnp.concatenate([part[size - depth :] for part in rest], axis=0)
        branch_early = tensor_rows(last_branch[:early_rows])

    def branch_whole(early, late):
        parts = []
        for k in range(tensor_count):
            parts.append(early[k * early_rows : (k + 1) * early_rows])
            size = local_rows - early_rows
            parts.append(late[k * size : (k + 1) * size])
        return jnp.concatenate(parts, axis=0)

    vectors = jnp.concatenate(
        [norm1_gain, norm1_shift, out_bias, norm2_gain, norm2_shift, down_bias], axis=0
    )
    vectors = reorder(vectors, to_slots)
    gain_one, shift_one, bias_out, gain_two, shift_two, bias_down = [
        vectors[i * layer_total : (i + 1) * layer_total] for i in range(6)
    ]

    def rows_back(values):
        slots_out = place_rows(place_table.T, values, from_slots)
        come = lax.all_to_all(slots_out, "dp", split_axis=0, concat_axis=0, tiled=True)
        return slots_out, come

    saved = []
    for l in range(layer_total):
        if 0 < l < last:
            query_rows = tensor_rows(after(query_payload(l + 1), out_rows))
            out_rows = tensor_rows(after(out_turned[l + 1], query_rows))
        if l == 0:
            stream, normed = add_and_norm(stream, None, None, gain_one[:1], shift_one[:1])
        bias = jnp.concatenate([bias_full, jnp.zeros((HEAD,), F32), value_bias[l]])[None]
        queries = product(normed, w_query, bias)
        projected = queries
        pair_own = queries[:, width:]
        pair_all = tensor_swap(jnp.concatenate([pair_own] * tensor_count))
        pair_t = pair_all.T
        if l == 0:
            out_gather.settle(projected).send(projected)
            ff_gather = Gather([up_weight[0]], [down_turned[0]]).send(pair_all)
        mixed, log_totals = attend(
            queries, width, pair_all[:, :HEAD], pair_t[HEAD:], score_bias, score_scale
        )
        if l == 0:
            w_out = out_gather.settle(mixed).finish(mixed)
        if l > 0:
            mixed = after(mixed, *ff_gather.come)
            w_up, w_down = ff_gather.settle(mixed).finish(mixed)
        hidden_state, normed_two = add_and_norm(
            stream,
            product_turned(mixed, w_out),
            bias_out[l : l + 1],
            gain_two[l : l + 1],
            shift_two[l : l + 1],
        )
        if l == 0:
            normed_two = after(normed_two, *ff_gather.come)
            w_up, w_down = ff_gather.settle(normed_two).finish(normed_two)
        if l == 0 and last > 0:
            normed_two = after(normed_two, branch_early)
        normed_two_all = tensor_rows(normed_two)
        normed_two_all = after(normed_two_all, *arrays_of(w_up, w_down))
        if l == last:
            if last == 0:
                branch_all = tensor_rows(last_branch)
            act_grad = times(branch_all, w_down, plain_product, (), (F32,))[0]
            normed_two_all = after(normed_two_all, act_grad)
            activation, pre_grad = times(
                normed_two_all, w_up, gelu_and_back, (up_bias[l][None], act_grad), (BF16, BF16)
            )
            pre_gelu = None
        else:
            pre_gelu, activation = times(
                normed_two_all, w_up, gelu_both, (up_bias[l][None],), (F32, BF16)
            )
        saved.append(
            (
                stream,
                normed,
                queries,
                pair_all,
                pair_t,
                log_totals,
                mixed,
                hidden_state,
                normed_two_all,
                pre_gelu,
                activation,
                w_query,
                w_out,
                w_up,
                w_down,
            )
        )
        if l < last:
            query_each, kv_full, bias_full = query_parts(query_rows)
            attn_gather = Gather(
                [jnp.concatenate(query_each + [kv_full], axis=1)], [columns(out_rows)]
            )
            attn_gather.send(normed_two_all)
            down_part = times_turned(activation, w_down, BF16)
            down_part = after(down_part, *attn_gather.come)
            down_sum = tensor_sum(down_part)
            ff_gather = Gather([up_weight[l + 1]], [down_turned[l + 1]]).send(down_sum)
            w_query, w_out = [[parts] for parts in attn_gather.settle(down_part).finish(down_part)]
            if l == last - 1:
                sent = after(last_branch[early_rows:], w_query[0][0][0], w_out[0][0][0])
                branch_all = branch_whole(branch_early, tensor_rows(sent))
            down_sum = after(down_sum, *arrays_of(*w_query, *w_out))
            stream, normed = add_and_norm(
                hidden_state,
                down_sum,
                bias_down[l : l + 1],
                gain_one[l + 1 : l + 2],
                shift_one[l + 1 : l + 2],
            )

    reduced = [None] * layer_total
    ff_open = [None] * layer_total
    vector_grads = [None] * layer_total
    query_bias_grads = [None] * layer_total
    value_bias_grads = [None] * layer_total
    up_bias_grads = [None] * layer_total
    later = None
    for l in reversed(range(layer_total)):
        (
            stream_in,
            normed,
            queries,
            pair_all,
            pair_t,
            log_totals,
            mixed,
            hidden_state,
            normed_two_all,
            pre_gelu,
            activation,
            w_query,
            w_out,
            w_up,
            w_down,
        ) = saved[l]
        if l == last:
            branch_grad = last_branch
        if l < last:
            branch_all = tensor_rows(branch_grad)
            above, both_above, normed_above, attn_above, mixed_above, ff_scatter = later
            ff_scatter.settle(branch_grad).send()
            both_late, attn_late = after((both_above, attn_above), branch_grad, *ff_scatter.now())
            attn_scatter = Scatter(
                [gradient_half(normed_above, both_late, True)],
                [gradient_half(attn_late, mixed_above, True)],
            )
            attn_scatter.send()
            beside = ff_scatter.sent + attn_scatter.sent
            if above == last:
                final_sum = after(final_sum, *beside)
                layer_out = add_rounded(saved[last][7], final_sum, bias_down[last][None])
                out_slots, out_back = rows_back(layer_out)
                beside.append(out_slots)
            branch_all = after(branch_all, *beside)
            pre_grad = times(branch_all, w_down, gelu_back, (pre_gelu,), (BF16,))[0]
        normed_part = times_turned(pre_grad, w_up, BF16)
        if l < last:
            normed_part = after(normed_part, *ff_scatter.come, *attn_scatter.come)
        normed_two_grad = tensor_sum(normed_part)
        beside = []
        if l < last:
            attn_scatter.settle(normed_part).send()
            beside += attn_scatter.sent
            ff_open[above] = ff_scatter
        pre_late, branch_late = after((pre_grad, branch_all), normed_part)
        ff_scatter = Scatter(
            [gradient_half(normed_two_all, pre_late, True)],
            [gradient_half(branch_late, activation, True)],
        )
        ff_scatter.send()
        beside += ff_scatter.now() + ff_scatter.sent
        if l == last:
            down_bias_part = column_sum(after(branch_grad, normed_part))
        up_bias_grads[l] = column_sum(pre_late)
        beside += [down_bias_part, up_bias_grads[l]]
        if l == last:
            final_part = times_turned(after(activation, *ff_scatter.sent), w_down, BF16)
            beside.append(final_part)
        else:
            both_whole, out_whole = attn_scatter.finish(*ff_scatter.now())
            out_stack = stack_columns(out_whole, tensor_count)
            query_stack = stack_query(both_whole, width, query_cols, pair_cols)
            beside += [out_stack, query_stack]
        normed_two_grad = after(normed_two_grad, *beside)
        if l == last:
            final_sum = tensor_sum(after(final_part, normed_two_grad))
        else:
            out_grad = tensor_sum(after(out_stack, normed_two_grad)).astype(F32).T
            query_sum = tensor_sum(after(query_stack, normed_two_grad))
            query_w_grad, kv_grad = split_query(query_sum, depth, pair_cols)
        hidden_grad, attn_grad, two_sums = norm_back(
            hidden_state, normed_two_grad, gain_two[l : l + 1], tangent
        )
        mixed_grad = product(attn_grad, w_out)
        if l == 0:
            attn_late = after(attn_grad, mixed_grad)
            out_scatter = Scatter(
                [gradient_half(attn_late, mixed[:, :split])],
                [gradient_half(attn_late, mixed[:, split:])],
            ).send()
            mixed_grad = after(mixed_grad, *out_scatter.sent)
        query_grad, pair_part = attend_back(
            queries,
            width,
            mixed_grad,
            pair_all[:, :HEAD],
            pair_all[:, HEAD:],
            pair_t[:HEAD],
            score_bias,
            log_totals,
            score_scale,
        )
        pair_come = tensor_swap(pair_part.astype(BF16))
        pair_grad = sum(
            pair_come[k * local_rows : (k + 1) * local_rows].astype(F32)
            for k in range(tensor_count)
        ).astype(BF16)
        query_bias_grads[l] = jnp.sum(query_grad.astype(F32), axis=0)
        value_bias_grads[l] = jnp.sum(pair_grad[:, HEAD:].astype(F32), axis=0)
        both_grad = jnp.concatenate([query_grad, pair_grad], axis=1)
        if l == last > 0:
            both_grad = after(both_grad, *ff_scatter.come)
        if l == 0:
            both_grad = after(both_grad, *ff_scatter.come)
            both_scatter = Scatter(
                [gradient_half(normed, both_grad[:, :split])],
                [gradient_half(normed, both_grad[:, split:])],
            ).send()
            ff_scatter.settle(*both_scatter.sent).send()
            out_scatter.settle(*ff_scatter.sent).send()
            both_grad = after(both_grad, *both_scatter.sent, *out_scatter.sent, *ff_scatter.sent)
            ff_open[0] = ff_scatter
        normed_grad = product_turned(both_grad, w_query)
        if l == last > 0:
            normed_grad, final_sum = lax.optimization_barrier((normed_grad, final_sum))
        tangent, branch_grad, one_sums = norm_back(
            stream_in, normed_grad, gain_one[l : l + 1], hidden_grad
        )
        if l < last:
            reduced[above] = (query_w_grad, kv_grad, out_grad)
        later = (l, both_grad, normed, attn_grad, mixed, ff_scatter)
        vector_grads[l] = [
            one_sums[0],
            one_sums[1],
            two_sums[2],
            two_sums[0],
            two_sums[1],
            down_bias_part,
        ]
        down_bias_part = one_sums[2]

    stacked = jnp.stack([vector_grads[l][m] for m in range(6) for l in range(layer_total)])
    stacked = reorder(after(stacked, *ff_open[0].come), from_slots)
    query_rows = jnp.stack(query_bias_grads)
    value_rows = jnp.pad(jnp.stack(value_bias_grads), ((0, 0), (0, width - HEAD)))
    smalls = jnp.concatenate([stacked, query_rows, value_rows], axis=0)
    small_count = smalls.shape[0]
    smalls = jnp.concatenate([smalls, jnp.stack(up_bias_grads)], axis=0)
    smalls = smalls + flip(smalls, 1)
    total = smalls[:small_count]
    if tensor_count & (tensor_count - 1) == 0:
        for k in range(tensor_count.bit_length() - 1):
            total = total + lax.ppermute(
                total, "tensor", [(i, i ^ (1 << k)) for i in range(tensor_count)]
            )
    else:
        total = lax.psum(total, "tensor")
    total = jnp.concatenate([total, smalls[small_count:]], axis=0)
    for bit in plane_bits():
        total = total + flip(total, bit)
    up_bias_grad = total[small_count:]
    vector_sums = [total[m * layer_total : (m + 1) * layer_total] for m in range(8)]
    query_bias_grad = lax.dynamic_slice_in_dim(
        vector_sums[6], tensor_rank * query_cols, query_cols, 1
    )
    value_bias_grad = vector_sums[7][:, :HEAD]

    grad_back = rows_back(branch_grad)[1]
    out_back = after(out_back, tangent)
    both_scatter.settle(normed_grad).send()
    out_whole = jnp.concatenate(out_scatter.finish(), axis=1)
    out_grad = tensor_sum(stack_columns(out_whole, tensor_count)).astype(F32).T
    both_whole = jnp.concatenate(both_scatter.finish(), axis=1)
    query_stack = stack_query(both_whole, width, query_cols, pair_cols)
    query_w_grad, kv_grad = split_query(tensor_sum(query_stack), depth, pair_cols)
    reduced[0] = (query_w_grad, kv_grad, out_grad)
    up_stack, down_stack = [
        stack_sums([ff.open_sum(m) for ff in ff_open], m == 1) for m in range(2)
    ]
    if last == 0:
        layer_out = add_rounded(saved[last][7], final_sum, bias_down[last][None])
        out_back = rows_back(layer_out)[1]
    layer_rows = contract_rows(send_table, out_back).astype(BF16)
    token_rows = contract_rows(send_table, grad_back).astype(BF16)
    summed = [jnp.stack([reduced[l][m] for l in range(layer_total)]) for m in range(3)]
    return (
        layer_rows,
        token_rows,
        vector_sums[0],
        vector_sums[1],
        summed[0],
        query_bias_grad,
        summed[1],
        value_bias_grad,
        summed[2],
        vector_sums[2],
        vector_sums[3],
        vector_sums[4],
        up_stack,
        up_bias_grad,
        down_stack,
        vector_sums[5],
    )


def solution(mesh):
    rows = P(("dp", "tensor"), None)
    in_specs = (
        rows,
        rows,
        P(("dp", "tensor")),
        P("dp"),
        P(),
        P(),
        P(None, "dp", "tensor"),
        P(None, "tensor"),
        P(None, "dp", "tensor"),
        P(),
        P(None, "tensor", "dp"),
        P(),
        P(),
        P(),
        P(None, "dp", "tensor"),
        P(None, "tensor"),
        P(None, "tensor", "dp"),
        P(),
    )
    out_specs = (
        rows,
        rows,
        P(),
        P(),
        P(None, "dp", "tensor"),
        P(None, "tensor"),
        P(None, "dp", "tensor"),
        P(),
        P(None, "tensor", "dp"),
        P(),
        P(),
        P(),
        P(None, "dp", "tensor"),
        P(None, "tensor"),
        P(None, "tensor", "dp"),
        P(),
    )
    return jax.shard_map(local, mesh=mesh, in_specs=in_specs, out_specs=out_specs, check_vma=False)
```

```python
import jax
import jax.numpy as jnp
from jax import lax
from jax.experimental import pallas as pl
from jax.experimental.pallas import tpu as pltpu
from jax.sharding import PartitionSpec as P

HEAD = 128
EPSILON = 1e-05
BF16 = jnp.bfloat16
F32 = jnp.float32
LIGHT = pl.CostEstimate(flops=1, transcendentals=0, bytes_accessed=1)


def gelu_tanh(values):
    return jax.nn.gelu(values, approximate=True)


def matmul(left, right):
    return jnp.dot(left, right, preferred_element_type=F32)


def contract_rows(left, right):
    return lax.dot_general(left, right, (((0,), (0,)), ((), ())), preferred_element_type=F32)


def contract_cols(left, right):
    return lax.dot_general(left, right, (((1,), (1,)), ((), ())), preferred_element_type=F32)


def after(values, *others):
    return lax.optimization_barrier((values, others))[0]


def flip(values, bit):
    count = lax.axis_size("dp")
    return lax.ppermute(values, "dp", [(i, i ^ bit) for i in range(count)])


def turn(values, step):
    count = lax.axis_size("tensor")
    return lax.ppermute(values, "tensor", [((i + step) % count, i) for i in range(count)])


def plane_bits():
    count = lax.axis_size("dp")
    return [1 << k for k in range(1, count.bit_length() - 1)]


def slot_order():
    count = lax.axis_size("dp")
    evens = list(range(0, count, 2))
    return evens + [r ^ 1 for r in evens]


def join_rows(arrays):
    return arrays[0] if len(arrays) == 1 else jnp.concatenate(arrays, axis=0)


def blocks_of(parts, wanted):
    runs = []
    where = {}
    for array, blocks in parts:
        rows = array.shape[0] // len(blocks)
        for i, block in enumerate(blocks):
            where[block] = (array, i * rows, rows)
    for block in wanted:
        array, start, rows = where[block]
        if runs and runs[-1][0] is array and runs[-1][2] == start:
            runs[-1][2] += rows
        else:
            runs.append([array, start, start + rows])
    return join_rows([lax.slice_in_dim(array, low, high) for array, low, high in runs])


class Gather:
    def __init__(self, first, second):
        bits = plane_bits()
        self.members = [
            [order, [(array, [0])]]
            for group, order in ((first, bits), (second, bits[::-1]))
            for array in group
        ]
        self.taken = 0
        self.come = []

    def send(self, *gate):
        gate = gate + tuple(self.come)
        self.come = []
        for member in self.members:
            order, parts = member
            bit = order[self.taken]
            blocks = [block for _, part in parts for block in part]
            whole = join_rows([array for array, _ in parts])
            come = flip(after(whole, *gate) if gate else whole, bit)
            self.come.append(come)
            member[1] = [(whole, blocks), (come, [block | bit for block in blocks])]
        self.taken += 1
        return self

    def settle(self, *late):
        for member in self.members:
            own, (come, blocks) = member[1]
            member[1] = [own, (after(come, *late), blocks)]
        return self

    def finish(self, *gate):
        while self.taken < len(plane_bits()):
            self.send(*gate)
        return [
            parts + [(flip(array, 1), [block | 1 for block in blocks]) for array, blocks in parts]
            for _, parts in self.members
        ]


def add_blocks(half, count, keep, come, kind):
    rows, columns = half.shape[0] // count, half.shape[1]
    stride = keep[1] - keep[0] if len(keep) > 1 else 1

    def kernel(half_ref, come_ref, out_ref):
        out_ref[...] = (half_ref[...].astype(F32) + come_ref[...].astype(F32)).astype(kind)

    block = (rows, columns)
    return pl.pallas_call(
        kernel,
        grid=(len(keep),),
        in_specs=[
            pl.BlockSpec(block, lambda i: (keep[0] + i * stride, 0)),
            pl.BlockSpec(block, lambda i: (i, 0)),
        ],
        out_specs=pl.BlockSpec(block, lambda i: (i, 0)),
        out_shape=jax.ShapeDtypeStruct(come.shape, kind),
        cost_estimate=LIGHT,
        name="add_blocks",
    )(half, come)


def take_blocks(half, count, keep):
    rows, columns = half.shape[0] // count, half.shape[1]
    stride = keep[1] - keep[0] if len(keep) > 1 else 1
    block = (rows, columns)
    return pl.pallas_call(
        lambda half_ref, out_ref: out_ref.__setitem__(..., half_ref[...]),
        grid=(len(keep),),
        in_specs=[pl.BlockSpec(block, lambda i: (keep[0] + i * stride, 0))],
        out_specs=pl.BlockSpec(block, lambda i: (i, 0)),
        out_shape=jax.ShapeDtypeStruct((len(keep) * rows, columns), half.dtype),
        cost_estimate=LIGHT,
        name="take_blocks",
    )(half)


def column_sum(values):
    rows, columns = values.shape
    tile = 256 if rows % 256 == 0 else rows

    def kernel(values_ref, out_ref):
        @pl.when(pl.program_id(0) == 0)
        def _():
            out_ref[...] = jnp.zeros_like(out_ref)

        out_ref[...] += jnp.sum(values_ref[...].astype(F32), axis=0, keepdims=True)

    return pl.pallas_call(
        kernel,
        grid=(rows // tile,),
        in_specs=[pl.BlockSpec((tile, columns), lambda i: (i, 0))],
        out_specs=pl.BlockSpec((1, columns), lambda i: (0, 0)),
        out_shape=jax.ShapeDtypeStruct((1, columns), F32),
        cost_estimate=LIGHT,
        name="column_sum",
    )(values)[0]


class Scatter:
    def __init__(self, first, second):
        bits = plane_bits()
        evens = list(range(0, lax.axis_size("dp"), 2))
        self.members = [
            [order, half, evens]
            for group, order in ((first, bits), (second, bits[::-1]))
            for half in group
        ]
        self.taken = 0
        self.come = None

    def send(self, *gate):
        self.come = []
        self.sent = []
        for order, half, blocks in self.members:
            spots = [i for i, block in enumerate(blocks) if block & order[self.taken]]
            piece = take_blocks(half, len(blocks), spots)
            piece = after(piece, *gate) if gate else piece
            self.sent.append(piece)
            self.come.append(flip(piece, order[self.taken]))
        self.taken += 1
        return self

    def settle(self, *late):
        last = self.taken == len(plane_bits())
        late = late + tuple(self.come)
        for member, come in zip(self.members, self.come):
            order, half, blocks = member
            keep = [block for block in blocks if not block & order[self.taken - 1]]
            if late:
                come = after(come, *late)
            spots = [blocks.index(block) for block in keep]
            member[1:] = [
                add_blocks(half, len(blocks), spots, come, F32 if last else BF16),
                keep,
            ]
        self.come = None
        return self

    def now(self):
        return [half for _, half, _ in self.members]

    def open_sum(self, member):
        while self.taken < len(plane_bits()):
            self.settle()
            self.send()
        order, half, blocks = self.members[member]
        spot = next(i for i, block in enumerate(blocks) if not block & order[-1])
        return half, len(blocks), spot, self.come[member]

    def finish(self, *late):
        if self.come:
            self.settle(*late)
        while self.taken < len(plane_bits()):
            self.send()
            self.settle(*late)
        return [half.astype(F32) for _, half, _ in self.members]


def stack_sums(items, turned):
    rows, columns = items[0][3].shape
    shape = (1, columns, rows) if turned else (1, rows, columns)

    def kernel(*refs):
        for l in range(len(items)):

            @pl.when(pl.program_id(0) == l)
            def _():
                total = refs[2 * l][...].astype(F32) + refs[2 * l + 1][...].astype(F32)
                refs[-1][0] = total.T if turned else total

    specs, arrays = [], []
    for half, _, spot, come in items:
        specs.append(pl.BlockSpec((rows, columns), lambda l, spot=spot: (spot, 0)))
        specs.append(pl.BlockSpec((rows, columns), lambda l: (0, 0)))
        arrays += [half, come]
    return pl.pallas_call(
        kernel,
        grid=(len(items),),
        in_specs=specs,
        out_specs=pl.BlockSpec(shape, lambda l: (l, 0, 0)),
        out_shape=jax.ShapeDtypeStruct((len(items),) + shape[1:], F32),
        cost_estimate=LIGHT,
        name="stack_sums",
    )(*arrays)


def turned_product(features, values, side, extra=None):
    rows, depth = features.shape
    columns = values.shape[1]
    tile = 256
    steps = depth // 2 // tile

    def kernel(left_ref, right_ref, *refs):
        total = matmul(left_ref[...].T, right_ref[...])
        if extra is not None:
            total = total + refs[0][...].astype(F32)
        refs[-1][...] = total.astype(BF16)

    tiles = pl.BlockSpec((tile, columns), lambda i: (i, 0))
    return pl.pallas_call(
        kernel,
        grid=(steps,),
        in_specs=[
            pl.BlockSpec((rows, tile), lambda i: (0, i + side * steps)),
            pl.BlockSpec((rows, columns), lambda i: (0, 0)),
        ]
        + ([tiles] if extra is not None else []),
        out_specs=tiles,
        out_shape=jax.ShapeDtypeStruct((depth // 2, columns), BF16),
        cost_estimate=LIGHT,
        name="turned_product",
    )(features, values, *([extra] if extra is not None else []))


def gradient_half(features, values, kernel=False):
    if kernel:
        return turned_product(features, values, 0, flip(turned_product(features, values, 1), 1))
    half = features.shape[1] // 2
    far = contract_rows(features[:, half:], values).astype(BF16)
    near = contract_rows(features[:, :half], values) + flip(far, 1).astype(F32)
    return near.astype(BF16)


def norm_parts(values):
    centred = values - jnp.mean(values, axis=-1, keepdims=True)
    return centred, lax.rsqrt(jnp.mean(centred * centred, axis=-1, keepdims=True) + EPSILON)


def row_tile(rows):
    return 64 if rows % 64 == 0 else rows


def add_and_norm(base, part, bias, gain, shift):
    rows, width = base.shape
    tile = row_tile(rows)
    wide = pl.BlockSpec((tile, width), lambda i: (i, 0))
    line = pl.BlockSpec((1, width), lambda i: (0, 0))
    added = [] if part is None else [part, bias]

    def kernel(gain_ref, shift_ref, base_ref, *refs):
        total = base_ref[...].astype(F32)
        if part is not None:
            total = total + refs[0][...].astype(F32) + refs[1][...]
        centred, slope = norm_parts(total)
        refs[-2][...] = total
        refs[-1][...] = (centred * slope * gain_ref[...] + shift_ref[...]).astype(BF16)

    return pl.pallas_call(
        kernel,
        grid=(rows // tile,),
        in_specs=[line, line, wide] + [wide, line][: len(added)],
        out_specs=[wide, wide],
        out_shape=[
            jax.ShapeDtypeStruct((rows, width), F32),
            jax.ShapeDtypeStruct((rows, width), BF16),
        ],
        cost_estimate=LIGHT,
        name="add_and_norm",
    )(gain, shift, base, *added)


def norm_back(values, grad, gain, tangent):
    rows, width = values.shape
    tile = row_tile(rows)
    wide = pl.BlockSpec((tile, width), lambda i: (i, 0))

    def kernel(gain_ref, values_ref, grad_ref, tangent_ref, out_ref, low_ref, sums_ref):
        centred, slope = norm_parts(values_ref[...])
        scaled = centred * slope
        grads = grad_ref[...].astype(F32)
        inner = grads * gain_ref[...]
        mean_inner = jnp.mean(inner, axis=-1, keepdims=True)
        mean_scaled = jnp.mean(inner * scaled, axis=-1, keepdims=True)
        total = tangent_ref[...] + slope * (inner - mean_inner - scaled * mean_scaled)
        low = total.astype(BF16)
        out_ref[...] = total
        low_ref[...] = low

        @pl.when(pl.program_id(0) == 0)
        def _():
            sums_ref[...] = jnp.zeros_like(sums_ref)

        for i, term in enumerate((grads * scaled, grads, low.astype(F32))):
            sums_ref[i : i + 1, :] += jnp.sum(term, axis=0, keepdims=True)

    return pl.pallas_call(
        kernel,
        grid=(rows // tile,),
        in_specs=[pl.BlockSpec((1, width), lambda i: (0, 0)), wide, wide, wide],
        out_specs=[wide, wide, pl.BlockSpec((8, width), lambda i: (0, 0))],
        out_shape=[
            jax.ShapeDtypeStruct((rows, width), F32),
            jax.ShapeDtypeStruct((rows, width), BF16),
            jax.ShapeDtypeStruct((8, width), F32),
        ],
        cost_estimate=LIGHT,
        name="norm_back",
    )(gain, values, grad, tangent)


def plain_product(total):
    return (total,)


def round_product(total):
    return (total.astype(BF16),)


def bias_round(total, bias):
    return ((total + bias).astype(BF16),)


def gelu_both(total, bias):
    value = total + bias
    return value, gelu_tanh(value).astype(BF16)


def gelu_slope(values):
    factor = 0.7978845608028654
    square = values * values
    wave = jnp.tanh(factor * (values + 0.044715 * (square * values)))
    return 0.5 * (1.0 + wave) + (0.5 * factor) * values * (1.0 - wave * wave) * (
        1.0 + (3.0 * 0.044715) * square
    )


def gelu_and_back(total, bias, act_grad):
    value = total + bias
    return gelu_tanh(value).astype(BF16), (act_grad * gelu_slope(value)).astype(BF16)


def gelu_back(total, value):
    return ((total * gelu_slope(value)).astype(BF16),)


def times(left, parts, finish, extras, types):
    rows, depth = left.shape
    columns = parts[0][0].shape[1]
    height = depth // lax.axis_size("dp")
    place = {block: i for i, block in enumerate(slot_order())}
    if height % 128:
        return finish(matmul(left, blocks_of(parts, slot_order())), *extras)
    tile = next(size for size in (768, 640, 512, 384, 256, 128, columns) if columns % size == 0)
    spots = [[place[block] * height for block in blocks] for _, blocks in parts]

    def kernel(left_ref, *refs):
        part_refs = refs[: len(parts)]
        extra_refs = refs[len(parts) : len(parts) + len(extras)]
        total = None
        for ref, starts in zip(part_refs, spots):
            for i, start in enumerate(starts):
                piece = matmul(
                    left_ref[:, start : start + height], ref[i * height : (i + 1) * height, :]
                )
                total = piece if total is None else total + piece
        values = finish(total, *[ref[...] for ref in extra_refs])
        for ref, value in zip(refs[len(parts) + len(extras) :], values):
            ref[...] = value

    return pl.pallas_call(
        kernel,
        grid=(columns // tile,),
        in_specs=[pl.BlockSpec((rows, depth), lambda j: (0, 0))]
        + [pl.BlockSpec((array.shape[0], tile), lambda j: (0, j)) for array, _ in parts]
        + [pl.BlockSpec((extra.shape[0], tile), lambda j: (0, j)) for extra in extras],
        out_specs=[pl.BlockSpec((rows, tile), lambda j: (0, j)) for _ in types],
        out_shape=[jax.ShapeDtypeStruct((rows, columns), kind) for kind in types],
        cost_estimate=LIGHT,
        name="times",
    )(left, *[array for array, _ in parts], *extras)


def times_turned(left, parts, kind):
    rows, depth = left.shape
    count = lax.axis_size("dp")
    height = sum(array.shape[0] for array, _ in parts) // count
    place = {block: i for i, block in enumerate(slot_order())}
    if height % 128:
        return contract_cols(left, blocks_of(parts, slot_order())).astype(kind)
    tile = 256 if rows % 256 == 0 else rows
    spots = [[place[block] * height for block in blocks] for _, blocks in parts]

    def kernel(left_ref, *refs):
        for ref, starts in zip(refs, spots):
            for i, start in enumerate(starts):
                piece = contract_cols(left_ref[...], ref[i * height : (i + 1) * height, :])
                refs[-1][:, start : start + height] = piece.astype(kind)

    whole = [
        pl.BlockSpec(array.shape, lambda i: (0, 0), pipeline_mode=pl.Buffered(1))
        for array, _ in parts
    ]
    return pl.pallas_call(
        kernel,
        grid=(rows // tile,),
        in_specs=[pl.BlockSpec((tile, depth), lambda i: (i, 0))] + whole,
        out_specs=pl.BlockSpec((tile, count * height), lambda i: (i, 0)),
        out_shape=jax.ShapeDtypeStruct((rows, count * height), kind),
        cost_estimate=LIGHT,
        name="times_turned",
    )(left, *[array for array, _ in parts])


def arrays_of(*weights):
    return [array for parts in weights for array, _ in parts]


def tensor_swap(values):
    return lax.all_to_all(values, "tensor", split_axis=0, concat_axis=0, tiled=True)


def tensor_rows(values):
    return lax.all_gather(values, "tensor", axis=0, tiled=True)


def tensor_sum(values):
    return lax.psum_scatter(values, "tensor", scatter_dimension=0, tiled=True)


def stack_columns(whole, count):
    width = whole.shape[1] // count
    whole = whole.astype(BF16)
    return jnp.concatenate([whole[:, k * width : (k + 1) * width] for k in range(count)], axis=0)


def stack_query(whole, width, query_cols, pair_cols):
    rows = whole.shape[0]
    whole = whole.astype(BF16)
    pieces = []
    for k in range(width // query_cols):
        pieces.append(whole[:, k * query_cols : (k + 1) * query_cols])
        pair = whole[:, width + k * pair_cols : width + (k + 1) * pair_cols]
        pieces.append(pair.reshape(rows * pair_cols // query_cols, query_cols))
    return jnp.concatenate(pieces, axis=0)


def split_query(total, rows, pair_cols):
    total = total.astype(F32)
    return total[:rows], total[rows:].reshape(rows, pair_cols)


def copy_block(table, source, target):
    target[...] = source[...]


def reorder(values, table):
    rows, columns = values.shape
    count = table.shape[0]
    width = columns // count
    if width % 128:
        return jnp.take(values.reshape(rows, count, width), table, axis=1).reshape(rows, columns)
    return pl.pallas_call(
        copy_block,
        grid_spec=pltpu.PrefetchScalarGridSpec(
            num_scalar_prefetch=1,
            grid=(count,),
            in_specs=[pl.BlockSpec((rows, width), lambda j, table: (0, table[j]))],
            out_specs=pl.BlockSpec((rows, width), lambda j, table: (0, j)),
        ),
        out_shape=jax.ShapeDtypeStruct(values.shape, values.dtype),
        cost_estimate=LIGHT,
        name="reorder",
    )(table, values)


def place_rows(left, values, table):
    rows, count = values.shape[0], table.shape[0]
    width = values.shape[1] // (128 * count) * 128
    if width * count != values.shape[1] // 256 * 256:
        columns = values.shape[1] // (count * 64) * (count * 64)
        return matmul(left, reorder(values[:, :columns], table)).astype(BF16)

    def kernel(table_ref, left_ref, source, target):
        target[...] = matmul(left_ref[...], source[...]).astype(BF16)

    return pl.pallas_call(
        kernel,
        grid_spec=pltpu.PrefetchScalarGridSpec(
            num_scalar_prefetch=1,
            grid=(count,),
            in_specs=[
                pl.BlockSpec((rows, rows), lambda j, table: (0, 0)),
                pl.BlockSpec((rows, width), lambda j, table: (0, table[j])),
            ],
            out_specs=pl.BlockSpec((rows, width), lambda j, table: (0, j)),
        ),
        out_shape=jax.ShapeDtypeStruct((rows, width * count), BF16),
        cost_estimate=LIGHT,
        name="place_rows",
    )(table, left, values)


def add_rounded(base, part, bias):
    rows, width = base.shape
    tile = 64 if rows % 64 == 0 else rows
    wide = pl.BlockSpec((tile, width), lambda i: (i, 0))

    def kernel(base_ref, part_ref, bias_ref, out_ref):
        total = base_ref[...] + part_ref[...].astype(F32) + bias_ref[...]
        out_ref[...] = total.astype(BF16)

    return pl.pallas_call(
        kernel,
        grid=(rows // tile,),
        in_specs=[wide, wide, pl.BlockSpec((1, width), lambda i: (0, 0))],
        out_specs=wide,
        out_shape=jax.ShapeDtypeStruct((rows, width), BF16),
        cost_estimate=LIGHT,
        name="add_rounded",
    )(base, part, bias)


def stack_heads(block):
    return jnp.concatenate([block[:, :HEAD], block[:, HEAD:]], axis=0)


def attend_kernel(scale, query_ref, key_ref, value_t_ref, bias_ref, out_ref, log_ref):
    rows = query_ref.shape[0]
    queries = stack_heads(query_ref[...])
    scores = contract_cols(key_ref[...], queries) * scale + bias_ref[...]
    top = jnp.max(scores, axis=0, keepdims=True)
    exps = jnp.exp(scores - top)
    total = jnp.sum(exps, axis=0, keepdims=True)
    probs = (exps * (1.0 / total)).astype(BF16)
    mixed = matmul(value_t_ref[...], probs).T.astype(BF16)
    out_ref[:, :HEAD] = mixed[:rows]
    out_ref[:, HEAD:] = mixed[rows:]
    log_ref[0] = top + jnp.log(total)


def attend(queries, columns, key_rows, value_t, bias, scale):
    rows, keys = queries.shape[0], key_rows.shape[0]
    pairs = columns // (2 * HEAD)

    def kernel(*refs):
        attend_kernel(scale, *refs)

    return pl.pallas_call(
        kernel,
        grid=(pairs,),
        in_specs=[
            pl.BlockSpec((rows, 2 * HEAD), lambda i: (0, i)),
            pl.BlockSpec((keys, HEAD), lambda i: (0, 0)),
            pl.BlockSpec((HEAD, keys), lambda i: (0, 0)),
            pl.BlockSpec((keys, 2 * rows), lambda i: (0, 0)),
        ],
        out_specs=[
            pl.BlockSpec((rows, 2 * HEAD), lambda i: (0, i)),
            pl.BlockSpec((1, 1, 2 * rows), lambda i: (i, 0, 0)),
        ],
        out_shape=[
            jax.ShapeDtypeStruct((rows, columns), BF16),
            jax.ShapeDtypeStruct((pairs, 1, 2 * rows), F32),
        ],
        cost_estimate=LIGHT,
        name="attend",
    )(queries, key_rows, value_t, bias)


def attend_back_kernel(
    scale, query_ref, dout_ref, key_ref, value_ref, key_t_ref, bias_ref, log_ref, grad_ref, pair_ref
):
    rows = query_ref.shape[0]

    @pl.when(pl.program_id(0) == 0)
    def _():
        pair_ref[...] = jnp.zeros_like(pair_ref)

    queries = stack_heads(query_ref[...])
    douts = stack_heads(dout_ref[...])
    scores = contract_cols(key_ref[...], queries) * scale + bias_ref[...]
    probs = jnp.exp(scores - log_ref[0])
    prob_grad = contract_cols(value_ref[...], douts)
    inner = jnp.sum(probs * prob_grad, axis=0, keepdims=True)
    score_grad = (probs * (prob_grad - inner) * scale).astype(BF16)
    pair_ref[:, :HEAD] += matmul(score_grad, queries)
    pair_ref[:, HEAD:] += matmul(probs.astype(BF16), douts)
    query_grad = matmul(key_t_ref[...], score_grad).T.astype(BF16)
    grad_ref[:, :HEAD] = query_grad[:rows]
    grad_ref[:, HEAD:] = query_grad[rows:]


def attend_back(queries, columns, douts, key_rows, value_rows, key_t, bias, log_totals, scale):
    rows, keys = queries.shape[0], key_rows.shape[0]
    pairs = columns // (2 * HEAD)

    def kernel(*refs):
        attend_back_kernel(scale, *refs)

    return pl.pallas_call(
        kernel,
        grid=(pairs,),
        in_specs=[
            pl.BlockSpec((rows, 2 * HEAD), lambda i: (0, i)),
            pl.BlockSpec((rows, 2 * HEAD), lambda i: (0, i)),
            pl.BlockSpec((keys, HEAD), lambda i: (0, 0)),
            pl.BlockSpec((keys, HEAD), lambda i: (0, 0)),
            pl.BlockSpec((HEAD, keys), lambda i: (0, 0)),
            pl.BlockSpec((keys, 2 * rows), lambda i: (0, 0)),
            pl.BlockSpec((1, 1, 2 * rows), lambda i: (i, 0, 0)),
        ],
        out_specs=[
            pl.BlockSpec((rows, 2 * HEAD), lambda i: (0, i)),
            pl.BlockSpec((keys, 2 * HEAD), lambda i: (0, 0)),
        ],
        out_shape=[
            jax.ShapeDtypeStruct((rows, columns), BF16),
            jax.ShapeDtypeStruct((keys, 2 * HEAD), F32),
        ],
        cost_estimate=LIGHT,
        name="attend_back",
    )(queries, douts, key_rows, value_rows, key_t, bias, log_totals)


def local(
    tokens,
    cotangent,
    deal,
    segment,
    norm1_gain,
    norm1_shift,
    query_weight,
    query_bias,
    kv_weight,
    value_bias,
    out_weight,
    out_bias,
    norm2_gain,
    norm2_shift,
    up_weight,
    up_bias,
    down_weight,
    down_bias,
):
    local_rows, width = tokens.shape
    dp_count = lax.axis_size("dp")
    tensor_count = lax.axis_size("tensor")
    dp_rank = lax.axis_index("dp")
    tensor_rank = lax.axis_index("tensor")
    slot_rows = local_rows // dp_count
    layer_total = query_weight.shape[0]
    group_rows = local_rows * tensor_count
    query_cols = query_weight.shape[2]
    pair_cols = kv_weight.shape[2]
    score_scale = HEAD ** (-0.5)
    order = slot_order()
    to_slots = jnp.asarray(order, jnp.int32) ^ dp_rank
    place_of = [order.index(r) for r in range(dp_count)]
    from_slots = jnp.take(
        jnp.asarray(place_of, jnp.int32), jnp.arange(dp_count, dtype=jnp.int32) ^ dp_rank
    )

    target_dev = deal // local_rows // tensor_count
    target_row = deal % local_rows
    dev_ids = jnp.arange(dp_count, dtype=jnp.int32)
    dev_match = (target_dev[:, None] == dev_ids[None, :]).astype(jnp.int32)
    earlier = jnp.cumsum(dev_match, axis=0) - dev_match
    slot_of = target_dev * slot_rows + jnp.sum(earlier * dev_match, axis=1)
    row_ids = jnp.arange(local_rows, dtype=jnp.int32)
    send_table = (row_ids[:, None] == slot_of[None, :]).astype(BF16)
    place_cols = jnp.broadcast_to(target_row.astype(BF16)[:, None], (local_rows, HEAD))
    tokens_sent = matmul(send_table, jnp.concatenate([tokens, place_cols], axis=1)).astype(BF16)
    tokens_come = lax.all_to_all(tokens_sent, "dp", split_axis=0, concat_axis=0, tiled=True)
    tangent_sent = matmul(send_table, cotangent).astype(BF16)
    tangent_come = lax.all_to_all(tangent_sent, "dp", split_axis=0, concat_axis=0, tiled=True)
    arrived_place = tokens_come[:, width].astype(jnp.int32)
    place_table = (row_ids[:, None] == arrived_place[None, :]).astype(BF16)

    places = jnp.arange(group_rows, dtype=jnp.int32)
    own_places = tensor_rank * local_rows + row_ids
    own_labels = lax.dynamic_slice_in_dim(segment, tensor_rank * local_rows, local_rows)
    allowed = (places[:, None] <= own_places[None, :]) & (
        segment[:, None] == own_labels[None, :]
    )
    score_bias = jnp.where(allowed, 0.0, -1e30).astype(F32)
    score_bias = jnp.concatenate([score_bias, score_bias], axis=1)

    def product(left, weights, bias=None):
        pieces, start = [], 0
        for parts in weights:
            size = parts[0][0].shape[1]
            if bias is None:
                pieces.append(times(left, parts, round_product, (), (BF16,))[0])
            else:
                extra = (bias[:, start : start + size],)
                pieces.append(times(left, parts, bias_round, extra, (BF16,))[0])
            start += size
        return pieces[0] if len(pieces) == 1 else jnp.concatenate(pieces, axis=1)

    def product_turned(left, weights):
        total, start = None, 0
        for parts in weights:
            size = parts[0][0].shape[1]
            piece = times_turned(left[:, start : start + size], parts, F32)
            total = piece if total is None else total + piece
            start += size
        return total

    last = layer_total - 1
    split = width // 2
    cut = tensor_count // 2
    depth = query_weight.shape[1]
    pair_rows = depth * pair_cols // query_cols
    bias_rows = 16

    def query_payload(l):
        rest, terms = query_bias[l], []
        for _ in range(3):
            terms.append(rest.astype(BF16))
            rest = rest - terms[-1].astype(F32)
        terms = jnp.pad(jnp.stack(terms), ((0, bias_rows - 3), (0, 0)))
        return jnp.concatenate(
            [query_weight[l], kv_weight[l].reshape(pair_rows, query_cols), terms], axis=0
        )

    def query_parts(rows):
        size = rows.shape[0] // tensor_count
        each = [rows[k * size : (k + 1) * size] for k in range(tensor_count)]
        pair = [part[depth : depth + pair_rows].reshape(depth, pair_cols) for part in each]
        bias = [
            sum(part[depth + pair_rows + i].astype(F32) for i in range(3)) for part in each
        ]
        return (
            [part[:depth] for part in each],
            jnp.concatenate(pair, axis=1),
            jnp.concatenate(bias),
        )

    def columns(rows):
        count = rows.shape[0] // depth
        return jnp.concatenate([rows[k * depth : (k + 1) * depth] for k in range(count)], axis=1)

    out_turned = [out_weight[l].T for l in range(layer_total)]
    down_turned = [down_weight[l].T for l in range(layer_total)]
    query_rows = tensor_rows(query_payload(0))
    out_rows = tensor_rows(after(out_turned[0], tangent_come))
    if last > 0:
        rest = jnp.concatenate([query_payload(1), out_turned[1]], axis=0)
        rest = tensor_rows(after(rest, tokens_come))
        size = rest.shape[0] // tensor_count
        rest = [rest[k * size : (k + 1) * size] for k in range(tensor_count)]
    query_rows = after(query_rows, tokens_come, tangent_come, score_bias)
    cut_rows = cut * depth
    query_each, kv_full, bias_full = query_parts(query_rows)
    query_gather = Gather(
        [jnp.concatenate(query_each[:cut], axis=1)],
        [jnp.concatenate(query_each[cut:] + [kv_full], axis=1)],
    ).send()
    out_gather = Gather([columns(out_rows[:cut_rows])], [columns(out_rows[cut_rows:])]).send(
        *query_gather.come
    )
    w_query = query_gather.finish()
    sent = [parts[0][0] for parts in w_query]
    tokens_come, tangent_come = after((tokens_come, tangent_come), *sent)
    stream = place_rows(place_table, tokens_come, to_slots)
    last_branch = place_rows(place_table, tangent_come, to_slots)
    tangent = last_branch.astype(F32)
    stream = after(stream, last_branch)
    early_rows = local_rows // 2
    if last > 0:
        query_rows = jnp.concatenate([part[: size - depth] for part in rest], axis=0)
        out_rows = jnp.concatenate([part[size - depth :] for part in rest], axis=0)

    def branch_whole(early, late):
        parts = []
        for k in range(tensor_count):
            parts.append(early[k * early_rows : (k + 1) * early_rows])
            size = local_rows - early_rows
            parts.append(late[k * size : (k + 1) * size])
        return jnp.concatenate(parts, axis=0)

    vectors = jnp.concatenate(
        [norm1_gain, norm1_shift, out_bias, norm2_gain, norm2_shift, down_bias], axis=0
    )
    vectors = reorder(vectors, to_slots)
    gain_one, shift_one, bias_out, gain_two, shift_two, bias_down = [
        vectors[i * layer_total : (i + 1) * layer_total] for i in range(6)
    ]

    def rows_back(values):
        slots_out = place_rows(place_table.T, values, from_slots)
        come = lax.all_to_all(slots_out, "dp", split_axis=0, concat_axis=0, tiled=True)
        return slots_out, come

    saved = []
    for l in range(layer_total):
        if 0 < l < last:
            query_rows = tensor_rows(after(query_payload(l + 1), out_rows))
            out_rows = tensor_rows(after(out_turned[l + 1], query_rows))
        if l == 0:
            stream, normed = add_and_norm(stream, None, None, gain_one[:1], shift_one[:1])
        bias = jnp.concatenate([bias_full, jnp.zeros((HEAD,), F32), value_bias[l]])[None]
        queries = product(normed, w_query, bias)
        projected = queries
        pair_own = queries[:, width:]
        pair_all = tensor_swap(jnp.concatenate([pair_own] * tensor_count))
        pair_t = pair_all.T
        if l == 0:
            out_gather.settle(projected).send(projected)
            if last > 0:
                branch_early = tensor_rows(after(last_branch[:early_rows], projected))
            ff_gather = Gather([up_weight[0]], [down_turned[0]]).send(pair_all)
        mixed, log_totals = attend(
            queries, width, pair_all[:, :HEAD], pair_t[HEAD:], score_bias, score_scale
        )
        if l == 0:
            w_out = out_gather.settle(mixed).finish(mixed)
        if l > 0:
            mixed = after(mixed, *ff_gather.come)
            w_up, w_down = ff_gather.settle(mixed).finish(mixed)
        hidden_state, normed_two = add_and_norm(
            stream,
            product_turned(mixed, w_out),
            bias_out[l : l + 1],
            gain_two[l : l + 1],
            shift_two[l : l + 1],
        )
        if l == 0:
            normed_two = after(normed_two, *ff_gather.come)
            w_up, w_down = ff_gather.settle(normed_two).finish(normed_two)
        if l == 0 and last > 0:
            normed_two = after(normed_two, branch_early)
        normed_two_all = tensor_rows(normed_two)
        normed_two_all = after(normed_two_all, *arrays_of(w_up, w_down))
        if l == last:
            if last == 0:
                branch_all = tensor_rows(last_branch)
            act_grad = times(branch_all, w_down, plain_product, (), (F32,))[0]
            normed_two_all = after(normed_two_all, act_grad)
            activation, pre_grad = times(
                normed_two_all, w_up, gelu_and_back, (up_bias[l][None], act_grad), (BF16, BF16)
            )
            pre_gelu = None
        else:
            pre_gelu, activation = times(
                normed_two_all, w_up, gelu_both, (up_bias[l][None],), (F32, BF16)
            )
        saved.append(
            (
                stream,
                normed,
                queries,
                pair_all,
                pair_t,
                log_totals,
                mixed,
                hidden_state,
                normed_two_all,
                pre_gelu,
                activation,
                w_query,
                w_out,
                w_up,
                w_down,
            )
        )
        if l < last:
            query_each, kv_full, bias_full = query_parts(query_rows)
            attn_gather = Gather(
                [jnp.concatenate(query_each + [kv_full], axis=1)], [columns(out_rows)]
            )
            attn_gather.send(normed_two_all)
            down_part = times_turned(activation, w_down, BF16)
            down_part = after(down_part, *attn_gather.come)
            down_sum = tensor_sum(down_part)
            ff_gather = Gather([up_weight[l + 1]], [down_turned[l + 1]]).send(down_sum)
            w_query, w_out = [[parts] for parts in attn_gather.settle(down_part).finish(down_part)]
            if l == last - 1:
                sent = after(last_branch[early_rows:], w_query[0][0][0], w_out[0][0][0])
                branch_all = branch_whole(branch_early, tensor_rows(sent))
            down_sum = after(down_sum, *arrays_of(*w_query, *w_out))
            stream, normed = add_and_norm(
                hidden_state,
                down_sum,
                bias_down[l : l + 1],
                gain_one[l + 1 : l + 2],
                shift_one[l + 1 : l + 2],
            )

    reduced = [None] * layer_total
    ff_open = [None] * layer_total
    vector_grads = [None] * layer_total
    query_bias_grads = [None] * layer_total
    value_bias_grads = [None] * layer_total
    up_bias_grads = [None] * layer_total
    later = None
    for l in reversed(range(layer_total)):
        (
            stream_in,
            normed,
            queries,
            pair_all,
            pair_t,
            log_totals,
            mixed,
            hidden_state,
            normed_two_all,
            pre_gelu,
            activation,
            w_query,
            w_out,
            w_up,
            w_down,
        ) = saved[l]
        if l == last:
            branch_grad = last_branch
        if l < last:
            branch_all = tensor_rows(branch_grad)
            above, both_above, normed_above, attn_above, mixed_above, ff_scatter = later
            ff_scatter.settle(branch_grad).send()
            both_late, attn_late = after((both_above, attn_above), branch_grad, *ff_scatter.now())
            attn_scatter = Scatter(
                [gradient_half(normed_above, both_late, True)],
                [gradient_half(attn_late, mixed_above, True)],
            )
            attn_scatter.send()
            beside = ff_scatter.sent + attn_scatter.sent
            if above == last:
                final_sum = after(final_sum, *beside)
                layer_out = add_rounded(saved[last][7], final_sum, bias_down[last][None])
                out_slots, out_back = rows_back(layer_out)
                beside.append(out_slots)
            branch_all = after(branch_all, *beside)
            pre_grad = times(branch_all, w_down, gelu_back, (pre_gelu,), (BF16,))[0]
        normed_part = times_turned(pre_grad, w_up, BF16)
        if l < last:
            normed_part = after(normed_part, *ff_scatter.come, *attn_scatter.come)
        normed_two_grad = tensor_sum(normed_part)
        beside = []
        if l < last:
            attn_scatter.settle(normed_part).send()
            beside += attn_scatter.sent
            ff_open[above] = ff_scatter
        pre_late, branch_late = after((pre_grad, branch_all), normed_part)
        ff_scatter = Scatter(
            [gradient_half(normed_two_all, pre_late, True)],
            [gradient_half(branch_late, activation, True)],
        )
        ff_scatter.send()
        beside += ff_scatter.now() + ff_scatter.sent
        if l == last:
            down_bias_part = column_sum(after(branch_grad, normed_part))
        up_bias_grads[l] = column_sum(pre_late)
        beside += [down_bias_part, up_bias_grads[l]]
        if l == last:
            final_part = times_turned(after(activation, *ff_scatter.sent), w_down, BF16)
            beside.append(final_part)
        else:
            both_whole, out_whole = attn_scatter.finish(*ff_scatter.now())
            beside += [both_whole, out_whole]
        normed_two_grad = after(normed_two_grad, *beside)
        if l == last:
            final_sum = tensor_sum(after(final_part, normed_two_grad))
        hidden_grad, attn_grad, two_sums = norm_back(
            hidden_state, normed_two_grad, gain_two[l : l + 1], tangent
        )
        mixed_grad = product(attn_grad, w_out)
        if l == 0:
            attn_late = after(attn_grad, mixed_grad)
            out_scatter = Scatter(
                [gradient_half(attn_late, mixed[:, :split])],
                [gradient_half(attn_late, mixed[:, split:])],
            ).send()
            mixed_grad = after(mixed_grad, *out_scatter.sent)
        query_grad, pair_part = attend_back(
            queries,
            width,
            mixed_grad,
            pair_all[:, :HEAD],
            pair_all[:, HEAD:],
            pair_t[:HEAD],
            score_bias,
            log_totals,
            score_scale,
        )
        if l < last:
            both_whole, out_whole = after((both_whole, out_whole), query_grad)
            out_grad = tensor_sum(stack_columns(out_whole, tensor_count)).astype(F32).T
            query_sum = tensor_sum(stack_query(both_whole, width, query_cols, pair_cols))
            query_w_grad, kv_grad = split_query(query_sum, depth, pair_cols)
        pair_come = tensor_swap(pair_part.astype(BF16))
        pair_grad = sum(
            pair_come[k * local_rows : (k + 1) * local_rows].astype(F32)
            for k in range(tensor_count)
        ).astype(BF16)
        query_bias_grads[l] = jnp.sum(query_grad.astype(F32), axis=0)
        value_bias_grads[l] = jnp.sum(pair_grad[:, HEAD:].astype(F32), axis=0)
        both_grad = jnp.concatenate([query_grad, pair_grad], axis=1)
        if l == last > 0:
            both_grad = after(both_grad, *ff_scatter.come)
        if l == 0:
            both_grad = after(both_grad, *ff_scatter.come)
            both_scatter = Scatter(
                [gradient_half(normed, both_grad[:, :split])],
                [gradient_half(normed, both_grad[:, split:])],
            ).send()
            ff_scatter.settle(*both_scatter.sent).send()
            out_scatter.settle(*ff_scatter.sent).send()
            both_grad = after(both_grad, *both_scatter.sent, *out_scatter.sent, *ff_scatter.sent)
            ff_open[0] = ff_scatter
        normed_grad = product_turned(both_grad, w_query)
        if l == last > 0:
            normed_grad, final_sum = lax.optimization_barrier((normed_grad, final_sum))
        tangent, branch_grad, one_sums = norm_back(
            stream_in, normed_grad, gain_one[l : l + 1], hidden_grad
        )
        if l < last:
            reduced[above] = (query_w_grad, kv_grad, out_grad)
        later = (l, both_grad, normed, attn_grad, mixed, ff_scatter)
        vector_grads[l] = [
            one_sums[0],
            one_sums[1],
            two_sums[2],
            two_sums[0],
            two_sums[1],
            down_bias_part,
        ]
        down_bias_part = one_sums[2]

    stacked = jnp.stack([vector_grads[l][m] for m in range(6) for l in range(layer_total)])
    stacked = reorder(after(stacked, *ff_open[0].come), from_slots)
    query_rows = jnp.stack(query_bias_grads)
    value_rows = jnp.pad(jnp.stack(value_bias_grads), ((0, 0), (0, width - HEAD)))
    smalls = jnp.concatenate([stacked, query_rows, value_rows], axis=0)
    small_count = smalls.shape[0]
    smalls = jnp.concatenate([smalls, jnp.stack(up_bias_grads)], axis=0)
    smalls = smalls + flip(smalls, 1)
    total = smalls[:small_count]
    if tensor_count & (tensor_count - 1) == 0:
        for k in range(tensor_count.bit_length() - 1):
            total = total + lax.ppermute(
                total, "tensor", [(i, i ^ (1 << k)) for i in range(tensor_count)]
            )
    else:
        total = lax.psum(total, "tensor")
    total = jnp.concatenate([total, smalls[small_count:]], axis=0)
    for bit in plane_bits():
        total = total + flip(total, bit)
    up_bias_grad = total[small_count:]
    vector_sums = [total[m * layer_total : (m + 1) * layer_total] for m in range(8)]
    query_bias_grad = lax.dynamic_slice_in_dim(
        vector_sums[6], tensor_rank * query_cols, query_cols, 1
    )
    value_bias_grad = vector_sums[7][:, :HEAD]

    grad_back = rows_back(branch_grad)[1]
    out_back = after(out_back, tangent)
    both_scatter.settle(normed_grad).send()
    out_whole = jnp.concatenate(out_scatter.finish(), axis=1)
    out_grad = tensor_sum(stack_columns(out_whole, tensor_count)).astype(F32).T
    both_whole = jnp.concatenate(both_scatter.finish(), axis=1)
    query_stack = stack_query(both_whole, width, query_cols, pair_cols)
    query_w_grad, kv_grad = split_query(tensor_sum(query_stack), depth, pair_cols)
    reduced[0] = (query_w_grad, kv_grad, out_grad)
    up_stack, down_stack = [
        stack_sums([ff.open_sum(m) for ff in ff_open], m == 1) for m in range(2)
    ]
    if last == 0:
        layer_out = add_rounded(saved[last][7], final_sum, bias_down[last][None])
        out_back = rows_back(layer_out)[1]
    layer_rows = contract_rows(send_table, out_back).astype(BF16)
    token_rows = contract_rows(send_table, grad_back).astype(BF16)
    summed = [jnp.stack([reduced[l][m] for l in range(layer_total)]) for m in range(3)]
    return (
        layer_rows,
        token_rows,
        vector_sums[0],
        vector_sums[1],
        summed[0],
        query_bias_grad,
        summed[1],
        value_bias_grad,
        summed[2],
        vector_sums[2],
        vector_sums[3],
        vector_sums[4],
        up_stack,
        up_bias_grad,
        down_stack,
        vector_sums[5],
    )


def solution(mesh):
    rows = P(("dp", "tensor"), None)
    in_specs = (
        rows,
        rows,
        P(("dp", "tensor")),
        P("dp"),
        P(),
        P(),
        P(None, "dp", "tensor"),
        P(None, "tensor"),
        P(None, "dp", "tensor"),
        P(),
        P(None, "tensor", "dp"),
        P(),
        P(),
        P(),
        P(None, "dp", "tensor"),
        P(None, "tensor"),
        P(None, "tensor", "dp"),
        P(),
    )
    out_specs = (
        rows,
        rows,
        P(),
        P(),
        P(None, "dp", "tensor"),
        P(None, "tensor"),
        P(None, "dp", "tensor"),
        P(),
        P(None, "tensor", "dp"),
        P(),
        P(),
        P(),
        P(None, "dp", "tensor"),
        P(None, "tensor"),
        P(None, "tensor", "dp"),
        P(),
    )
    return jax.shard_map(local, mesh=mesh, in_specs=in_specs, out_specs=out_specs, check_vma=False)
```

```python
import jax
import jax.numpy as jnp
from jax import lax
from jax.experimental import pallas as pl
from jax.experimental.pallas import tpu as pltpu
from jax.sharding import PartitionSpec as P

HEAD = 128
EPSILON = 1e-05
BF16 = jnp.bfloat16
F32 = jnp.float32
LIGHT = pl.CostEstimate(flops=1, transcendentals=0, bytes_accessed=1)


def gelu_tanh(values):
    return jax.nn.gelu(values, approximate=True)


def matmul(left, right):
    return jnp.dot(left, right, preferred_element_type=F32)


def contract_rows(left, right):
    return lax.dot_general(left, right, (((0,), (0,)), ((), ())), preferred_element_type=F32)


def contract_cols(left, right):
    return lax.dot_general(left, right, (((1,), (1,)), ((), ())), preferred_element_type=F32)


def after(values, *others):
    return lax.optimization_barrier((values, others))[0]


def flip(values, bit):
    count = lax.axis_size("dp")
    return lax.ppermute(values, "dp", [(i, i ^ bit) for i in range(count)])


def turn(values, step):
    count = lax.axis_size("tensor")
    return lax.ppermute(values, "tensor", [((i + step) % count, i) for i in range(count)])


def plane_bits():
    count = lax.axis_size("dp")
    return [1 << k for k in range(1, count.bit_length() - 1)]


def slot_order():
    count = lax.axis_size("dp")
    evens = list(range(0, count, 2))
    return evens + [r ^ 1 for r in evens]


def join_rows(arrays):
    return arrays[0] if len(arrays) == 1 else jnp.concatenate(arrays, axis=0)


def blocks_of(parts, wanted):
    runs = []
    where = {}
    for array, blocks in parts:
        rows = array.shape[0] // len(blocks)
        for i, block in enumerate(blocks):
            where[block] = (array, i * rows, rows)
    for block in wanted:
        array, start, rows = where[block]
        if runs and runs[-1][0] is array and runs[-1][2] == start:
            runs[-1][2] += rows
        else:
            runs.append([array, start, start + rows])
    return join_rows([lax.slice_in_dim(array, low, high) for array, low, high in runs])


class Gather:
    def __init__(self, first, second):
        bits = plane_bits()
        self.members = [
            [order, [(array, [0])]]
            for group, order in ((first, bits), (second, bits[::-1]))
            for array in group
        ]
        self.taken = 0
        self.come = []

    def send(self, *gate):
        gate = gate + tuple(self.come)
        self.come = []
        for member in self.members:
            order, parts = member
            bit = order[self.taken]
            blocks = [block for _, part in parts for block in part]
            whole = join_rows([array for array, _ in parts])
            come = flip(after(whole, *gate) if gate else whole, bit)
            self.come.append(come)
            member[1] = [(whole, blocks), (come, [block | bit for block in blocks])]
        self.taken += 1
        return self

    def settle(self, *late):
        for member in self.members:
            own, (come, blocks) = member[1]
            member[1] = [own, (after(come, *late), blocks)]
        return self

    def finish(self, *gate):
        while self.taken < len(plane_bits()):
            self.send(*gate)
        return [
            parts + [(flip(array, 1), [block | 1 for block in blocks]) for array, blocks in parts]
            for _, parts in self.members
        ]


def add_blocks(half, count, keep, come, kind):
    rows, columns = half.shape[0] // count, half.shape[1]
    stride = keep[1] - keep[0] if len(keep) > 1 else 1

    def kernel(half_ref, come_ref, out_ref):
        out_ref[...] = (half_ref[...].astype(F32) + come_ref[...].astype(F32)).astype(kind)

    block = (rows, columns)
    return pl.pallas_call(
        kernel,
        grid=(len(keep),),
        in_specs=[
            pl.BlockSpec(block, lambda i: (keep[0] + i * stride, 0)),
            pl.BlockSpec(block, lambda i: (i, 0)),
        ],
        out_specs=pl.BlockSpec(block, lambda i: (i, 0)),
        out_shape=jax.ShapeDtypeStruct(come.shape, kind),
        cost_estimate=LIGHT,
        name="add_blocks",
    )(half, come)


def take_blocks(half, count, keep):
    rows, columns = half.shape[0] // count, half.shape[1]
    stride = keep[1] - keep[0] if len(keep) > 1 else 1
    block = (rows, columns)
    return pl.pallas_call(
        lambda half_ref, out_ref: out_ref.__setitem__(..., half_ref[...]),
        grid=(len(keep),),
        in_specs=[pl.BlockSpec(block, lambda i: (keep[0] + i * stride, 0))],
        out_specs=pl.BlockSpec(block, lambda i: (i, 0)),
        out_shape=jax.ShapeDtypeStruct((len(keep) * rows, columns), half.dtype),
        cost_estimate=LIGHT,
        name="take_blocks",
    )(half)


def column_sum(values):
    rows, columns = values.shape
    tile = 256 if rows % 256 == 0 else rows

    def kernel(values_ref, out_ref):
        @pl.when(pl.program_id(0) == 0)
        def _():
            out_ref[...] = jnp.zeros_like(out_ref)

        out_ref[...] += jnp.sum(values_ref[...].astype(F32), axis=0, keepdims=True)

    return pl.pallas_call(
        kernel,
        grid=(rows // tile,),
        in_specs=[pl.BlockSpec((tile, columns), lambda i: (i, 0))],
        out_specs=pl.BlockSpec((1, columns), lambda i: (0, 0)),
        out_shape=jax.ShapeDtypeStruct((1, columns), F32),
        cost_estimate=LIGHT,
        name="column_sum",
    )(values)[0]


class Scatter:
    def __init__(self, first, second):
        bits = plane_bits()
        evens = list(range(0, lax.axis_size("dp"), 2))
        self.members = [
            [order, half, evens]
            for group, order in ((first, bits), (second, bits[::-1]))
            for half in group
        ]
        self.taken = 0
        self.come = None

    def send(self, *gate):
        self.come = []
        self.sent = []
        for order, half, blocks in self.members:
            spots = [i for i, block in enumerate(blocks) if block & order[self.taken]]
            piece = take_blocks(half, len(blocks), spots)
            piece = after(piece, *gate) if gate else piece
            self.sent.append(piece)
            self.come.append(flip(piece, order[self.taken]))
        self.taken += 1
        return self

    def settle(self, *late):
        last = self.taken == len(plane_bits())
        late = late + tuple(self.come)
        for member, come in zip(self.members, self.come):
            order, half, blocks = member
            keep = [block for block in blocks if not block & order[self.taken - 1]]
            if late:
                come = after(come, *late)
            spots = [blocks.index(block) for block in keep]
            member[1:] = [
                add_blocks(half, len(blocks), spots, come, F32 if last else BF16),
                keep,
            ]
        self.come = None
        return self

    def now(self):
        return [half for _, half, _ in self.members]

    def open_sum(self, member):
        while self.taken < len(plane_bits()):
            self.settle()
            self.send()
        order, half, blocks = self.members[member]
        spot = next(i for i, block in enumerate(blocks) if not block & order[-1])
        return half, len(blocks), spot, self.come[member]

    def finish(self, *late):
        if self.come:
            self.settle(*late)
        while self.taken < len(plane_bits()):
            self.send()
            self.settle(*late)
        return [half.astype(F32) for _, half, _ in self.members]


def stack_sums(items, turned):
    rows, columns = items[0][3].shape
    shape = (1, columns, rows) if turned else (1, rows, columns)

    def kernel(*refs):
        for l in range(len(items)):

            @pl.when(pl.program_id(0) == l)
            def _():
                total = refs[2 * l][...].astype(F32) + refs[2 * l + 1][...].astype(F32)
                refs[-1][0] = total.T if turned else total

    specs, arrays = [], []
    for half, _, spot, come in items:
        specs.append(pl.BlockSpec((rows, columns), lambda l, spot=spot: (spot, 0)))
        specs.append(pl.BlockSpec((rows, columns), lambda l: (0, 0)))
        arrays += [half, come]
    return pl.pallas_call(
        kernel,
        grid=(len(items),),
        in_specs=specs,
        out_specs=pl.BlockSpec(shape, lambda l: (l, 0, 0)),
        out_shape=jax.ShapeDtypeStruct((len(items),) + shape[1:], F32),
        cost_estimate=LIGHT,
        name="stack_sums",
    )(*arrays)


def turned_product(features, values, side, extra=None):
    rows, depth = features.shape
    columns = values.shape[1]
    tile = 256
    steps = depth // 2 // tile

    def kernel(left_ref, right_ref, *refs):
        total = matmul(left_ref[...].T, right_ref[...])
        if extra is not None:
            total = total + refs[0][...].astype(F32)
        refs[-1][...] = total.astype(BF16)

    tiles = pl.BlockSpec((tile, columns), lambda i: (i, 0))
    return pl.pallas_call(
        kernel,
        grid=(steps,),
        in_specs=[
            pl.BlockSpec((rows, tile), lambda i: (0, i + side * steps)),
            pl.BlockSpec((rows, columns), lambda i: (0, 0)),
        ]
        + ([tiles] if extra is not None else []),
        out_specs=tiles,
        out_shape=jax.ShapeDtypeStruct((depth // 2, columns), BF16),
        cost_estimate=LIGHT,
        name="turned_product",
    )(features, values, *([extra] if extra is not None else []))


def gradient_half(features, values, kernel=False):
    if kernel:
        return turned_product(features, values, 0, flip(turned_product(features, values, 1), 1))
    half = features.shape[1] // 2
    far = contract_rows(features[:, half:], values).astype(BF16)
    near = contract_rows(features[:, :half], values) + flip(far, 1).astype(F32)
    return near.astype(BF16)


def norm_parts(values):
    centred = values - jnp.mean(values, axis=-1, keepdims=True)
    return centred, lax.rsqrt(jnp.mean(centred * centred, axis=-1, keepdims=True) + EPSILON)


def row_tile(rows):
    return 64 if rows % 64 == 0 else rows


def add_and_norm(base, part, bias, gain, shift):
    rows, width = base.shape
    tile = row_tile(rows)
    wide = pl.BlockSpec((tile, width), lambda i: (i, 0))
    line = pl.BlockSpec((1, width), lambda i: (0, 0))
    added = [] if part is None else [part, bias]

    def kernel(gain_ref, shift_ref, base_ref, *refs):
        total = base_ref[...].astype(F32)
        if part is not None:
            total = total + refs[0][...].astype(F32) + refs[1][...]
        centred, slope = norm_parts(total)
        refs[-2][...] = total
        refs[-1][...] = (centred * slope * gain_ref[...] + shift_ref[...]).astype(BF16)

    return pl.pallas_call(
        kernel,
        grid=(rows // tile,),
        in_specs=[line, line, wide] + [wide, line][: len(added)],
        out_specs=[wide, wide],
        out_shape=[
            jax.ShapeDtypeStruct((rows, width), F32),
            jax.ShapeDtypeStruct((rows, width), BF16),
        ],
        cost_estimate=LIGHT,
        name="add_and_norm",
    )(gain, shift, base, *added)


def norm_back(values, grad, gain, tangent):
    rows, width = values.shape
    tile = row_tile(rows)
    wide = pl.BlockSpec((tile, width), lambda i: (i, 0))

    def kernel(gain_ref, values_ref, grad_ref, tangent_ref, out_ref, low_ref, sums_ref):
        centred, slope = norm_parts(values_ref[...])
        scaled = centred * slope
        grads = grad_ref[...].astype(F32)
        inner = grads * gain_ref[...]
        mean_inner = jnp.mean(inner, axis=-1, keepdims=True)
        mean_scaled = jnp.mean(inner * scaled, axis=-1, keepdims=True)
        total = tangent_ref[...] + slope * (inner - mean_inner - scaled * mean_scaled)
        low = total.astype(BF16)
        out_ref[...] = total
        low_ref[...] = low

        @pl.when(pl.program_id(0) == 0)
        def _():
            sums_ref[...] = jnp.zeros_like(sums_ref)

        for i, term in enumerate((grads * scaled, grads, low.astype(F32))):
            sums_ref[i : i + 1, :] += jnp.sum(term, axis=0, keepdims=True)

    return pl.pallas_call(
        kernel,
        grid=(rows // tile,),
        in_specs=[pl.BlockSpec((1, width), lambda i: (0, 0)), wide, wide, wide],
        out_specs=[wide, wide, pl.BlockSpec((8, width), lambda i: (0, 0))],
        out_shape=[
            jax.ShapeDtypeStruct((rows, width), F32),
            jax.ShapeDtypeStruct((rows, width), BF16),
            jax.ShapeDtypeStruct((8, width), F32),
        ],
        cost_estimate=LIGHT,
        name="norm_back",
    )(gain, values, grad, tangent)


def plain_product(total):
    return (total,)


def round_product(total):
    return (total.astype(BF16),)


def bias_round(total, bias):
    return ((total + bias).astype(BF16),)


def gelu_both(total, bias):
    value = total + bias
    return value, gelu_tanh(value).astype(BF16)


def gelu_slope(values):
    factor = 0.7978845608028654
    square = values * values
    wave = jnp.tanh(factor * (values + 0.044715 * (square * values)))
    return 0.5 * (1.0 + wave) + (0.5 * factor) * values * (1.0 - wave * wave) * (
        1.0 + (3.0 * 0.044715) * square
    )


def gelu_and_back(total, bias, act_grad):
    value = total + bias
    return gelu_tanh(value).astype(BF16), (act_grad * gelu_slope(value)).astype(BF16)


def gelu_back(total, value):
    return ((total * gelu_slope(value)).astype(BF16),)


def times(left, parts, finish, extras, types):
    rows, depth = left.shape
    columns = parts[0][0].shape[1]
    height = depth // lax.axis_size("dp")
    place = {block: i for i, block in enumerate(slot_order())}
    if height % 128:
        return finish(matmul(left, blocks_of(parts, slot_order())), *extras)
    tile = next(size for size in (768, 640, 512, 384, 256, 128, columns) if columns % size == 0)
    spots = [[place[block] * height for block in blocks] for _, blocks in parts]

    def kernel(left_ref, *refs):
        part_refs = refs[: len(parts)]
        extra_refs = refs[len(parts) : len(parts) + len(extras)]
        total = None
        for ref, starts in zip(part_refs, spots):
            for i, start in enumerate(starts):
                piece = matmul(
                    left_ref[:, start : start + height], ref[i * height : (i + 1) * height, :]
                )
                total = piece if total is None else total + piece
        values = finish(total, *[ref[...] for ref in extra_refs])
        for ref, value in zip(refs[len(parts) + len(extras) :], values):
            ref[...] = value

    return pl.pallas_call(
        kernel,
        grid=(columns // tile,),
        in_specs=[pl.BlockSpec((rows, depth), lambda j: (0, 0))]
        + [pl.BlockSpec((array.shape[0], tile), lambda j: (0, j)) for array, _ in parts]
        + [pl.BlockSpec((extra.shape[0], tile), lambda j: (0, j)) for extra in extras],
        out_specs=[pl.BlockSpec((rows, tile), lambda j: (0, j)) for _ in types],
        out_shape=[jax.ShapeDtypeStruct((rows, columns), kind) for kind in types],
        cost_estimate=LIGHT,
        name="times",
    )(left, *[array for array, _ in parts], *extras)


def times_turned(left, parts, kind):
    rows, depth = left.shape
    count = lax.axis_size("dp")
    height = sum(array.shape[0] for array, _ in parts) // count
    place = {block: i for i, block in enumerate(slot_order())}
    if height % 128:
        return contract_cols(left, blocks_of(parts, slot_order())).astype(kind)
    tile = 256 if rows % 256 == 0 else rows
    spots = [[place[block] * height for block in blocks] for _, blocks in parts]

    def kernel(left_ref, *refs):
        for ref, starts in zip(refs, spots):
            for i, start in enumerate(starts):
                piece = contract_cols(left_ref[...], ref[i * height : (i + 1) * height, :])
                refs[-1][:, start : start + height] = piece.astype(kind)

    whole = [
        pl.BlockSpec(array.shape, lambda i: (0, 0), pipeline_mode=pl.Buffered(1))
        for array, _ in parts
    ]
    return pl.pallas_call(
        kernel,
        grid=(rows // tile,),
        in_specs=[pl.BlockSpec((tile, depth), lambda i: (i, 0))] + whole,
        out_specs=pl.BlockSpec((tile, count * height), lambda i: (i, 0)),
        out_shape=jax.ShapeDtypeStruct((rows, count * height), kind),
        cost_estimate=LIGHT,
        name="times_turned",
    )(left, *[array for array, _ in parts])


def arrays_of(*weights):
    return [array for parts in weights for array, _ in parts]


def tensor_swap(values):
    return lax.all_to_all(values, "tensor", split_axis=0, concat_axis=0, tiled=True)


def tensor_rows(values):
    return lax.all_gather(values, "tensor", axis=0, tiled=True)


def tensor_sum(values):
    return lax.psum_scatter(values, "tensor", scatter_dimension=0, tiled=True)


def stack_columns(whole, count):
    width = whole.shape[1] // count
    whole = whole.astype(BF16)
    return jnp.concatenate([whole[:, k * width : (k + 1) * width] for k in range(count)], axis=0)


def stack_query(whole, width, query_cols, pair_cols):
    rows = whole.shape[0]
    whole = whole.astype(BF16)
    pieces = []
    for k in range(width // query_cols):
        pieces.append(whole[:, k * query_cols : (k + 1) * query_cols])
        pair = whole[:, width + k * pair_cols : width + (k + 1) * pair_cols]
        pieces.append(pair.reshape(rows * pair_cols // query_cols, query_cols))
    return jnp.concatenate(pieces, axis=0)


def split_query(total, rows, pair_cols):
    total = total.astype(F32)
    return total[:rows], total[rows:].reshape(rows, pair_cols)


def copy_block(table, source, target):
    target[...] = source[...]


def reorder(values, table):
    rows, columns = values.shape
    count = table.shape[0]
    width = columns // count
    if width % 128:
        return jnp.take(values.reshape(rows, count, width), table, axis=1).reshape(rows, columns)
    return pl.pallas_call(
        copy_block,
        grid_spec=pltpu.PrefetchScalarGridSpec(
            num_scalar_prefetch=1,
            grid=(count,),
            in_specs=[pl.BlockSpec((rows, width), lambda j, table: (0, table[j]))],
            out_specs=pl.BlockSpec((rows, width), lambda j, table: (0, j)),
        ),
        out_shape=jax.ShapeDtypeStruct(values.shape, values.dtype),
        cost_estimate=LIGHT,
        name="reorder",
    )(table, values)


def place_rows(left, values, table):
    rows, count = values.shape[0], table.shape[0]
    width = values.shape[1] // (128 * count) * 128
    if width * count != values.shape[1] // 256 * 256:
        columns = values.shape[1] // (count * 64) * (count * 64)
        return matmul(left, reorder(values[:, :columns], table)).astype(BF16)

    def kernel(table_ref, left_ref, source, target):
        target[...] = matmul(left_ref[...], source[...]).astype(BF16)

    return pl.pallas_call(
        kernel,
        grid_spec=pltpu.PrefetchScalarGridSpec(
            num_scalar_prefetch=1,
            grid=(count,),
            in_specs=[
                pl.BlockSpec((rows, rows), lambda j, table: (0, 0)),
                pl.BlockSpec((rows, width), lambda j, table: (0, table[j])),
            ],
            out_specs=pl.BlockSpec((rows, width), lambda j, table: (0, j)),
        ),
        out_shape=jax.ShapeDtypeStruct((rows, width * count), BF16),
        cost_estimate=LIGHT,
        name="place_rows",
    )(table, left, values)


def add_rounded(base, part, bias):
    rows, width = base.shape
    tile = 64 if rows % 64 == 0 else rows
    wide = pl.BlockSpec((tile, width), lambda i: (i, 0))

    def kernel(base_ref, part_ref, bias_ref, out_ref):
        total = base_ref[...] + part_ref[...].astype(F32) + bias_ref[...]
        out_ref[...] = total.astype(BF16)

    return pl.pallas_call(
        kernel,
        grid=(rows // tile,),
        in_specs=[wide, wide, pl.BlockSpec((1, width), lambda i: (0, 0))],
        out_specs=wide,
        out_shape=jax.ShapeDtypeStruct((rows, width), BF16),
        cost_estimate=LIGHT,
        name="add_rounded",
    )(base, part, bias)


def stack_heads(block):
    return jnp.concatenate([block[:, :HEAD], block[:, HEAD:]], axis=0)


def attend_kernel(scale, query_ref, key_ref, value_t_ref, bias_ref, out_ref, log_ref):
    rows = query_ref.shape[0]
    queries = stack_heads(query_ref[...])
    scores = contract_cols(key_ref[...], queries) * scale + bias_ref[...]
    top = jnp.max(scores, axis=0, keepdims=True)
    exps = jnp.exp(scores - top)
    total = jnp.sum(exps, axis=0, keepdims=True)
    probs = (exps * (1.0 / total)).astype(BF16)
    mixed = matmul(value_t_ref[...], probs).T.astype(BF16)
    out_ref[:, :HEAD] = mixed[:rows]
    out_ref[:, HEAD:] = mixed[rows:]
    log_ref[0] = top + jnp.log(total)


def attend(queries, columns, key_rows, value_t, bias, scale):
    rows, keys = queries.shape[0], key_rows.shape[0]
    pairs = columns // (2 * HEAD)

    def kernel(*refs):
        attend_kernel(scale, *refs)

    return pl.pallas_call(
        kernel,
        grid=(pairs,),
        in_specs=[
            pl.BlockSpec((rows, 2 * HEAD), lambda i: (0, i)),
            pl.BlockSpec((keys, HEAD), lambda i: (0, 0)),
            pl.BlockSpec((HEAD, keys), lambda i: (0, 0)),
            pl.BlockSpec((keys, 2 * rows), lambda i: (0, 0)),
        ],
        out_specs=[
            pl.BlockSpec((rows, 2 * HEAD), lambda i: (0, i)),
            pl.BlockSpec((1, 1, 2 * rows), lambda i: (i, 0, 0)),
        ],
        out_shape=[
            jax.ShapeDtypeStruct((rows, columns), BF16),
            jax.ShapeDtypeStruct((pairs, 1, 2 * rows), F32),
        ],
        cost_estimate=LIGHT,
        name="attend",
    )(queries, key_rows, value_t, bias)


def attend_back_kernel(
    scale, query_ref, dout_ref, key_ref, value_ref, key_t_ref, bias_ref, log_ref, grad_ref, pair_ref
):
    rows = query_ref.shape[0]

    @pl.when(pl.program_id(0) == 0)
    def _():
        pair_ref[...] = jnp.zeros_like(pair_ref)

    queries = stack_heads(query_ref[...])
    douts = stack_heads(dout_ref[...])
    scores = contract_cols(key_ref[...], queries) * scale + bias_ref[...]
    probs = jnp.exp(scores - log_ref[0])
    prob_grad = contract_cols(value_ref[...], douts)
    inner = jnp.sum(probs * prob_grad, axis=0, keepdims=True)
    score_grad = (probs * (prob_grad - inner) * scale).astype(BF16)
    pair_ref[:, :HEAD] += matmul(score_grad, queries)
    pair_ref[:, HEAD:] += matmul(probs.astype(BF16), douts)
    query_grad = matmul(key_t_ref[...], score_grad).T.astype(BF16)
    grad_ref[:, :HEAD] = query_grad[:rows]
    grad_ref[:, HEAD:] = query_grad[rows:]


def attend_back(queries, columns, douts, key_rows, value_rows, key_t, bias, log_totals, scale):
    rows, keys = queries.shape[0], key_rows.shape[0]
    pairs = columns // (2 * HEAD)

    def kernel(*refs):
        attend_back_kernel(scale, *refs)

    return pl.pallas_call(
        kernel,
        grid=(pairs,),
        in_specs=[
            pl.BlockSpec((rows, 2 * HEAD), lambda i: (0, i)),
            pl.BlockSpec((rows, 2 * HEAD), lambda i: (0, i)),
            pl.BlockSpec((keys, HEAD), lambda i: (0, 0)),
            pl.BlockSpec((keys, HEAD), lambda i: (0, 0)),
            pl.BlockSpec((HEAD, keys), lambda i: (0, 0)),
            pl.BlockSpec((keys, 2 * rows), lambda i: (0, 0)),
            pl.BlockSpec((1, 1, 2 * rows), lambda i: (i, 0, 0)),
        ],
        out_specs=[
            pl.BlockSpec((rows, 2 * HEAD), lambda i: (0, i)),
            pl.BlockSpec((keys, 2 * HEAD), lambda i: (0, 0)),
        ],
        out_shape=[
            jax.ShapeDtypeStruct((rows, columns), BF16),
            jax.ShapeDtypeStruct((keys, 2 * HEAD), F32),
        ],
        cost_estimate=LIGHT,
        name="attend_back",
    )(queries, douts, key_rows, value_rows, key_t, bias, log_totals)


def local(
    tokens,
    cotangent,
    deal,
    segment,
    norm1_gain,
    norm1_shift,
    query_weight,
    query_bias,
    kv_weight,
    value_bias,
    out_weight,
    out_bias,
    norm2_gain,
    norm2_shift,
    up_weight,
    up_bias,
    down_weight,
    down_bias,
):
    local_rows, width = tokens.shape
    dp_count = lax.axis_size("dp")
    tensor_count = lax.axis_size("tensor")
    dp_rank = lax.axis_index("dp")
    tensor_rank = lax.axis_index("tensor")
    slot_rows = local_rows // dp_count
    layer_total = query_weight.shape[0]
    group_rows = local_rows * tensor_count
    query_cols = query_weight.shape[2]
    pair_cols = kv_weight.shape[2]
    score_scale = HEAD ** (-0.5)
    order = slot_order()
    to_slots = jnp.asarray(order, jnp.int32) ^ dp_rank
    place_of = [order.index(r) for r in range(dp_count)]
    from_slots = jnp.take(
        jnp.asarray(place_of, jnp.int32), jnp.arange(dp_count, dtype=jnp.int32) ^ dp_rank
    )

    target_dev = deal // local_rows // tensor_count
    target_row = deal % local_rows
    dev_ids = jnp.arange(dp_count, dtype=jnp.int32)
    dev_match = (target_dev[:, None] == dev_ids[None, :]).astype(jnp.int32)
    earlier = jnp.cumsum(dev_match, axis=0) - dev_match
    slot_of = target_dev * slot_rows + jnp.sum(earlier * dev_match, axis=1)
    row_ids = jnp.arange(local_rows, dtype=jnp.int32)
    send_table = (row_ids[:, None] == slot_of[None, :]).astype(BF16)
    place_cols = jnp.broadcast_to(target_row.astype(BF16)[:, None], (local_rows, HEAD))
    tokens_sent = matmul(send_table, jnp.concatenate([tokens, place_cols], axis=1)).astype(BF16)
    tokens_come = lax.all_to_all(tokens_sent, "dp", split_axis=0, concat_axis=0, tiled=True)
    tangent_sent = matmul(send_table, cotangent).astype(BF16)
    tangent_come = lax.all_to_all(tangent_sent, "dp", split_axis=0, concat_axis=0, tiled=True)
    arrived_place = tokens_come[:, width].astype(jnp.int32)
    place_table = (row_ids[:, None] == arrived_place[None, :]).astype(BF16)

    places = jnp.arange(group_rows, dtype=jnp.int32)
    own_places = tensor_rank * local_rows + row_ids
    own_labels = lax.dynamic_slice_in_dim(segment, tensor_rank * local_rows, local_rows)
    allowed = (places[:, None] <= own_places[None, :]) & (
        segment[:, None] == own_labels[None, :]
    )
    score_bias = jnp.where(allowed, 0.0, -1e30).astype(F32)
    score_bias = jnp.concatenate([score_bias, score_bias], axis=1)

    def product(left, weights, bias=None):
        pieces, start = [], 0
        for parts in weights:
            size = parts[0][0].shape[1]
            if bias is None:
                pieces.append(times(left, parts, round_product, (), (BF16,))[0])
            else:
                extra = (bias[:, start : start + size],)
                pieces.append(times(left, parts, bias_round, extra, (BF16,))[0])
            start += size
        return pieces[0] if len(pieces) == 1 else jnp.concatenate(pieces, axis=1)

    def product_turned(left, weights):
        total, start = None, 0
        for parts in weights:
            size = parts[0][0].shape[1]
            piece = times_turned(left[:, start : start + size], parts, F32)
            total = piece if total is None else total + piece
            start += size
        return total

    last = layer_total - 1
    split = width // 2
    cut = tensor_count // 2
    depth = query_weight.shape[1]
    pair_rows = depth * pair_cols // query_cols
    bias_rows = 16

    def query_payload(l):
        rest, terms = query_bias[l], []
        for _ in range(3):
            terms.append(rest.astype(BF16))
            rest = rest - terms[-1].astype(F32)
        terms = jnp.pad(jnp.stack(terms), ((0, bias_rows - 3), (0, 0)))
        return jnp.concatenate(
            [query_weight[l], kv_weight[l].reshape(pair_rows, query_cols), terms], axis=0
        )

    def query_parts(rows):
        size = rows.shape[0] // tensor_count
        each = [rows[k * size : (k + 1) * size] for k in range(tensor_count)]
        pair = [part[depth : depth + pair_rows].reshape(depth, pair_cols) for part in each]
        bias = [
            sum(part[depth + pair_rows + i].astype(F32) for i in range(3)) for part in each
        ]
        return (
            [part[:depth] for part in each],
            jnp.concatenate(pair, axis=1),
            jnp.concatenate(bias),
        )

    def columns(rows):
        count = rows.shape[0] // depth
        return jnp.concatenate([rows[k * depth : (k + 1) * depth] for k in range(count)], axis=1)

    out_turned = [out_weight[l].T for l in range(layer_total)]
    down_turned = [down_weight[l].T for l in range(layer_total)]
    query_rows = tensor_rows(query_payload(0))
    out_rows = tensor_rows(after(out_turned[0], tangent_come))
    if last > 0:
        rest = jnp.concatenate([query_payload(1), out_turned[1]], axis=0)
        rest = tensor_rows(after(rest, tokens_come))
        size = rest.shape[0] // tensor_count
        rest = [rest[k * size : (k + 1) * size] for k in range(tensor_count)]
    query_rows = after(query_rows, tokens_come, tangent_come, score_bias)
    cut_rows = cut * depth
    query_each, kv_full, bias_full = query_parts(query_rows)
    query_gather = Gather(
        [jnp.concatenate(query_each[:cut], axis=1)],
        [jnp.concatenate(query_each[cut:] + [kv_full], axis=1)],
    ).send()
    out_gather = Gather([columns(out_rows[:cut_rows])], [columns(out_rows[cut_rows:])]).send(
        *query_gather.come
    )
    w_query = query_gather.finish()
    sent = [parts[0][0] for parts in w_query]
    tokens_come, tangent_come = after((tokens_come, tangent_come), *sent)
    stream = place_rows(place_table, tokens_come, to_slots)
    last_branch = place_rows(place_table, tangent_come, to_slots)
    tangent = last_branch.astype(F32)
    stream = after(stream, last_branch)
    early_rows = local_rows // 2
    if last > 0:
        query_rows = jnp.concatenate([part[: size - depth] for part in rest], axis=0)
        out_rows = jnp.concatenate([part[size - depth :] for part in rest], axis=0)

    def branch_whole(early, late):
        parts = []
        for k in range(tensor_count):
            parts.append(early[k * early_rows : (k + 1) * early_rows])
            size = local_rows - early_rows
            parts.append(late[k * size : (k + 1) * size])
        return jnp.concatenate(parts, axis=0)

    vectors = jnp.concatenate(
        [norm1_gain, norm1_shift, out_bias, norm2_gain, norm2_shift, down_bias], axis=0
    )
    vectors = reorder(vectors, to_slots)
    gain_one, shift_one, bias_out, gain_two, shift_two, bias_down = [
        vectors[i * layer_total : (i + 1) * layer_total] for i in range(6)
    ]

    def rows_back(values):
        slots_out = place_rows(place_table.T, values, from_slots)
        come = lax.all_to_all(slots_out, "dp", split_axis=0, concat_axis=0, tiled=True)
        return slots_out, come

    saved = []
    for l in range(layer_total):
        if 0 < l < last:
            query_rows = tensor_rows(after(query_payload(l + 1), out_rows))
            out_rows = tensor_rows(after(out_turned[l + 1], query_rows))
        if l == 0:
            stream, normed = add_and_norm(stream, None, None, gain_one[:1], shift_one[:1])
        bias = jnp.concatenate([bias_full, jnp.zeros((HEAD,), F32), value_bias[l]])[None]
        queries = product(normed, w_query, bias)
        projected = queries
        pair_own = queries[:, width:]
        pair_all = tensor_swap(jnp.concatenate([pair_own] * tensor_count))
        pair_t = pair_all.T
        if l == 0:
            out_gather.settle(projected).send(projected)
            if last > 0:
                branch_early = tensor_rows(after(last_branch[:early_rows], projected))
            ff_gather = Gather([up_weight[0]], [down_turned[0]]).send(projected)
        mixed, log_totals = attend(
            queries, width, pair_all[:, :HEAD], pair_t[HEAD:], score_bias, score_scale
        )
        if l == 0:
            w_out = out_gather.settle(mixed).finish(mixed)
        if l > 0:
            mixed = after(mixed, *ff_gather.come)
            w_up, w_down = ff_gather.settle(mixed).finish(mixed)
        hidden_state, normed_two = add_and_norm(
            stream,
            product_turned(mixed, w_out),
            bias_out[l : l + 1],
            gain_two[l : l + 1],
            shift_two[l : l + 1],
        )
        if l == 0:
            normed_two = after(normed_two, *ff_gather.come)
            w_up, w_down = ff_gather.settle(normed_two).finish(normed_two)
        if l == 0 and last > 0:
            normed_two = after(normed_two, branch_early)
        normed_two_all = tensor_rows(normed_two)
        normed_two_all = after(normed_two_all, *arrays_of(w_up, w_down))
        if l == last:
            if last == 0:
                branch_all = tensor_rows(last_branch)
            act_grad = times(branch_all, w_down, plain_product, (), (F32,))[0]
            normed_two_all = after(normed_two_all, act_grad)
            activation, pre_grad = times(
                normed_two_all, w_up, gelu_and_back, (up_bias[l][None], act_grad), (BF16, BF16)
            )
            pre_gelu = None
        else:
            pre_gelu, activation = times(
                normed_two_all, w_up, gelu_both, (up_bias[l][None],), (F32, BF16)
            )
        saved.append(
            (
                stream,
                normed,
                queries,
                pair_all,
                pair_t,
                log_totals,
                mixed,
                hidden_state,
                normed_two_all,
                pre_gelu,
                activation,
                w_query,
                w_out,
                w_up,
                w_down,
            )
        )
        if l < last:
            query_each, kv_full, bias_full = query_parts(query_rows)
            attn_gather = Gather(
                [jnp.concatenate(query_each + [kv_full], axis=1)], [columns(out_rows)]
            )
            attn_gather.send(normed_two_all)
            down_part = times_turned(activation, w_down, BF16)
            down_part = after(down_part, *attn_gather.come)
            down_sum = tensor_sum(down_part)
            ff_gather = Gather([up_weight[l + 1]], [down_turned[l + 1]]).send(down_sum)
            w_query, w_out = [[parts] for parts in attn_gather.settle(down_part).finish(down_part)]
            if l == last - 1:
                sent = after(last_branch[early_rows:], w_query[0][0][0], w_out[0][0][0])
                branch_all = branch_whole(branch_early, tensor_rows(sent))
            down_sum = after(down_sum, *arrays_of(*w_query, *w_out))
            stream, normed = add_and_norm(
                hidden_state,
                down_sum,
                bias_down[l : l + 1],
                gain_one[l + 1 : l + 2],
                shift_one[l + 1 : l + 2],
            )

    reduced = [None] * layer_total
    ff_open = [None] * layer_total
    vector_grads = [None] * layer_total
    query_bias_grads = [None] * layer_total
    value_bias_grads = [None] * layer_total
    up_bias_grads = [None] * layer_total
    later = None
    for l in reversed(range(layer_total)):
        (
            stream_in,
            normed,
            queries,
            pair_all,
            pair_t,
            log_totals,
            mixed,
            hidden_state,
            normed_two_all,
            pre_gelu,
            activation,
            w_query,
            w_out,
            w_up,
            w_down,
        ) = saved[l]
        if l == last:
            branch_grad = last_branch
        if l < last:
            branch_all = tensor_rows(branch_grad)
            above, both_above, normed_above, attn_above, mixed_above, ff_scatter = later
            ff_scatter.settle(branch_grad).send()
            both_late, attn_late = after((both_above, attn_above), branch_grad, *ff_scatter.now())
            attn_scatter = Scatter(
                [gradient_half(normed_above, both_late, True)],
                [gradient_half(attn_late, mixed_above, True)],
            )
            attn_scatter.send()
            beside = ff_scatter.sent + attn_scatter.sent
            if above == last:
                final_sum = after(final_sum, *beside)
                layer_out = add_rounded(saved[last][7], final_sum, bias_down[last][None])
                out_slots, out_back = rows_back(layer_out)
                beside.append(out_slots)
            branch_all = after(branch_all, *beside)
            pre_grad = times(branch_all, w_down, gelu_back, (pre_gelu,), (BF16,))[0]
        normed_part = times_turned(pre_grad, w_up, BF16)
        if l < last:
            normed_part = after(normed_part, *ff_scatter.come, *attn_scatter.come)
        normed_two_grad = tensor_sum(normed_part)
        beside = []
        if l < last:
            attn_scatter.settle(normed_part).send()
            beside += attn_scatter.sent
            ff_open[above] = ff_scatter
        pre_late, branch_late = after((pre_grad, branch_all), normed_part)
        ff_scatter = Scatter(
            [gradient_half(normed_two_all, pre_late, True)],
            [gradient_half(branch_late, activation, True)],
        )
        ff_scatter.send()
        beside += ff_scatter.now() + ff_scatter.sent
        if l == last:
            down_bias_part = column_sum(after(branch_grad, normed_part))
        up_bias_grads[l] = column_sum(pre_late)
        beside += [down_bias_part, up_bias_grads[l]]
        if l == last:
            final_part = times_turned(after(activation, *ff_scatter.sent), w_down, BF16)
            beside.append(final_part)
        else:
            both_whole, out_whole = attn_scatter.finish(*ff_scatter.now())
            beside += [both_whole, out_whole]
        normed_two_grad = after(normed_two_grad, *beside)
        if l == last:
            final_sum = tensor_sum(after(final_part, normed_two_grad))
        hidden_grad, attn_grad, two_sums = norm_back(
            hidden_state, normed_two_grad, gain_two[l : l + 1], tangent
        )
        mixed_grad = product(attn_grad, w_out)
        if l == 0:
            attn_late = after(attn_grad, mixed_grad)
            out_scatter = Scatter(
                [gradient_half(attn_late, mixed[:, :split])],
                [gradient_half(attn_late, mixed[:, split:])],
            ).send()
            mixed_grad = after(mixed_grad, *out_scatter.sent)
        query_grad, pair_part = attend_back(
            queries,
            width,
            mixed_grad,
            pair_all[:, :HEAD],
            pair_all[:, HEAD:],
            pair_t[:HEAD],
            score_bias,
            log_totals,
            score_scale,
        )
        if l < last:
            both_whole, out_whole = after((both_whole, out_whole), query_grad)
            out_grad = tensor_sum(stack_columns(out_whole, tensor_count)).astype(F32).T
            query_sum = tensor_sum(stack_query(both_whole, width, query_cols, pair_cols))
            query_w_grad, kv_grad = split_query(query_sum, depth, pair_cols)
        pair_come = tensor_swap(pair_part.astype(BF16))
        pair_grad = sum(
            pair_come[k * local_rows : (k + 1) * local_rows].astype(F32)
            for k in range(tensor_count)
        ).astype(BF16)
        query_bias_grads[l] = jnp.sum(query_grad.astype(F32), axis=0)
        value_bias_grads[l] = jnp.sum(pair_grad[:, HEAD:].astype(F32), axis=0)
        both_grad = jnp.concatenate([query_grad, pair_grad], axis=1)
        if l == last > 0:
            both_grad = after(both_grad, *ff_scatter.come)
        if l == 0:
            both_grad = after(both_grad, *ff_scatter.come)
            both_scatter = Scatter(
                [gradient_half(normed, both_grad[:, :split])],
                [gradient_half(normed, both_grad[:, split:])],
            ).send()
            ff_scatter.settle(*both_scatter.sent).send()
            out_scatter.settle(*ff_scatter.sent).send()
            both_grad = after(both_grad, *both_scatter.sent, *out_scatter.sent, *ff_scatter.sent)
            ff_open[0] = ff_scatter
        normed_grad = product_turned(both_grad, w_query)
        if l == last > 0:
            normed_grad, final_sum = lax.optimization_barrier((normed_grad, final_sum))
        tangent, branch_grad, one_sums = norm_back(
            stream_in, normed_grad, gain_one[l : l + 1], hidden_grad
        )
        if l < last:
            reduced[above] = (query_w_grad, kv_grad, out_grad)
        later = (l, both_grad, normed, attn_grad, mixed, ff_scatter)
        vector_grads[l] = [
            one_sums[0],
            one_sums[1],
            two_sums[2],
            two_sums[0],
            two_sums[1],
            down_bias_part,
        ]
        down_bias_part = one_sums[2]

    stacked = jnp.stack([vector_grads[l][m] for m in range(6) for l in range(layer_total)])
    stacked = reorder(after(stacked, *ff_open[0].come), from_slots)
    query_rows = jnp.stack(query_bias_grads)
    value_rows = jnp.pad(jnp.stack(value_bias_grads), ((0, 0), (0, width - HEAD)))
    smalls = jnp.concatenate([stacked, query_rows, value_rows], axis=0)
    small_count = smalls.shape[0]
    smalls = jnp.concatenate([smalls, jnp.stack(up_bias_grads)], axis=0)
    smalls = smalls + flip(smalls, 1)
    total = smalls[:small_count]
    if tensor_count & (tensor_count - 1) == 0:
        for k in range(tensor_count.bit_length() - 1):
            total = total + lax.ppermute(
                total, "tensor", [(i, i ^ (1 << k)) for i in range(tensor_count)]
            )
    else:
        total = lax.psum(total, "tensor")
    total = jnp.concatenate([total, smalls[small_count:]], axis=0)
    for bit in plane_bits():
        total = total + flip(total, bit)
    up_bias_grad = total[small_count:]
    vector_sums = [total[m * layer_total : (m + 1) * layer_total] for m in range(8)]
    query_bias_grad = lax.dynamic_slice_in_dim(
        vector_sums[6], tensor_rank * query_cols, query_cols, 1
    )
    value_bias_grad = vector_sums[7][:, :HEAD]

    grad_back = rows_back(branch_grad)[1]
    out_back = after(out_back, tangent)
    both_scatter.settle(normed_grad).send()
    out_whole = jnp.concatenate(out_scatter.finish(), axis=1)
    out_grad = tensor_sum(stack_columns(out_whole, tensor_count)).astype(F32).T
    both_whole = jnp.concatenate(both_scatter.finish(), axis=1)
    query_stack = stack_query(both_whole, width, query_cols, pair_cols)
    query_w_grad, kv_grad = split_query(tensor_sum(query_stack), depth, pair_cols)
    reduced[0] = (query_w_grad, kv_grad, out_grad)
    up_stack, down_stack = [
        stack_sums([ff.open_sum(m) for ff in ff_open], m == 1) for m in range(2)
    ]
    if last == 0:
        layer_out = add_rounded(saved[last][7], final_sum, bias_down[last][None])
        out_back = rows_back(layer_out)[1]
    layer_rows = contract_rows(send_table, out_back).astype(BF16)
    token_rows = contract_rows(send_table, grad_back).astype(BF16)
    summed = [jnp.stack([reduced[l][m] for l in range(layer_total)]) for m in range(3)]
    return (
        layer_rows,
        token_rows,
        vector_sums[0],
        vector_sums[1],
        summed[0],
        query_bias_grad,
        summed[1],
        value_bias_grad,
        summed[2],
        vector_sums[2],
        vector_sums[3],
        vector_sums[4],
        up_stack,
        up_bias_grad,
        down_stack,
        vector_sums[5],
    )


def solution(mesh):
    rows = P(("dp", "tensor"), None)
    in_specs = (
        rows,
        rows,
        P(("dp", "tensor")),
        P("dp"),
        P(),
        P(),
        P(None, "dp", "tensor"),
        P(None, "tensor"),
        P(None, "dp", "tensor"),
        P(),
        P(None, "tensor", "dp"),
        P(),
        P(),
        P(),
        P(None, "dp", "tensor"),
        P(None, "tensor"),
        P(None, "tensor", "dp"),
        P(),
    )
    out_specs = (
        rows,
        rows,
        P(),
        P(),
        P(None, "dp", "tensor"),
        P(None, "tensor"),
        P(None, "dp", "tensor"),
        P(),
        P(None, "tensor", "dp"),
        P(),
        P(),
        P(),
        P(None, "dp", "tensor"),
        P(None, "tensor"),
        P(None, "tensor", "dp"),
        P(),
    )
    return jax.shard_map(local, mesh=mesh, in_specs=in_specs, out_specs=out_specs, check_vma=False)
```
